256 devices in a mesh: owner: 8 (over y, core), tensor: 32 (over x, z).
Axes of the slice: x: 4, y: 4, z: 8, core: 2. Of those that a mesh axis runs over, the one named last changes fastest.
Arguments:
- hidden: bfloat16 [256, 2048], P('owner', 'tensor'), may hold values from -6 to 6
- attention_gain: bfloat16 [2048], replicated, may hold values from 0.5 to 1.5
- query_weight: bfloat16 [9216, 2048], P('tensor'), may hold values from -1 to 1
- out_weight: bfloat16 [2048, 8192], P('tensor'), may hold values from -1.796875 to 1.796875
- root_cache: bfloat16 [32768, 576], P('tensor'), may hold values from -4 to 4
- group_cache: bfloat16 [96, 1024, 576], P('owner', 'tensor'), may hold values from -4 to 4
- group_length: int32 [96], P('owner'), may hold values from 128 to 1024, as said below
- suffix_cache: bfloat16 [256, 512, 576], P('owner', 'tensor'), may hold values from -4 to 4
- suffix_length: int32 [256], P('owner'), may hold values from 1 to 512, as said below
- group_of: int32 [256], P('owner'), may hold values from 0 to 95, as said below
- mixture_gain: bfloat16 [2048], replicated, may hold values from 0.5 to 1.5
- routes: int32 [256, 6], P('owner'), may hold values from 0 to 63, all different within a row; in each aligned block of 32 rows (0 to 31, 32 to 63, ...) at most 6 rows name the same one
- route_weight: float32 [256, 6], P('owner'), may hold values from 0.1 to 1
- expert_gate: bfloat16 [256, 352, 2048], P(('owner', 'tensor')), may hold values from -0.125 to 0.125
- expert_up: bfloat16 [256, 352, 2048], P(('owner', 'tensor')), may hold values from -0.125 to 0.125
- expert_down: bfloat16 [256, 352, 2048], P(('owner', 'tensor')), may hold values from -0.15625 to 0.15625
- shared_gate: bfloat16 [2816, 2048], P('tensor'), may hold values from -0.125 to 0.125
- shared_up: bfloat16 [2816, 2048], P('tensor'), may hold values from -0.125 to 0.125
- shared_down: bfloat16 [2816, 2048], P('tensor'), may hold values from -0.109375 to 0.109375
Outputs:
- layer_out: bfloat16 [256, 2048], P('owner', 'tensor')
The draws below stay inside these ranges and needn't reach their ends.
Inputs may be any that keep to these rules, and one draw needn't show every extreme that they name: `group_of`: the groups of owner o are o * 12 to (o + 1) * 12 - 1. Among the requests of one owner (rows o * 32 to (o + 1) * 32 - 1), at most 8 have their group on any one owner, and some owner gets exactly 8 of them. `group_length`: some group prompt uses all 1024 positions. `suffix_length`: some request uses all 512 suffix positions. `routes`: each row names 6 different experts; among the rows of one owner no expert is named more than 6 times, and that is reached.
All inputs are finite; a program needn't handle non-finite values.
Results may differ from the reference program's by a relative error of at most 0.012.
The reference program's roundings to bfloat16 on the way count: a program that leaves them out, or rounds other values in their place, can miss the bound.
Values may be sent and summed in bfloat16 or wider, within the bound.
A program may use at most 128 MiB of HBM per device.

```python
import math
import jax
import jax.numpy as jnp
import numpy as np
from jax import lax

D = 2048
H = 16
LAT = 512
ROPE = 64
KVW = 576
FF = 1408
SHARED_FF = 2816
TOPK = 6
EXPERTS = 64
FSPLIT = 4
ROOT = 32768
GROUP_OWN = 12
GROUPS = 96
GMAX = 1024
SMAX = 512
REQ_OWN = 32
REQUESTS = 256
CAP = 8
ECAP = 6
RSEG = 1024
GSEG = 32
SSEG = 16
N_OWNER = 8
N_TENSOR = 32


def cache_rows(key, salt_value, array_shape, spread):
    inner_key = jax.random.fold_in(key, salt_value)
    base_rows = jnp.clip(jax.random.normal(inner_key, array_shape, jnp.float32) * spread, -4.0, 4.0)
    return base_rows


def root_rows(key):
    inner_key = jax.random.fold_in(key, 11)
    row_scale = jnp.exp(jax.random.uniform(jax.random.fold_in(key, 14), (ROOT, 1), jnp.float32, -1.15, 1.15))
    mean_sign = jax.random.rademacher(jax.random.fold_in(key, 15), (LAT,), jnp.float32)
    mean_pick = jax.random.uniform(jax.random.fold_in(key, 16), (LAT,), jnp.float32) < 0.25
    mean_vector = jnp.concatenate([jnp.where(mean_pick, 0.3 * mean_sign, 0.0), jnp.zeros((ROPE,), jnp.float32)])
    base_rows = jax.random.normal(inner_key, (ROOT, KVW), jnp.float32) * 0.5
    rows = jnp.clip(mean_vector[None, :] + row_scale * base_rows, -4.0, 4.0)
    return rows


def draw_root_cache(key, part):
    return root_rows(key).astype(jnp.bfloat16)


def draw_group_cache(key, part):
    return cache_rows(key, 12, (GROUPS, GMAX, KVW), 1.6).astype(jnp.bfloat16)


def draw_suffix_cache(key, part):
    return cache_rows(key, 13, (REQUESTS, SMAX, KVW), 1.4).astype(jnp.bfloat16)


def draw_query_weight(key, part):
    array_shape = (H * KVW, D)
    inner_key = jax.random.fold_in(key, 21)
    base_rows = jnp.clip(jax.random.normal(inner_key, array_shape, jnp.float32), -4.0, 4.0) / math.sqrt(D)
    return base_rows.astype(jnp.bfloat16)


def draw_group_of(key, part):

    def one_block(block_key):
        block_keys = jax.random.split(block_key, 4)
        hot_owner = jax.random.randint(block_keys[0], (), 0, N_OWNER)
        slots = jnp.arange(N_OWNER * CAP)
        priority = jax.random.permutation(block_keys[1], N_OWNER * CAP)
        ranked = jnp.where(slots // CAP == hot_owner, priority - N_OWNER * CAP, priority)
        taken_slots = jnp.argsort(ranked, stable=True)[:REQ_OWN]
        owner_index = taken_slots // CAP
        member = jax.random.randint(block_keys[2], (REQ_OWN,), 0, GROUP_OWN)
        shuffle = jax.random.permutation(block_keys[3], REQ_OWN)
        return (owner_index * GROUP_OWN + member)[shuffle]
    block_keys = jax.random.split(jax.random.fold_in(key, 31), N_OWNER)
    return jax.vmap(one_block)(block_keys).reshape(-1).astype(jnp.int32)


def draw_group_length(key, part):
    lengths = jax.random.randint(jax.random.fold_in(key, 41), (GROUPS,), GMAX // 8, GMAX + 1)
    longest = jax.random.randint(jax.random.fold_in(key, 42), (), 0, GROUPS)
    return jnp.where(jnp.arange(GROUPS) == longest, GMAX, lengths).astype(jnp.int32)


def draw_suffix_length(key, part):
    lengths = jax.random.randint(jax.random.fold_in(key, 51), (REQUESTS,), 1, SMAX + 1)
    longest = jax.random.randint(jax.random.fold_in(key, 52), (), 0, REQUESTS)
    return jnp.where(jnp.arange(REQUESTS) == longest, SMAX, lengths).astype(jnp.int32)


def steps_of(own_key, extent, cuts, least, high):
    loudness = 1.0
    for position, shards_of in cuts:
        heights = jax.random.uniform(jax.random.fold_in(jax.random.fold_in(own_key, 6), position), (shards_of,), jnp.float32, least / len(cuts), high / len(cuts))
        loudness = loudness * jnp.repeat(jnp.exp(heights), extent[position] // shards_of).reshape((-1,) + (1,) * (len(extent) - 1 - position))
    return loudness


def routed_block(key, own, number, rows, count, top, limit, lean):
    order = jax.random.permutation(key, count)
    heavy_load, common = load_shares(count, rows * top, limit, lean, True), load_shares(count, rows * top, limit, lean, False)
    places = jnp.arange(count)

    def named(sizes, rotation):
        used = int((sizes > 0).sum())
        fixed = max(1, used // 4)
        shifted = fixed + (places - fixed + rotation * (used - fixed)) % max(1, count - fixed)
        return jnp.zeros((count,), jnp.int32).at[order[jnp.where(places < fixed, places, shifted)]].set(jnp.asarray(sizes, jnp.int32))

    sizes = jnp.where(number % 4 == 0, named(heavy_load, number // 4), named(common, number - number // 4 - 1))
    mixed = jax.random.permutation(jax.random.fold_in(own, 3), count)
    source_of, receiver = mixed[0:count // 2 * 2:2], mixed[1:count // 2 * 2:2]
    slack = jnp.minimum(sizes[source_of] - 1, limit - sizes[receiver]) // 2
    slack = jnp.where((source_of == order[0]) | (receiver == order[0]) | (sizes[receiver] == 0), 0, jnp.maximum(slack, 0))
    shifted = jax.random.randint(jax.random.fold_in(own, 4), (count // 2,), 0, 1 << 20) % (slack + 1)
    sizes = sizes.at[source_of].add(-shifted).at[receiver].add(shifted)
    labels = jnp.searchsorted(jnp.cumsum(sizes), jnp.arange(rows * top), side="right").astype(jnp.int32)
    table = labels.reshape(top, rows).T
    table = table[jax.random.permutation(jax.random.fold_in(own, 1), rows)]
    rotation = jax.random.randint(jax.random.fold_in(own, 2), (rows, 1), 0, top)
    return jnp.take_along_axis(table, (jnp.arange(top)[None, :] + rotation) % top, axis=1)


def load_shares(count, total, limit, skew, full):
    weights = [(1 << 20) // math.isqrt(rank ** skew) + 1 for rank in range(1, count + 1)]
    largest = limit if full else min(limit, max(-(-total // count), total * weights[0] // sum(weights)))
    least = 1 if total - largest >= count - 1 else 0
    counts, rest = [largest] + [least] * (count - 1), total - largest - least * (count - 1)
    while rest > 0:
        movable = [i for i in range(1, count) if counts[i] < largest] or [i for i in range(1, count) if counts[i] < limit]
        whole, budget = sum([weights[i] for i in movable]), rest
        for i in movable:
            addition = min(limit - counts[i], max(1, budget * weights[i] // whole), rest)
            counts[i] = counts[i] + addition
            rest = rest - addition
    return np.array(counts)


def gaussian(own_key, dims, deviation, reach, cuts=(), dtype=jnp.bfloat16):
    factor_of = steps_of(own_key, dims, cuts, -0.22, 0.18) if cuts else 1.0
    drawn = jax.random.normal(own_key, dims, jnp.float32) * deviation * factor_of
    return jnp.minimum(jnp.maximum(drawn, -reach), reach).astype(dtype)


def setup_inputs(seed: int = 0) -> dict:
    seeds = jax.random.split(jax.random.key(seed), 20)
    hidden = gaussian(seeds[0], (REQUESTS, D), 1.0, 6.0, ((0, 8), (1, 32)))
    attention_gain = jnp.clip(1.0 + 0.1 * jax.random.normal(seeds[1], (D,), jnp.float32), 0.5, 1.5).astype(jnp.bfloat16)
    query_weight = draw_query_weight(jax.random.fold_in(seeds[19], 71), 0)
    out_weight = gaussian(seeds[3], (D, H * LAT), 0.3, 1.796875, ((0, 32),))
    root_cache = draw_root_cache(jax.random.fold_in(seeds[19], 71), 0)
    group_cache = draw_group_cache(jax.random.fold_in(seeds[19], 71), 0)
    group_length = draw_group_length(jax.random.fold_in(seeds[19], 71), 0)
    suffix_cache = draw_suffix_cache(jax.random.fold_in(seeds[19], 71), 0)
    suffix_length = draw_suffix_length(jax.random.fold_in(seeds[19], 71), 0)
    group_of = draw_group_of(jax.random.fold_in(seeds[19], 71), 0)
    mixture_gain = jnp.clip(1.0 + 0.1 * jax.random.normal(seeds[10], (D,), jnp.float32), 0.5, 1.5).astype(jnp.bfloat16)
    routes_keys = jax.random.split(jax.random.fold_in(seeds[11], 1), REQUESTS // REQ_OWN)
    routes_turns = jax.random.permutation(jax.random.fold_in(seeds[11], 3), REQUESTS // REQ_OWN)
    routes = jax.vmap(lambda own, number: routed_block(jax.random.fold_in(seeds[11], 2), own, number, REQ_OWN, EXPERTS, TOPK, ECAP, 2))(routes_keys, routes_turns).reshape((REQUESTS, TOPK))
    route_weight = jnp.clip(jnp.exp(math.log(1.0) - 2.3025851 * jax.random.uniform(seeds[12], (REQUESTS, TOPK), jnp.float32) ** steps_of(seeds[12], (REQUESTS, TOPK), ((0, 8),), -0.2, 0.2)), 0.1, 1.0)
    expert_gate = gaussian(seeds[13], (EXPERTS * FSPLIT, FF // FSPLIT, D), D ** -0.5, 0.125, ((0, 256),))
    expert_up = gaussian(seeds[14], (EXPERTS * FSPLIT, FF // FSPLIT, D), D ** -0.5, 0.125, ((0, 256),))
    expert_down = gaussian(seeds[15], (EXPERTS * FSPLIT, FF // FSPLIT, D), FF ** -0.5, 0.15625, ((0, 256),))
    shared_gate = gaussian(seeds[16], (SHARED_FF, D), D ** -0.5, 0.125, ((0, 32),))
    shared_up = gaussian(seeds[17], (SHARED_FF, D), D ** -0.5, 0.125, ((0, 32),))
    shared_down = gaussian(seeds[18], (SHARED_FF, D), SHARED_FF ** -0.5, 0.109375, ((0, 32),))
    return dict(hidden=hidden, attention_gain=attention_gain, query_weight=query_weight, out_weight=out_weight, root_cache=root_cache, group_cache=group_cache, group_length=group_length, suffix_cache=suffix_cache, suffix_length=suffix_length, group_of=group_of, mixture_gain=mixture_gain, routes=routes, route_weight=route_weight, expert_gate=expert_gate, expert_up=expert_up, expert_down=expert_down, shared_gate=shared_gate, shared_up=shared_up, shared_down=shared_down)


score_scale = 192.0 ** (-0.5)
lowest = -1e+30
epsilon = 1e-06

def rms_rows(values, gain_vector):
    values = values.astype(jnp.float32)
    scaled = values * lax.rsqrt(lax.optimization_barrier(jnp.mean(values * values, axis=-1, keepdims=True)) + epsilon)
    return scaled * gain_vector.astype(jnp.float32)

def settle(rounded):
    return lax.optimization_barrier(rounded).astype(jnp.float32)

def block_softmax(scores, usable, values, formula):
    masked = jnp.where(usable, scores, lowest)
    peak_score = lax.optimization_barrier(jnp.max(masked, axis=-1, keepdims=True))
    weights = jnp.where(usable, jnp.exp(masked - peak_score), 0.0)
    total_mass = lax.optimization_barrier(jnp.sum(weights, axis=-1))
    numerator = jnp.einsum(formula, settle(weights.astype(jnp.bfloat16)), values)
    present = total_mass > 0.0
    safe_total = jnp.where(present, total_mass, 1.0)
    block_out = numerator / safe_total[..., None]
    log_mass = jnp.where(present, peak_score[..., 0] + jnp.log(safe_total), lowest)
    return (block_out, log_mass)

def reference(hidden, attention_gain, query_weight, out_weight, root_cache, group_cache, group_length, suffix_cache, suffix_length, group_of, mixture_gain, routes, route_weight, expert_gate, expert_up, expert_down, shared_gate, shared_up, shared_down):
    normed = rms_rows(hidden, attention_gain).astype(jnp.bfloat16)
    queries = jnp.dot(normed, query_weight.T, preferred_element_type=jnp.float32).astype(jnp.bfloat16)
    queries = queries.reshape(N_OWNER, REQ_OWN, H, KVW)
    root_blocks = root_cache.astype(jnp.float32).reshape(N_TENSOR, RSEG, KVW)
    suffix_all = suffix_cache.reshape(N_OWNER, REQ_OWN, SMAX, KVW)
    suffix_counts = suffix_length.reshape(N_OWNER, REQ_OWN)
    parents = group_of.reshape(N_OWNER, REQ_OWN)
    suffix_positions = jnp.arange(SMAX).reshape(N_TENSOR, SSEG)
    group_positions = jnp.arange(GMAX).reshape(N_TENSOR, GSEG)

    def attend(pieces):
        query_rows, suffix_rows, suffix_count, parent = pieces
        query_rows = query_rows.astype(jnp.float32)
        root_scores = jnp.einsum('rhc,bpc->rhbp', query_rows, root_blocks) * score_scale
        root_out, root_mass = block_softmax(root_scores, jnp.ones(root_scores.shape, bool), root_blocks[..., :LAT], 'rhbp,bpl->rhbl')
        suffix_rows = suffix_rows.astype(jnp.float32).reshape(REQ_OWN, N_TENSOR, SSEG, KVW)
        suffix_scores = jnp.einsum('rhc,rbpc->rhbp', query_rows, suffix_rows) * score_scale
        suffix_usable = (suffix_positions[None, :, :] < suffix_count[:, None, None])[:, None, :, :]
        suffix_out, suffix_mass = block_softmax(suffix_scores, suffix_usable, suffix_rows[..., :LAT], 'rhbp,rbpl->rhbl')
        group_rows = group_cache[parent].astype(jnp.float32).reshape(REQ_OWN, N_TENSOR, GSEG, KVW)
        group_scores = jnp.einsum('rhc,rbpc->rhbp', query_rows, group_rows) * score_scale
        group_usable = (group_positions[None, :, :] < group_length[parent][:, None, None])[:, None, :, :]
        group_out, group_mass = block_softmax(group_scores, group_usable, group_rows[..., :LAT], 'rhbp,rbpl->rhbl')
        group_out = settle(group_out.astype(jnp.bfloat16))
        all_mass = jnp.concatenate([root_mass, suffix_mass, group_mass], axis=2)
        all_out = jnp.concatenate([root_out, suffix_out, group_out], axis=2)
        peak_mass = lax.optimization_barrier(jnp.max(all_mass, axis=2, keepdims=True))
        scales = jnp.exp(all_mass - peak_mass)
        joined = lax.optimization_barrier(jnp.sum(scales[..., None] * all_out, axis=2)) / lax.optimization_barrier(jnp.sum(scales, axis=2))[..., None]
        return joined.astype(jnp.bfloat16).reshape(REQ_OWN, H * LAT)
    attention = lax.map(attend, (queries, suffix_all, suffix_counts, parents)).reshape(REQUESTS, H * LAT)
    mid = (hidden.astype(jnp.float32) + jnp.dot(attention, out_weight.T, preferred_element_type=jnp.float32)).astype(jnp.bfloat16)
    mixture_in = rms_rows(mid, mixture_gain).astype(jnp.bfloat16)
    matches = routes[:, :, None] == jnp.arange(EXPERTS).astype(jnp.int32)[None, None, :]
    share = lax.optimization_barrier(jnp.sum(matches.astype(jnp.float32) * route_weight[:, :, None], axis=1))
    hit_table = jnp.any(matches, axis=1).astype(jnp.int32)
    gate_all = expert_gate.reshape(EXPERTS, FF, D)
    up_all = expert_up.reshape(EXPERTS, FF, D)
    down_all = expert_down.reshape(EXPERTS, FSPLIT, FF // FSPLIT, D)

    def expert_step(routed_total, pieces):
        gate_rows, up_rows, down_rows, column, hit_rows = pieces
        picked = jnp.argsort(1 - hit_rows, stable=True)[:N_OWNER * ECAP].astype(jnp.int32)
        inputs = mixture_in[picked]
        gate_part = jnp.dot(inputs, gate_rows.T, preferred_element_type=jnp.float32)
        up_part = jnp.dot(inputs, up_rows.T, preferred_element_type=jnp.float32)
        activation = settle((jax.nn.silu(gate_part) * up_part).astype(jnp.bfloat16))
        blocks = jnp.einsum('rbf,bfd->rbd', activation.reshape(N_OWNER * ECAP, FSPLIT, FF // FSPLIT), down_rows.astype(jnp.float32))
        parts = lax.optimization_barrier(jnp.sum(settle(blocks.astype(jnp.bfloat16)), axis=1))
        return (routed_total.at[picked].add(column[picked][:, None] * parts), None)
    routed, _ = lax.scan(expert_step, jnp.zeros((REQUESTS, D), jnp.float32), (gate_all, up_all, down_all, share.T, hit_table.T))
    shared_gate_part = jnp.dot(mixture_in, shared_gate.T, preferred_element_type=jnp.float32)
    shared_up_part = jnp.dot(mixture_in, shared_up.T, preferred_element_type=jnp.float32)
    shared_act = (jax.nn.silu(shared_gate_part) * shared_up_part).astype(jnp.bfloat16)
    shared = jnp.dot(shared_act, shared_down, preferred_element_type=jnp.float32)
    return (mid.astype(jnp.float32) + routed + shared).astype(jnp.bfloat16)
```

```python
import functools

import jax
import jax.numpy as jnp
from jax import lax
from jax.experimental import pallas as pl
from jax.experimental.pallas import tpu as pltpu
from jax.sharding import PartitionSpec as P

D = 2048
H = 16
LAT = 512
KVW = 576
GROUP_OWN = 12
REQ = 32
NT = 32
NO = 8
SLOT = 8
HALF = 1024
SCALE = 192.0 ** (-0.5)
LOWEST = -1e30
EPS = 1e-06
MESH = pl.DeviceIdType.MESH
F32 = jnp.float32
BF16 = jnp.bfloat16


def dot_t(a, b):
    return lax.dot_general(a, b, (((1,), (1,)), ((), ())), preferred_element_type=F32)


def dot_n(a, b):
    return lax.dot_general(a, b, (((1,), (0,)), ((), ())), preferred_element_type=F32)


def lanes(shape):
    return lax.broadcasted_iota(jnp.int32, shape, len(shape) - 1)


def rows(shape):
    return lax.broadcasted_iota(jnp.int32, shape, len(shape) - 2)


def pack(x):
    return jnp.concatenate([x[:16], x[16:]], axis=1)


def unpack_all(blocks_ref, wide_ref):
    low = lanes((16, 128)) < 64
    for i in range(NT // 2):
        a = blocks_ref[2 * i].astype(F32)
        b = blocks_ref[2 * i + 1].astype(F32)
        wide_ref[0:16, 128 * i : 128 * i + 128] = jnp.where(low, a, pltpu.roll(b, 64, 1))
        wide_ref[16:32, 128 * i : 128 * i + 128] = jnp.where(low, pltpu.roll(a, 64, 1), b)


def rms(wide_ref, gain_ref):
    x = wide_ref[...]
    scaled = x * lax.rsqrt(jnp.mean(x * x, axis=-1, keepdims=True) + EPS)
    return (scaled * gain_ref[...].astype(F32)).astype(BF16)


def block_part(q, keys, usable):
    scores = dot_t(q, keys) * SCALE
    if usable is not None:
        scores = jnp.where(usable, scores, LOWEST)
    peak = jnp.max(scores, axis=-1, keepdims=True)
    weights = jnp.exp(scores - peak)
    if usable is not None:
        weights = jnp.where(usable, weights, 0.0)
    total = jnp.sum(weights, axis=-1, keepdims=True)
    numerator = dot_n(weights.astype(BF16), keys[:, :LAT])
    present = total > 0.0
    safe = jnp.where(present, total, 1.0)
    return numerator / safe, jnp.where(present, peak + jnp.log(safe), LOWEST)


def silu(v):
    return v / (1.0 + jnp.exp(-v))


def kernel(
    hidden_ref,
    again_ref,
    wq_hbm,
    wo_hbm,
    root_hbm,
    gcache_hbm,
    glen_s,
    sfx_hbm,
    slen_s,
    gof_s,
    mgain_ref,
    routes_ref,
    rweight_ref,
    eg_hbm,
    eu_hbm,
    ed_hbm,
    sg_hbm,
    su_hbm,
    sd_hbm,
    out_ref,
    wq,
    wo,
    root,
    gc,
    gg,
    sfx,
    eg,
    eu,
    ed,
    sg,
    su,
    sd,
    glr,
    hid_g,
    q_g,
    q_all,
    po,
    pr,
    att_g,
    mid_g,
    dsp_s,
    dsp_r,
    ret_s,
    ret_r,
    rs_s,
    rs_r,
    wide,
    part,
    load_sem,
    hid_ss,
    hid_rs,
    q_ss,
    q_rs,
    p_ss,
    p_rs,
    att_ss,
    att_rs,
    mid_ss,
    mid_rs,
    rs_ss,
    rs_rs,
    dsp_ss,
    dsp_rs,
    ret_ss,
    ret_rs,
    gl_ss,
    gl_rs,
    gc_ss,
    gc_rs,
):
    o = lax.axis_index("owner")
    t = lax.axis_index("tensor")

    def tpeer(k):
        return lax.rem(t + k, NT)

    def opeer(k):
        return lax.rem(o + k, NO)

    wq[0:32, :] = jnp.zeros((32, D), BF16)
    wq[288:384, :] = jnp.zeros((96, D), BF16)
    shift = pl.multiple_of(lax.rem(t, 2) * 32, 32)
    loads = [
        pltpu.make_async_copy(wq_hbm, wq.at[pl.ds(shift, 288)], load_sem.at[0]),
        pltpu.make_async_copy(root_hbm, root, load_sem.at[1]),
        pltpu.make_async_copy(sfx_hbm, sfx, load_sem.at[2]),
        pltpu.make_async_copy(
            gcache_hbm, gc.at[pl.ds(GROUP_OWN * o, GROUP_OWN)], load_sem.at[3]
        ),
        pltpu.make_async_copy(wo_hbm, wo, load_sem.at[4]),
        pltpu.make_async_copy(sg_hbm, sg, load_sem.at[5]),
        pltpu.make_async_copy(su_hbm, su, load_sem.at[6]),
        pltpu.make_async_copy(sd_hbm, sd, load_sem.at[7]),
        pltpu.make_async_copy(eg_hbm.at[0], eg, load_sem.at[8]),
        pltpu.make_async_copy(eu_hbm.at[0], eu, load_sem.at[9]),
        pltpu.make_async_copy(ed_hbm.at[0], ed, load_sem.at[10]),
    ]
    for load in loads:
        load.start()

    hid_g[t] = pack(hidden_ref[...])
    lane_row = lanes((8, 128))
    own_lengths = jnp.zeros((8, 128), jnp.int32)
    for g in range(GROUP_OWN):
        own_lengths = jnp.where(lane_row == g, glen_s[g], own_lengths)
    glr[o] = own_lengths

    barrier = pltpu.get_barrier_semaphore()

    def greet_tensor(k, carry):
        pl.semaphore_signal(
            barrier, inc=1, device_id={"tensor": tpeer(k)}, device_id_type=MESH
        )
        return carry

    def greet_owner(k, carry):
        pl.semaphore_signal(
            barrier, inc=1, device_id={"owner": opeer(k)}, device_id_type=MESH
        )
        return carry

    lax.fori_loop(1, NT, greet_tensor, 0)
    lax.fori_loop(1, NO, greet_owner, 0)
    pl.semaphore_wait(barrier, NT - 1 + NO - 1)

    def gather_copy(buf, ss, rs, k, slot):
        return pltpu.make_async_remote_copy(
            src_ref=buf.at[slot],
            dst_ref=buf.at[slot],
            send_sem=ss.at[k],
            recv_sem=rs.at[slot],
            device_id={"tensor": tpeer(k)},
            device_id_type=MESH,
        )

    def gather_start(buf, ss, rs):
        def step(k, carry):
            gather_copy(buf, ss, rs, k, t).start()
            return carry

        lax.fori_loop(1, NT, step, 0)

    def gather_wait(buf, ss, rs):
        def step(k, carry):
            gather_copy(buf, ss, rs, k, lax.rem(t + NT - k, NT)).wait_recv()
            return carry

        lax.fori_loop(1, NT, step, 0)

    def gather_sent(buf, ss, rs):
        def step(k, carry):
            gather_copy(buf, ss, rs, k, t).wait_send()
            return carry

        lax.fori_loop(1, NT, step, 0)

    def spread_copy(src, dst, ss, rs, axis, me, peer, came_from):
        return pltpu.make_async_remote_copy(
            src_ref=src.at[peer],
            dst_ref=dst.at[came_from],
            send_sem=ss.at[peer],
            recv_sem=rs.at[came_from],
            device_id={axis: peer},
            device_id_type=MESH,
        )

    def owner_start(src, dst, ss, rs):
        def step(k, carry):
            spread_copy(src, dst, ss, rs, "owner", o, opeer(k), o).start()
            return carry

        lax.fori_loop(1, NO, step, 0)

    def owner_wait(src, dst, ss, rs):
        def step(k, carry):
            p = opeer(k)
            spread_copy(src, dst, ss, rs, "owner", o, p, p).wait_recv()
            return carry

        lax.fori_loop(1, NO, step, 0)

    def owner_sent(src, dst, ss, rs):
        def step(k, carry):
            spread_copy(src, dst, ss, rs, "owner", o, opeer(k), o).wait_send()
            return carry

        lax.fori_loop(1, NO, step, 0)

    gather_start(hid_g, hid_ss, hid_rs)

    up = opeer(2)
    down = opeer(6)
    far = opeer(4)
    mate = o + 1 - 2 * lax.rem(o, 2)

    def groups(owner, first=0, count=GROUP_OWN):
        return gc.at[pl.ds(GROUP_OWN * owner + first, count)]

    def cache_copy(src, dst, n, to):
        return pltpu.make_async_remote_copy(
            src_ref=src,
            dst_ref=dst,
            send_sem=gc_ss.at[n],
            recv_sem=gc_rs.at[n],
            device_id={"owner": to},
            device_id_type=MESH,
        )

    half = GROUP_OWN // 2
    mate_up = lax.rem(mate + 2, NO)
    mate_down = lax.rem(mate + 6, NO)
    mate_far = lax.rem(mate + 4, NO)
    cache_copy(gcache_hbm, groups(o), 0, up).start()
    cache_copy(gcache_hbm, groups(o), 1, down).start()
    cache_copy(gcache_hbm, groups(o), 2, mate).start()

    def lengths_copy(k, slot):
        return pltpu.make_async_remote_copy(
            src_ref=glr.at[slot],
            dst_ref=glr.at[slot],
            send_sem=gl_ss.at[k],
            recv_sem=gl_rs.at[slot],
            device_id={"owner": opeer(k)},
            device_id_type=MESH,
        )

    def lengths_start(k, carry):
        lengths_copy(k, o).start()
        return carry

    def lengths_wait(k, carry):
        lengths_copy(k, lax.rem(o + NO - k, NO)).wait_recv()
        return carry

    def lengths_sent(k, carry):
        lengths_copy(k, o).wait_send()
        return carry

    lax.fori_loop(1, NO, lengths_start, 0)

    loads[0].wait()
    gather_wait(hid_g, hid_ss, hid_rs)
    unpack_all(hid_g, wide)
    q_g[t] = dot_t(rms(wide, again_ref), wq[...]).astype(BF16)
    gather_start(q_g, q_ss, q_rs)

    cache_copy(groups(down), groups(down), 0, up).wait_recv()
    cache_copy(groups(down), groups(down), 3, mate).start()
    cache_copy(groups(down, 0, half), groups(down, 0, half), 5, up).start()
    cache_copy(groups(up), groups(up), 1, down).wait_recv()
    cache_copy(groups(up), groups(up), 4, mate).start()
    cache_copy(groups(up, half, half), groups(up, half, half), 6, down).start()

    col = lanes((REQ, NO * SLOT))
    wanted = (col // SLOT) * 8 + t // 4
    hits = jnp.zeros((REQ, NO * SLOT), F32)
    share = jnp.zeros((REQ, NO * SLOT), F32)
    for k in range(6):
        match = routes_ref[:, k : k + 1] == wanted
        hits = jnp.where(match, 1.0, hits)
        share = jnp.where(match, rweight_ref[:, k : k + 1], share)
    below = (lanes((REQ, REQ)) < rows((REQ, REQ))).astype(BF16)
    rank = dot_n(below, hits.astype(BF16))
    picked = (hits > 0.5) & (rank == (col % SLOT).astype(F32))
    pick = jnp.where(picked, 1.0, 0.0)
    share = jnp.where(picked, share, 0.0)
    pick_t = jnp.transpose(pick).astype(BF16)

    r_iota = rows((REQ, 1))
    slen = jnp.zeros((REQ, 1), jnp.int32)
    gof = jnp.zeros((REQ, 1), jnp.int32)
    for r in range(REQ):
        slen = jnp.where(r_iota == r, slen_s[r], slen)
        gof = jnp.where(r_iota == r, gof_s[r], gof)
    lax.fori_loop(1, NO, lengths_wait, 0)
    lane128 = lanes((REQ, 128))
    glen_wide = jnp.zeros((REQ, 128), jnp.int32)
    for d in range(NO):
        mine = (gof - GROUP_OWN * d == lane128) & (lane128 < GROUP_OWN)
        glen_wide = jnp.where(mine, glr[d, 0:1, :], glen_wide)
    glen = jnp.sum(glen_wide, axis=1, keepdims=True)

    gather_wait(q_g, q_ss, q_rs)
    for h in range(H):
        a = q_g[2 * h]
        b = q_g[2 * h + 1]
        q_all[h, :, 0:256] = a[:, 0:256]
        q_all[h, :, 256:384] = (a[:, 256:384].astype(F32) + b[:, 0:128].astype(F32)).astype(BF16)
        q_all[h, :, 384:576] = b[:, 128:320]

    loads[1].wait()
    loads[2].wait()
    loads[3].wait()

    cache_copy(groups(far, 0, half), groups(far, 0, half), 5, up).wait_recv()
    cache_copy(groups(far, half, half), groups(far, half, half), 6, down).wait_recv()
    cache_copy(groups(far), groups(far), 7, mate).start()
    cache_copy(groups(mate), groups(mate), 2, mate).wait_recv()
    cache_copy(groups(mate_down), groups(mate_down), 3, mate).wait_recv()
    cache_copy(groups(mate_up), groups(mate_up), 4, mate).wait_recv()
    cache_copy(groups(mate_far), groups(mate_far), 7, mate).wait_recv()

    def fetch(r, carry):
        gg[r] = gc[gof_s[r]]
        return carry

    lax.fori_loop(0, REQ, fetch, 0)

    lane_p = lanes((16, 128))
    for c in range(2):
        r0 = 16 * c
        q = q_all[:, r0 : r0 + 16, :].reshape(256, KVW)
        root_out, root_mass = block_part(q, root[...], None)
        s_col = lanes((256, 256))
        s_row = rows((256, 256)) % 16
        s_len = jnp.concatenate([slen[r0 : r0 + 16]] * H, axis=0)
        s_ok = (s_col // 16 == s_row) & (t * 16 + s_col % 16 < s_len)
        sfx_out, sfx_mass = block_part(q, sfx[r0 : r0 + 16].reshape(256, KVW), s_ok)
        g_col = lanes((256, 512))
        g_row = rows((256, 512)) % 16
        g_len = jnp.concatenate([glen[r0 : r0 + 16]] * H, axis=0)
        g_ok = (g_col // 32 == g_row) & (t * 32 + g_col % 32 < g_len)
        grp_out, grp_mass = block_part(q, gg[r0 : r0 + 16].reshape(512, KVW), g_ok)
        grp_out = grp_out.astype(BF16).astype(F32)
        top = jnp.maximum(jnp.maximum(root_mass, sfx_mass), grp_mass)
        root_w = jnp.exp(root_mass - top)
        sfx_w = jnp.exp(sfx_mass - top)
        grp_w = jnp.exp(grp_mass - top)
        total = root_w + sfx_w + grp_w
        joined = ((root_w * root_out + sfx_w * sfx_out + grp_w * grp_out) / total).astype(BF16)
        mass = top + jnp.log(total)
        m0 = mass.astype(BF16).astype(F32)
        m1 = (mass - m0).astype(BF16).astype(F32)
        m2 = mass - m0 - m1
        for h in range(H):
            s = slice(16 * h, 16 * h + 16)
            po[2 * h + c, :, 0:LAT] = joined[s]
            po[2 * h + c, :, LAT : LAT + 128] = jnp.where(
                lane_p == 0,
                m0[s],
                jnp.where(lane_p == 1, m1[s], jnp.where(lane_p == 2, m2[s], 0.0)),
            ).astype(BF16)

    def part_start(k, carry):
        spread_copy(po, pr, p_ss, p_rs, "tensor", t, tpeer(k), t).start()
        return carry

    def part_wait(k, carry):
        p = lax.rem(t + NT - k, NT)
        spread_copy(po, pr, p_ss, p_rs, "tensor", t, p, p).wait_recv()
        return carry

    def part_sent(k, carry):
        spread_copy(po, pr, p_ss, p_rs, "tensor", t, tpeer(k), t).wait_send()
        return carry

    lax.fori_loop(1, NT, part_start, 0)
    pr[t] = po[t]
    lax.fori_loop(1, NT, part_wait, 0)

    masses = jnp.sum(pr[:, :, LAT : LAT + 128].astype(F32), axis=-1, keepdims=True)
    top = jnp.max(masses, axis=0, keepdims=True)
    w = jnp.exp(masses - top)
    acc = jnp.zeros((16, LAT), F32)
    for k in range(NT):
        acc = acc + w[k] * pr[k, :, 0:LAT].astype(F32)
    att_g[t] = (acc / jnp.sum(w, axis=0)).astype(BF16)
    gather_start(att_g, att_ss, att_rs)
    loads[4].wait()
    gather_wait(att_g, att_ss, att_rs)

    proj = jnp.zeros((REQ, 64), F32)
    for h in range(H):
        a = att_g[2 * h : 2 * h + 2].reshape(REQ, LAT)
        proj = proj + dot_t(a, wo[:, LAT * h : LAT * h + LAT])
    mid = (hidden_ref[...].astype(F32) + proj).astype(BF16)
    mid_g[t] = pack(mid)
    gather_start(mid_g, mid_ss, mid_rs)
    gather_wait(mid_g, mid_ss, mid_rs)
    unpack_all(mid_g, wide)
    mix = rms(wide, mgain_ref)

    sent = dot_n(pick_t, mix)
    for d in range(NO):
        s = sent[SLOT * d : SLOT * d + SLOT]
        dsp_s[d] = jnp.concatenate([s[:, :HALF], s[:, HALF:]], axis=0).astype(BF16)
    owner_start(dsp_s, dsp_r, dsp_ss, dsp_rs)
    dsp_r[o] = dsp_s[o]

    for n in range(5, 11):
        loads[n].wait()
    act = (silu(dot_t(mix, sg[...])) * dot_t(mix, su[...])).astype(BF16)
    part[...] = dot_n(act, sd[...])

    def slots(buf):
        low = jnp.concatenate([buf[d].astype(F32)[:SLOT] for d in range(NO)], axis=0)
        high = jnp.concatenate([buf[d].astype(F32)[SLOT:] for d in range(NO)], axis=0)
        return jnp.concatenate([low, high], axis=1).astype(BF16)

    owner_wait(dsp_s, dsp_r, dsp_ss, dsp_rs)
    x = slots(dsp_r)
    act = (silu(dot_t(x, eg[...])) * dot_t(x, eu[...])).astype(BF16)
    res = dot_n(act, ed[...])
    for d in range(NO):
        s = res[SLOT * d : SLOT * d + SLOT]
        ret_s[d] = jnp.concatenate([s[:, :HALF], s[:, HALF:]], axis=0).astype(BF16)
    owner_start(ret_s, ret_r, ret_ss, ret_rs)
    ret_r[o] = ret_s[o]
    s0 = share.astype(BF16)
    s1 = (share - s0.astype(F32)).astype(BF16)
    s2 = (share - s0.astype(F32) - s1.astype(F32)).astype(BF16)
    owner_wait(ret_s, ret_r, ret_ss, ret_rs)
    y = slots(ret_r)
    part[...] += dot_n(s0, y) + dot_n(s1, y) + dot_n(s2, y)

    low = lanes((16, 128)) < 64
    for i in range(NT // 2):
        a = part[0:16, 128 * i : 128 * i + 128]
        b = part[16:32, 128 * i : 128 * i + 128]
        rs_s[2 * i] = jnp.where(low, a, pltpu.roll(b, 64, 1)).astype(BF16)
        rs_s[2 * i + 1] = jnp.where(low, pltpu.roll(a, 64, 1), b).astype(BF16)

    def rs_start(k, carry):
        spread_copy(rs_s, rs_r, rs_ss, rs_rs, "tensor", t, tpeer(k), t).start()
        return carry

    def rs_wait(k, carry):
        p = lax.rem(t + NT - k, NT)
        spread_copy(rs_s, rs_r, rs_ss, rs_rs, "tensor", t, p, p).wait_recv()
        return carry

    def rs_sent(k, carry):
        spread_copy(rs_s, rs_r, rs_ss, rs_rs, "tensor", t, tpeer(k), t).wait_send()
        return carry

    lax.fori_loop(1, NT, rs_start, 0)
    rs_r[t] = rs_s[t]
    lax.fori_loop(1, NT, rs_wait, 0)
    total = jnp.zeros((16, 128), F32)
    for k in range(NT):
        total = total + rs_r[k].astype(F32)
    summed = jnp.concatenate([total, pltpu.roll(total, 64, 1)], axis=0)[:, :64]
    out_ref[...] = (mid.astype(F32) + summed).astype(BF16)

    gather_sent(hid_g, hid_ss, hid_rs)
    gather_sent(q_g, q_ss, q_rs)
    lax.fori_loop(1, NT, part_sent, 0)
    gather_sent(att_g, att_ss, att_rs)
    gather_sent(mid_g, mid_ss, mid_rs)
    owner_sent(dsp_s, dsp_r, dsp_ss, dsp_rs)
    owner_sent(ret_s, ret_r, ret_ss, ret_rs)
    lax.fori_loop(1, NT, rs_sent, 0)
    lax.fori_loop(1, NO, lengths_sent, 0)
    cache_copy(gcache_hbm, groups(o), 0, up).wait_send()
    cache_copy(gcache_hbm, groups(o), 1, down).wait_send()
    cache_copy(gcache_hbm, groups(o), 2, mate).wait_send()
    cache_copy(groups(down), groups(down), 3, mate).wait_send()
    cache_copy(groups(up), groups(up), 4, mate).wait_send()
    cache_copy(groups(down, 0, half), groups(down, 0, half), 5, up).wait_send()
    cache_copy(groups(up, half, half), groups(up, half, half), 6, down).wait_send()
    cache_copy(groups(far), groups(far), 7, mate).wait_send()


def local(
    hidden,
    attention_gain,
    query_weight,
    out_weight,
    root_cache,
    group_cache,
    group_length,
    suffix_cache,
    suffix_length,
    group_of,
    mixture_gain,
    routes,
    route_weight,
    expert_gate,
    expert_up,
    expert_down,
    shared_gate,
    shared_up,
    shared_down,
):
    vmem = pl.BlockSpec(memory_space=pltpu.VMEM)
    smem = pl.BlockSpec(memory_space=pltpu.SMEM)
    hbm = pl.BlockSpec(memory_space=pl.ANY)
    dma = pltpu.SemaphoreType.DMA
    return pl.pallas_call(
        kernel,
        out_shape=jax.ShapeDtypeStruct((REQ, 64), BF16),
        in_specs=[
            vmem, vmem, hbm, hbm, hbm, hbm, smem, hbm, smem, smem, vmem, vmem, vmem,
            hbm, hbm, hbm, hbm, hbm, hbm,
        ],
        out_specs=vmem,
        scratch_shapes=[
            pltpu.VMEM((384, D), BF16),
            pltpu.VMEM((64, H * LAT), BF16),
            pltpu.VMEM((1024, KVW), BF16),
            pltpu.VMEM((NO * GROUP_OWN, 32, KVW), BF16),
            pltpu.VMEM((REQ, 32, KVW), BF16),
            pltpu.VMEM((REQ, 16, KVW), BF16),
            pltpu.VMEM((352, D), BF16),
            pltpu.VMEM((352, D), BF16),
            pltpu.VMEM((352, D), BF16),
            pltpu.VMEM((88, D), BF16),
            pltpu.VMEM((88, D), BF16),
            pltpu.VMEM((88, D), BF16),
            pltpu.VMEM((NO, 8, 128), jnp.int32),
            pltpu.VMEM((NT, 16, 128), BF16),
            pltpu.VMEM((NT, REQ, 384), BF16),
            pltpu.VMEM((H, REQ, KVW), BF16),
            pltpu.VMEM((NT, 16, LAT + 128), BF16),
            pltpu.VMEM((NT, 16, LAT + 128), BF16),
            pltpu.VMEM((NT, 16, LAT), BF16),
            pltpu.VMEM((NT, 16, 128), BF16),
            pltpu.VMEM((NO, 2 * SLOT, HALF), BF16),
            pltpu.VMEM((NO, 2 * SLOT, HALF), BF16),
            pltpu.VMEM((NO, 2 * SLOT, HALF), BF16),
            pltpu.VMEM((NO, 2 * SLOT, HALF), BF16),
            pltpu.VMEM((NT, 16, 128), BF16),
            pltpu.VMEM((NT, 16, 128), BF16),
            pltpu.VMEM((REQ, D), F32),
            pltpu.VMEM((REQ, D), F32),
            dma((11,)),
        ]
        + [dma((NT,))] * 12
        + [dma((NO,))] * 8,
        compiler_params=pltpu.CompilerParams(
            collective_id=0, has_side_effects=True, vmem_limit_bytes=60 * 1024 * 1024
        ),
        name="layer",
    )(
        hidden,
        attention_gain.reshape(1, D),
        query_weight,
        out_weight,
        root_cache,
        group_cache,
        group_length,
        suffix_cache,
        suffix_length,
        group_of,
        mixture_gain.reshape(1, D),
        routes,
        route_weight,
        expert_gate,
        expert_up,
        expert_down,
        shared_gate,
        shared_up,
        shared_down,
    )


def solution(mesh):
    return jax.shard_map(
        local,
        mesh=mesh,
        in_specs=(
            P("owner", "tensor"),
            P(),
            P("tensor", None),
            P("tensor", None),
            P("tensor", None),
            P("owner", "tensor", None),
            P("owner"),
            P("owner", "tensor", None),
            P("owner"),
            P("owner"),
            P(),
            P("owner", None),
            P("owner", None),
            P(("owner", "tensor"), None, None),
            P(("owner", "tensor"), None, None),
            P(("owner", "tensor"), None, None),
            P("tensor", None),
            P("tensor", None),
            P("tensor", None),
        ),
        out_specs=P("owner", "tensor"),
        check_vma=False,
    )
```

```python
import functools

import jax
import jax.numpy as jnp
from jax import lax
from jax.experimental import pallas as pl
from jax.experimental.pallas import tpu as pltpu
from jax.sharding import PartitionSpec as P

D = 2048
H = 16
LAT = 512
KVW = 576
GROUP_OWN = 12
REQ = 32
NT = 32
NO = 8
SLOT = 8
HALF = 1024
SCALE = 192.0 ** (-0.5)
LOWEST = -1e30
EPS = 1e-06
MESH = pl.DeviceIdType.MESH
F32 = jnp.float32
BF16 = jnp.bfloat16


def dot_t(a, b):
    return lax.dot_general(a, b, (((1,), (1,)), ((), ())), preferred_element_type=F32)


def dot_n(a, b):
    return lax.dot_general(a, b, (((1,), (0,)), ((), ())), preferred_element_type=F32)


def lanes(shape):
    return lax.broadcasted_iota(jnp.int32, shape, len(shape) - 1)


def rows(shape):
    return lax.broadcasted_iota(jnp.int32, shape, len(shape) - 2)


def pack(x):
    return jnp.concatenate([x[:16], x[16:]], axis=1)


def unpack_all(blocks_ref, wide_ref):
    low = lanes((16, 128)) < 64
    for i in range(NT // 2):
        a = blocks_ref[2 * i].astype(F32)
        b = blocks_ref[2 * i + 1].astype(F32)
        wide_ref[0:16, 128 * i : 128 * i + 128] = jnp.where(low, a, pltpu.roll(b, 64, 1))
        wide_ref[16:32, 128 * i : 128 * i + 128] = jnp.where(low, pltpu.roll(a, 64, 1), b)


def rms(wide_ref, gain_ref):
    x = wide_ref[...]
    scaled = x * lax.rsqrt(jnp.mean(x * x, axis=-1, keepdims=True) + EPS)
    return (scaled * gain_ref[...].astype(F32)[None, :]).astype(BF16)


def block_part(q, keys, usable, keys_t=None):
    scores = (dot_t(q, keys) if keys_t is None else dot_n(q, keys_t)) * SCALE
    if usable is not None:
        scores = jnp.where(usable, scores, LOWEST)
    peak = jnp.max(scores, axis=-1, keepdims=True)
    weights = jnp.exp(scores - peak)
    if usable is not None:
        weights = jnp.where(usable, weights, 0.0)
    total = jnp.sum(weights, axis=-1, keepdims=True)
    weights = weights.astype(BF16)
    numerator = dot_n(weights, keys[:, :LAT]) if keys_t is None else dot_t(weights, keys_t[:LAT])
    present = total > 0.0
    safe = jnp.where(present, total, 1.0)
    return numerator / safe, jnp.where(present, peak + jnp.log(safe), LOWEST)


def silu(v):
    return v / (1.0 + jnp.exp(-v))


def kernel(
    hidden_ref,
    again_ref,
    wq_hbm,
    wo_hbm,
    root_hbm,
    gcache_hbm,
    glen_s,
    sfx_hbm,
    slen_s,
    gof_s,
    mgain_ref,
    routes_ref,
    rweight_ref,
    eg_hbm,
    eu_hbm,
    ed_hbm,
    sg_hbm,
    su_hbm,
    sd_hbm,
    out_ref,
    wq,
    wo,
    root,
    gc,
    gg,
    sfx,
    eg,
    eu,
    ed,
    sg,
    su,
    sd,
    glr,
    hid_g,
    q_g,
    q_all,
    po,
    pr,
    att_g,
    mid_g,
    dsp_s,
    dsp_r,
    ret_s,
    ret_r,
    rs_s,
    rs_r,
    wide,
    part,
    load_sem,
    hid_ss,
    hid_rs,
    q_ss,
    q_rs,
    p_ss,
    p_rs,
    att_ss,
    att_rs,
    mid_ss,
    mid_rs,
    rs_ss,
    rs_rs,
    dsp_ss,
    dsp_rs,
    ret_ss,
    ret_rs,
    gl_ss,
    gl_rs,
    gc_ss,
    gc_rs,
):
    o = lax.axis_index("owner")
    t = lax.axis_index("tensor")

    def tpeer(k):
        return lax.rem(t + k, NT)

    def opeer(k):
        return lax.rem(o + k, NO)

    wq[0:32, :] = jnp.zeros((32, D), BF16)
    wq[288:384, :] = jnp.zeros((96, D), BF16)
    shift = pl.multiple_of(lax.rem(t, 2) * 32, 32)
    loads = [
        pltpu.make_async_copy(wq_hbm, wq.at[pl.ds(shift, 288)], load_sem.at[0]),
        pltpu.make_async_copy(root_hbm, root, load_sem.at[1]),
        pltpu.make_async_copy(sfx_hbm, sfx, load_sem.at[2]),
        pltpu.make_async_copy(
            gcache_hbm, gc.at[pl.ds(GROUP_OWN * o, GROUP_OWN)], load_sem.at[3]
        ),
        pltpu.make_async_copy(wo_hbm, wo, load_sem.at[4]),
        pltpu.make_async_copy(sg_hbm, sg, load_sem.at[5]),
        pltpu.make_async_copy(su_hbm, su, load_sem.at[6]),
        pltpu.make_async_copy(sd_hbm, sd, load_sem.at[7]),
        pltpu.make_async_copy(eg_hbm.at[0], eg, load_sem.at[8]),
        pltpu.make_async_copy(eu_hbm.at[0], eu, load_sem.at[9]),
        pltpu.make_async_copy(ed_hbm.at[0], ed, load_sem.at[10]),
    ]
    for load in loads:
        load.start()

    hid_g[t] = pack(hidden_ref[...])
    lane_row = lanes((8, 128))
    own_lengths = jnp.zeros((8, 128), jnp.int32)
    for g in range(GROUP_OWN):
        own_lengths = jnp.where(lane_row == g, glen_s[g], own_lengths)
    glr[o] = own_lengths

    barrier = pltpu.get_barrier_semaphore()

    def greet_tensor(k, carry):
        pl.semaphore_signal(
            barrier, inc=1, device_id={"tensor": tpeer(k)}, device_id_type=MESH
        )
        return carry

    def greet_owner(k, carry):
        pl.semaphore_signal(
            barrier, inc=1, device_id={"owner": opeer(k)}, device_id_type=MESH
        )
        return carry

    lax.fori_loop(1, NT, greet_tensor, 0)
    lax.fori_loop(1, NO, greet_owner, 0)
    pl.semaphore_wait(barrier, NT - 1 + NO - 1)

    def gather_copy(buf, ss, rs, k, slot):
        return pltpu.make_async_remote_copy(
            src_ref=buf.at[slot],
            dst_ref=buf.at[slot],
            send_sem=ss.at[k],
            recv_sem=rs.at[slot],
            device_id={"tensor": tpeer(k)},
            device_id_type=MESH,
        )

    def gather_start(buf, ss, rs):
        def step(k, carry):
            gather_copy(buf, ss, rs, k, t).start()
            return carry

        lax.fori_loop(1, NT, step, 0)

    def gather_wait(buf, ss, rs):
        def step(k, carry):
            gather_copy(buf, ss, rs, k, lax.rem(t + NT - k, NT)).wait_recv()
            return carry

        lax.fori_loop(1, NT, step, 0)

    def gather_sent(buf, ss, rs):
        def step(k, carry):
            gather_copy(buf, ss, rs, k, t).wait_send()
            return carry

        lax.fori_loop(1, NT, step, 0)

    def spread_copy(src, dst, ss, rs, axis, me, peer, came_from):
        return pltpu.make_async_remote_copy(
            src_ref=src.at[peer],
            dst_ref=dst.at[came_from],
            send_sem=ss.at[peer],
            recv_sem=rs.at[came_from],
            device_id={axis: peer},
            device_id_type=MESH,
        )

    def owner_start(src, dst, ss, rs):
        def step(k, carry):
            spread_copy(src, dst, ss, rs, "owner", o, opeer(k), o).start()
            return carry

        lax.fori_loop(1, NO, step, 0)

    def owner_wait(src, dst, ss, rs):
        def step(k, carry):
            p = opeer(k)
            spread_copy(src, dst, ss, rs, "owner", o, p, p).wait_recv()
            return carry

        lax.fori_loop(1, NO, step, 0)

    def owner_sent(src, dst, ss, rs):
        def step(k, carry):
            spread_copy(src, dst, ss, rs, "owner", o, opeer(k), o).wait_send()
            return carry

        lax.fori_loop(1, NO, step, 0)

    gather_start(hid_g, hid_ss, hid_rs)

    up = opeer(2)
    down = opeer(6)
    far = opeer(4)
    mate = o + 1 - 2 * lax.rem(o, 2)

    def groups(owner, first=0, count=GROUP_OWN):
        return gc.at[pl.ds(GROUP_OWN * owner + first, count)]

    def cache_copy(src, dst, n, to):
        return pltpu.make_async_remote_copy(
            src_ref=src,
            dst_ref=dst,
            send_sem=gc_ss.at[n],
            recv_sem=gc_rs.at[n],
            device_id={"owner": to},
            device_id_type=MESH,
        )

    half = GROUP_OWN // 2
    mate_up = lax.rem(mate + 2, NO)
    mate_down = lax.rem(mate + 6, NO)
    mate_far = lax.rem(mate + 4, NO)
    cache_copy(gcache_hbm, groups(o), 0, up).start()
    cache_copy(gcache_hbm, groups(o), 1, down).start()
    cache_copy(gcache_hbm, groups(o), 2, mate).start()

    def lengths_copy(k, slot):
        return pltpu.make_async_remote_copy(
            src_ref=glr.at[slot],
            dst_ref=glr.at[slot],
            send_sem=gl_ss.at[k],
            recv_sem=gl_rs.at[slot],
            device_id={"owner": opeer(k)},
            device_id_type=MESH,
        )

    def lengths_start(k, carry):
        lengths_copy(k, o).start()
        return carry

    def lengths_wait(k, carry):
        lengths_copy(k, lax.rem(o + NO - k, NO)).wait_recv()
        return carry

    def lengths_sent(k, carry):
        lengths_copy(k, o).wait_send()
        return carry

    lax.fori_loop(1, NO, lengths_start, 0)

    loads[0].wait()
    gather_wait(hid_g, hid_ss, hid_rs)
    unpack_all(hid_g, wide)
    q_g[t] = dot_t(rms(wide, again_ref), wq[...]).astype(BF16)
    gather_start(q_g, q_ss, q_rs)

    cache_copy(groups(down), groups(down), 0, up).wait_recv()
    cache_copy(groups(down), groups(down), 3, mate).start()
    cache_copy(groups(down, 0, half), groups(down, 0, half), 5, up).start()
    cache_copy(groups(up), groups(up), 1, down).wait_recv()
    cache_copy(groups(up), groups(up), 4, mate).start()
    cache_copy(groups(up, half, half), groups(up, half, half), 6, down).start()

    row = rows((NO * SLOT, REQ))
    wanted = (row // SLOT) * 8 + t // 4
    hits = jnp.zeros((NO * SLOT, REQ), F32)
    share = jnp.zeros((NO * SLOT, REQ), F32)
    for k in range(6):
        match = routes_ref[k : k + 1, :] == wanted
        hits = jnp.where(match, 1.0, hits)
        share = jnp.where(match, rweight_ref[k : k + 1, :], share)
    before = (rows((REQ, REQ)) < lanes((REQ, REQ))).astype(BF16)
    rank = dot_n(hits.astype(BF16), before)
    picked = (hits > 0.5) & (rank == (row % SLOT).astype(F32))
    pick_t = jnp.where(picked, 1.0, 0.0).astype(BF16)
    share = jnp.transpose(jnp.where(picked, share, 0.0))

    r_iota = rows((REQ, 1))
    slen = jnp.zeros((REQ, 1), jnp.int32)
    gof = jnp.zeros((REQ, 1), jnp.int32)
    for r in range(REQ):
        slen = jnp.where(r_iota == r, slen_s[r], slen)
        gof = jnp.where(r_iota == r, gof_s[r], gof)
    lax.fori_loop(1, NO, lengths_wait, 0)
    lane128 = lanes((REQ, 128))
    glen_wide = jnp.zeros((REQ, 128), jnp.int32)
    for d in range(NO):
        mine = (gof - GROUP_OWN * d == lane128) & (lane128 < GROUP_OWN)
        glen_wide = jnp.where(mine, glr[d, 0:1, :], glen_wide)
    glen = jnp.sum(glen_wide, axis=1, keepdims=True)

    gather_wait(q_g, q_ss, q_rs)
    for h in range(H):
        a = q_g[2 * h]
        b = q_g[2 * h + 1]
        q_all[h, :, 0:256] = a[:, 0:256]
        q_all[h, :, 256:384] = (a[:, 256:384].astype(F32) + b[:, 0:128].astype(F32)).astype(BF16)
        q_all[h, :, 384:576] = b[:, 128:320]

    loads[1].wait()
    loads[2].wait()
    loads[3].wait()

    cache_copy(groups(far, 0, half), groups(far, 0, half), 5, up).wait_recv()
    cache_copy(groups(far, half, half), groups(far, half, half), 6, down).wait_recv()
    cache_copy(groups(far), groups(far), 7, mate).start()
    cache_copy(groups(mate), groups(mate), 2, mate).wait_recv()
    cache_copy(groups(mate_down), groups(mate_down), 3, mate).wait_recv()
    cache_copy(groups(mate_up), groups(mate_up), 4, mate).wait_recv()
    cache_copy(groups(mate_far), groups(mate_far), 7, mate).wait_recv()

    def fetch(r, carry):
        gg[r] = gc[gof_s[r]]
        return carry

    lax.fori_loop(0, REQ, fetch, 0)

    lane_p = lanes((16, 128))
    for c in range(2):
        r0 = 16 * c
        q = q_all[:, r0 : r0 + 16, :].reshape(256, KVW)
        root_out, root_mass = block_part(q, None, None, root[...])
        s_col = lanes((256, 256))
        s_row = rows((256, 256)) % 16
        s_len = jnp.concatenate([slen[r0 : r0 + 16]] * H, axis=0)
        s_ok = (s_col // 16 == s_row) & (t * 16 + s_col % 16 < s_len)
        sfx_out, sfx_mass = block_part(q, sfx[r0 : r0 + 16].reshape(256, KVW), s_ok)
        g_col = lanes((256, 512))
        g_row = rows((256, 512)) % 16
        g_len = jnp.concatenate([glen[r0 : r0 + 16]] * H, axis=0)
        g_ok = (g_col // 32 == g_row) & (t * 32 + g_col % 32 < g_len)
        grp_out, grp_mass = block_part(q, gg[r0 : r0 + 16].reshape(512, KVW), g_ok)
        grp_out = grp_out.astype(BF16).astype(F32)
        top = jnp.maximum(jnp.maximum(root_mass, sfx_mass), grp_mass)
        root_w = jnp.exp(root_mass - top)
        sfx_w = jnp.exp(sfx_mass - top)
        grp_w = jnp.exp(grp_mass - top)
        total = root_w + sfx_w + grp_w
        joined = ((root_w * root_out + sfx_w * sfx_out + grp_w * grp_out) / total).astype(BF16)
        mass = top + jnp.log(total)
        m0 = mass.astype(BF16).astype(F32)
        m1 = (mass - m0).astype(BF16).astype(F32)
        m2 = mass - m0 - m1
        for h in range(H):
            s = slice(16 * h, 16 * h + 16)
            po[2 * h + c, :, 0:LAT] = joined[s]
            po[2 * h + c, :, LAT : LAT + 128] = jnp.where(
                lane_p == 0,
                m0[s],
                jnp.where(lane_p == 1, m1[s], jnp.where(lane_p == 2, m2[s], 0.0)),
            ).astype(BF16)

    def part_start(k, carry):
        spread_copy(po, pr, p_ss, p_rs, "tensor", t, tpeer(k), t).start()
        return carry

    def part_wait(k, carry):
        p = lax.rem(t + NT - k, NT)
        spread_copy(po, pr, p_ss, p_rs, "tensor", t, p, p).wait_recv()
        return carry

    def part_sent(k, carry):
        spread_copy(po, pr, p_ss, p_rs, "tensor", t, tpeer(k), t).wait_send()
        return carry

    lax.fori_loop(1, NT, part_start, 0)
    pr[t] = po[t]
    lax.fori_loop(1, NT, part_wait, 0)

    masses = jnp.sum(pr[:, :, LAT : LAT + 128].astype(F32), axis=-1, keepdims=True)
    top = jnp.max(masses, axis=0, keepdims=True)
    w = jnp.exp(masses - top)
    acc = jnp.zeros((16, LAT), F32)
    for k in range(NT):
        acc = acc + w[k] * pr[k, :, 0:LAT].astype(F32)
    att_g[t] = (acc / jnp.sum(w, axis=0)).astype(BF16)
    gather_start(att_g, att_ss, att_rs)
    loads[4].wait()
    gather_wait(att_g, att_ss, att_rs)

    proj = jnp.zeros((REQ, 64), F32)
    for h in range(H):
        a = att_g[2 * h : 2 * h + 2].reshape(REQ, LAT)
        proj = proj + dot_t(a, wo[:, LAT * h : LAT * h + LAT])
    mid = (hidden_ref[...].astype(F32) + proj).astype(BF16)
    mid_g[t] = pack(mid)
    gather_start(mid_g, mid_ss, mid_rs)
    gather_wait(mid_g, mid_ss, mid_rs)
    unpack_all(mid_g, wide)
    mix = rms(wide, mgain_ref)

    sent = dot_n(pick_t, mix)
    for d in range(NO):
        s = sent[SLOT * d : SLOT * d + SLOT]
        dsp_s[d] = jnp.concatenate([s[:, :HALF], s[:, HALF:]], axis=0).astype(BF16)
    owner_start(dsp_s, dsp_r, dsp_ss, dsp_rs)
    dsp_r[o] = dsp_s[o]

    for n in range(5, 11):
        loads[n].wait()
    act = (silu(dot_t(mix, sg[...])) * dot_t(mix, su[...])).astype(BF16)
    part[...] = dot_n(act, sd[...])

    def slots(buf):
        low = jnp.concatenate([buf[d].astype(F32)[:SLOT] for d in range(NO)], axis=0)
        high = jnp.concatenate([buf[d].astype(F32)[SLOT:] for d in range(NO)], axis=0)
        return jnp.concatenate([low, high], axis=1).astype(BF16)

    owner_wait(dsp_s, dsp_r, dsp_ss, dsp_rs)
    x = slots(dsp_r)
    act = (silu(dot_t(x, eg[...])) * dot_t(x, eu[...])).astype(BF16)
    res = dot_n(act, ed[...])
    for d in range(NO):
        s = res[SLOT * d : SLOT * d + SLOT]
        ret_s[d] = jnp.concatenate([s[:, :HALF], s[:, HALF:]], axis=0).astype(BF16)
    owner_start(ret_s, ret_r, ret_ss, ret_rs)
    ret_r[o] = ret_s[o]
    s0 = share.astype(BF16)
    s1 = (share - s0.astype(F32)).astype(BF16)
    s2 = (share - s0.astype(F32) - s1.astype(F32)).astype(BF16)
    owner_wait(ret_s, ret_r, ret_ss, ret_rs)
    y = slots(ret_r)
    part[...] += dot_n(s0, y) + dot_n(s1, y) + dot_n(s2, y)

    low = lanes((16, 128)) < 64
    for i in range(NT // 2):
        a = part[0:16, 128 * i : 128 * i + 128]
        b = part[16:32, 128 * i : 128 * i + 128]
        rs_s[2 * i] = jnp.where(low, a, pltpu.roll(b, 64, 1)).astype(BF16)
        rs_s[2 * i + 1] = jnp.where(low, pltpu.roll(a, 64, 1), b).astype(BF16)

    def rs_start(k, carry):
        spread_copy(rs_s, rs_r, rs_ss, rs_rs, "tensor", t, tpeer(k), t).start()
        return carry

    def rs_wait(k, carry):
        p = lax.rem(t + NT - k, NT)
        spread_copy(rs_s, rs_r, rs_ss, rs_rs, "tensor", t, p, p).wait_recv()
        return carry

    def rs_sent(k, carry):
        spread_copy(rs_s, rs_r, rs_ss, rs_rs, "tensor", t, tpeer(k), t).wait_send()
        return carry

    lax.fori_loop(1, NT, rs_start, 0)
    rs_r[t] = rs_s[t]
    lax.fori_loop(1, NT, rs_wait, 0)
    total = jnp.zeros((16, 128), F32)
    for k in range(NT):
        total = total + rs_r[k].astype(F32)
    summed = jnp.concatenate([total, pltpu.roll(total, 64, 1)], axis=0)[:, :64]
    out_ref[...] = (mid.astype(F32) + summed).astype(BF16)

    gather_sent(hid_g, hid_ss, hid_rs)
    gather_sent(q_g, q_ss, q_rs)
    lax.fori_loop(1, NT, part_sent, 0)
    gather_sent(att_g, att_ss, att_rs)
    gather_sent(mid_g, mid_ss, mid_rs)
    owner_sent(dsp_s, dsp_r, dsp_ss, dsp_rs)
    owner_sent(ret_s, ret_r, ret_ss, ret_rs)
    lax.fori_loop(1, NT, rs_sent, 0)
    lax.fori_loop(1, NO, lengths_sent, 0)
    cache_copy(gcache_hbm, groups(o), 0, up).wait_send()
    cache_copy(gcache_hbm, groups(o), 1, down).wait_send()
    cache_copy(gcache_hbm, groups(o), 2, mate).wait_send()
    cache_copy(groups(down), groups(down), 3, mate).wait_send()
    cache_copy(groups(up), groups(up), 4, mate).wait_send()
    cache_copy(groups(down, 0, half), groups(down, 0, half), 5, up).wait_send()
    cache_copy(groups(up, half, half), groups(up, half, half), 6, down).wait_send()
    cache_copy(groups(far), groups(far), 7, mate).wait_send()


def local(
    hidden,
    attention_gain,
    query_weight,
    out_weight,
    root_cache,
    group_cache,
    group_length,
    suffix_cache,
    suffix_length,
    group_of,
    mixture_gain,
    routes,
    route_weight,
    expert_gate,
    expert_up,
    expert_down,
    shared_gate,
    shared_up,
    shared_down,
):
    vmem = pl.BlockSpec(memory_space=pltpu.VMEM)
    smem = pl.BlockSpec(memory_space=pltpu.SMEM)
    hbm = pl.BlockSpec(memory_space=pl.ANY)
    dma = pltpu.SemaphoreType.DMA
    return pl.pallas_call(
        kernel,
        out_shape=jax.ShapeDtypeStruct((REQ, 64), BF16),
        in_specs=[
            vmem, vmem, hbm, hbm, hbm, hbm, smem, hbm, smem, smem, vmem, vmem, vmem,
            hbm, hbm, hbm, hbm, hbm, hbm,
        ],
        out_specs=vmem,
        scratch_shapes=[
            pltpu.VMEM((384, D), BF16),
            pltpu.VMEM((64, H * LAT), BF16),
            pltpu.VMEM((KVW, 1024), BF16),
            pltpu.VMEM((NO * GROUP_OWN, 32, KVW), BF16),
            pltpu.VMEM((REQ, 32, KVW), BF16),
            pltpu.VMEM((REQ, 16, KVW), BF16),
            pltpu.VMEM((352, D), BF16),
            pltpu.VMEM((352, D), BF16),
            pltpu.VMEM((352, D), BF16),
            pltpu.VMEM((88, D), BF16),
            pltpu.VMEM((88, D), BF16),
            pltpu.VMEM((88, D), BF16),
            pltpu.VMEM((NO, 8, 128), jnp.int32),
            pltpu.VMEM((NT, 16, 128), BF16),
            pltpu.VMEM((NT, REQ, 384), BF16),
            pltpu.VMEM((H, REQ, KVW), BF16),
            pltpu.VMEM((NT, 16, LAT + 128), BF16),
            pltpu.VMEM((NT, 16, LAT + 128), BF16),
            pltpu.VMEM((NT, 16, LAT), BF16),
            pltpu.VMEM((NT, 16, 128), BF16),
            pltpu.VMEM((NO, 2 * SLOT, HALF), BF16),
            pltpu.VMEM((NO, 2 * SLOT, HALF), BF16),
            pltpu.VMEM((NO, 2 * SLOT, HALF), BF16),
            pltpu.VMEM((NO, 2 * SLOT, HALF), BF16),
            pltpu.VMEM((NT, 16, 128), BF16),
            pltpu.VMEM((NT, 16, 128), BF16),
            pltpu.VMEM((REQ, D), F32),
            pltpu.VMEM((REQ, D), F32),
            dma((11,)),
        ]
        + [dma((NT,))] * 12
        + [dma((NO,))] * 8,
        compiler_params=pltpu.CompilerParams(
            collective_id=0, has_side_effects=True, vmem_limit_bytes=60 * 1024 * 1024
        ),
        name="layer",
    )(
        hidden,
        attention_gain,
        query_weight,
        out_weight,
        root_cache.T,
        group_cache,
        group_length,
        suffix_cache,
        suffix_length,
        group_of,
        mixture_gain,
        routes.T,
        route_weight.T,
        expert_gate,
        expert_up,
        expert_down,
        shared_gate,
        shared_up,
        shared_down,
    )


def solution(mesh):
    return jax.shard_map(
        local,
        mesh=mesh,
        in_specs=(
            P("owner", "tensor"),
            P(),
            P("tensor", None),
            P("tensor", None),
            P("tensor", None),
            P("owner", "tensor", None),
            P("owner"),
            P("owner", "tensor", None),
            P("owner"),
            P("owner"),
            P(),
            P("owner", None),
            P("owner", None),
            P(("owner", "tensor"), None, None),
            P(("owner", "tensor"), None, None),
            P(("owner", "tensor"), None, None),
            P("tensor", None),
            P("tensor", None),
            P("tensor", None),
        ),
        out_specs=P("owner", "tensor"),
        check_vma=False,
    )
```

```python
import functools

import jax
import jax.numpy as jnp
from jax import lax
from jax.experimental import pallas as pl
from jax.experimental.pallas import tpu as pltpu
from jax.sharding import PartitionSpec as P

D = 2048
H = 16
LAT = 512
KVW = 576
GROUP_OWN = 12
REQ = 32
NT = 32
NO = 8
SLOT = 8
HALF = 1024
HG = 4
SCALE = 192.0 ** (-0.5)
LOWEST = -1e30
EPS = 1e-06
MESH = pl.DeviceIdType.MESH
F32 = jnp.float32
BF16 = jnp.bfloat16


def dot_t(a, b):
    return lax.dot_general(a, b, (((1,), (1,)), ((), ())), preferred_element_type=F32)


def dot_n(a, b):
    return lax.dot_general(a, b, (((1,), (0,)), ((), ())), preferred_element_type=F32)


def lanes(shape):
    return lax.broadcasted_iota(jnp.int32, shape, len(shape) - 1)


def rows(shape):
    return lax.broadcasted_iota(jnp.int32, shape, len(shape) - 2)


def pack(x):
    return jnp.concatenate([x[:16], x[16:]], axis=1)


def unpack_all(blocks_ref, wide_ref):
    low = lanes((16, 128)) < 64
    for i in range(NT // 2):
        a = blocks_ref[2 * i].astype(F32)
        b = blocks_ref[2 * i + 1].astype(F32)
        wide_ref[0:16, 128 * i : 128 * i + 128] = jnp.where(low, a, pltpu.roll(b, 64, 1))
        wide_ref[16:32, 128 * i : 128 * i + 128] = jnp.where(low, pltpu.roll(a, 64, 1), b)


def rms(wide_ref, gain_ref):
    x = wide_ref[...]
    scaled = x * lax.rsqrt(jnp.mean(x * x, axis=-1, keepdims=True) + EPS)
    return (scaled * gain_ref[...].astype(F32)[None, :]).astype(BF16)


def block_part(q, keys, usable, keys_t=None):
    scores = (dot_t(q, keys) if keys_t is None else dot_n(q, keys_t)) * SCALE
    if usable is not None:
        scores = jnp.where(usable, scores, LOWEST)
    peak = jnp.max(scores, axis=-1, keepdims=True)
    weights = jnp.exp(scores - peak)
    if usable is not None:
        weights = jnp.where(usable, weights, 0.0)
    total = jnp.sum(weights, axis=-1, keepdims=True)
    weights = weights.astype(BF16)
    numerator = dot_n(weights, keys[:, :LAT]) if keys_t is None else dot_t(weights, keys_t[:LAT])
    present = total > 0.0
    safe = jnp.where(present, total, 1.0)
    return numerator / safe, jnp.where(present, peak + jnp.log(safe), LOWEST)


def join(first, second):
    first_out, first_mass = first
    second_out, second_mass = second
    top = jnp.maximum(first_mass, second_mass)
    first_w = jnp.exp(first_mass - top)
    second_w = jnp.exp(second_mass - top)
    total = first_w + second_w
    return (first_w * first_out + second_w * second_out) / total, top + jnp.log(total)


def silu(v):
    return v / (1.0 + jnp.exp(-v))


def kernel(
    hidden_ref,
    again_ref,
    wq_hbm,
    wo_hbm,
    root_hbm,
    gcache_hbm,
    glen_s,
    sfx_hbm,
    slen_s,
    gof_s,
    mgain_ref,
    routes_ref,
    rweight_ref,
    eg_hbm,
    eu_hbm,
    ed_hbm,
    sg_hbm,
    su_hbm,
    sd_hbm,
    out_ref,
    wq,
    wo,
    root,
    gc,
    gg,
    sfx,
    eg,
    eu,
    ed,
    sg,
    su,
    sd,
    glr,
    hid_g,
    q_g,
    q_all,
    rs_out,
    rs_mass,
    po,
    pr,
    pm,
    pmr,
    att_g,
    mid_g,
    dsp_s,
    dsp_r,
    ret_s,
    ret_r,
    rs_s,
    rs_r,
    wide,
    part,
    load_sem,
    hid_ss,
    hid_rs,
    q_ss,
    q_rs,
    p_ss,
    p_rs,
    pm_ss,
    pm_rs,
    att_ss,
    att_rs,
    mid_ss,
    mid_rs,
    rs_ss,
    rs_rs,
    dsp_ss,
    dsp_rs,
    ret_ss,
    ret_rs,
    gl_ss,
    gl_rs,
    gc_ss,
    gc_rs,
):
    o = lax.axis_index("owner")
    t = lax.axis_index("tensor")

    def tpeer(k):
        return lax.rem(t + k, NT)

    def opeer(k):
        return lax.rem(o + k, NO)

    x = t // 8
    z = lax.rem(t, 8)
    open_recv = {}
    open_send = {}

    def remote(src, dst, ss, rs, to):
        return pltpu.make_async_remote_copy(
            src_ref=src, dst_ref=dst, send_sem=ss, recv_sem=rs, device_id=to, device_id_type=MESH
        )

    def over(first, last, step):
        def body(k, carry):
            step(k)
            return carry

        lax.fori_loop(first, last, body, 0)

    def far_first(n):
        kz = n // 4
        kx = lax.rem(n, 4)
        dz = 4 + (1 - 2 * lax.rem(kz, 2)) * ((kz + 1) // 2)
        dx = 2 + (1 - 2 * lax.rem(kx, 2)) * ((kx + 1) // 2)
        return lax.rem(x + dx, 4) * 8 + lax.rem(z + dz, 8)

    barrier = pltpu.get_barrier_semaphore()

    def greet(to):
        pl.semaphore_signal(barrier, inc=1, device_id=to, device_id_type=MESH)

    over(0, NT - 1, lambda n: greet({"tensor": far_first(n)}))
    over(1, NO, lambda k: greet({"owner": opeer(k)}))

    wq[0:32, :] = jnp.zeros((32, D), BF16)
    wq[288:384, :] = jnp.zeros((96, D), BF16)
    shift = pl.multiple_of(lax.rem(t, 2) * 32, 32)
    loads = [
        pltpu.make_async_copy(wq_hbm, wq.at[pl.ds(shift, 288)], load_sem.at[0]),
        pltpu.make_async_copy(root_hbm, root, load_sem.at[1]),
        pltpu.make_async_copy(sfx_hbm, sfx, load_sem.at[2]),
        pltpu.make_async_copy(
            gcache_hbm, gc.at[pl.ds(GROUP_OWN * o, GROUP_OWN)], load_sem.at[3]
        ),
        pltpu.make_async_copy(wo_hbm, wo, load_sem.at[4]),
        pltpu.make_async_copy(sg_hbm, sg, load_sem.at[5]),
        pltpu.make_async_copy(su_hbm, su, load_sem.at[6]),
        pltpu.make_async_copy(sd_hbm, sd, load_sem.at[7]),
        pltpu.make_async_copy(eg_hbm.at[0], eg, load_sem.at[8]),
        pltpu.make_async_copy(eu_hbm.at[0], eu, load_sem.at[9]),
        pltpu.make_async_copy(ed_hbm.at[0], ed, load_sem.at[10]),
    ]
    for load in loads:
        load.start()

    hid_g[t] = pack(hidden_ref[...])
    lane_row = lanes((8, 128))
    own_lengths = jnp.zeros((8, 128), jnp.int32)
    for g in range(GROUP_OWN):
        own_lengths = jnp.where(lane_row == g, glen_s[g], own_lengths)
    glr[o] = own_lengths

    pl.semaphore_wait(barrier, NT - 1 + NO - 1)

    def gather_start(name, buf, ss, rs):
        def copy(p, slot):
            return remote(buf.at[slot], buf.at[slot], ss.at[p], rs.at[slot], {"tensor": p})

        over(0, NT - 1, lambda n: copy(far_first(n), t).start())
        open_recv[name] = lambda: over(1, NT, lambda k: copy(tpeer(k), tpeer(k)).wait_recv())
        open_send[name] = lambda: over(1, NT, lambda k: copy(tpeer(k), t).wait_send())

    def spread_copy(src, dst, ss, rs, axis, peer, came_from):
        return remote(src.at[peer], dst.at[came_from], ss.at[peer], rs.at[came_from], {axis: peer})

    def spread_start(name, src, dst, ss, rs, axis):
        me, n, at = (t, NT, tpeer) if axis == "tensor" else (o, NO, opeer)
        order = far_first if axis == "tensor" else lambda k: opeer(k + 1)
        over(0, n - 1, lambda k: spread_copy(src, dst, ss, rs, axis, order(k), me).start())
        open_recv[name] = lambda: over(
            1, n, lambda k: spread_copy(src, dst, ss, rs, axis, at(k), at(k)).wait_recv()
        )
        open_send[name] = lambda: over(
            1, n, lambda k: spread_copy(src, dst, ss, rs, axis, at(k), me).wait_send()
        )

    def column_copy(buf, ss, rs, dz, slot):
        return remote(
            buf.at[slot], buf.at[slot], ss.at[dz], rs.at[slot], {"tensor": x * 8 + lax.rem(z + dz, 8)}
        )

    def row_copy(buf, ss, rs, zz, n, slot):
        dx = jnp.where(n == 0, 2, 2 * n - 1)
        return remote(
            buf.at[slot],
            buf.at[slot],
            ss.at[8 + 3 * zz + n],
            rs.at[slot],
            {"tensor": lax.rem(x + dx, 4) * 8 + z},
        )

    def relay_start(name, buf, ss, rs):
        over(0, 7, lambda k: column_copy(buf, ss, rs, near(6 - k), t).start())
        over(0, 3, lambda n: row_copy(buf, ss, rs, 0, n, t).start())
        open_recv[name] = lambda: relay_pass(name, buf, ss, rs, True)

    def near(k):
        return 4 + (1 - 2 * lax.rem(6 - k, 2)) * ((7 - k) // 2)

    def column_of(buf, ss, rs, xx):
        def wait(k):
            slot = xx * 8 + k
            column_copy(buf, ss, rs, 1, slot).wait_recv()

        over(0, 8, wait)

    def relay_pass(name, buf, ss, rs, rest):
        def pass_on(k):
            dz = near(k)
            slot = x * 8 + lax.rem(z + dz, 8)
            column_copy(buf, ss, rs, dz, slot).wait_recv()
            over(0, 3, lambda n: row_copy(buf, ss, rs, dz, n, slot).start())

        over(0, 7, pass_on)

        def sent():
            over(1, 8, lambda dz: column_copy(buf, ss, rs, dz, t).wait_send())
            over(
                0,
                24,
                lambda m: row_copy(
                    buf, ss, rs, m // 3, lax.rem(m, 3), x * 8 + lax.rem(z + m // 3, 8)
                ).wait_send(),
            )

        open_send[name] = sent

        def columns():
            over(1, 4, lambda dx: column_of(buf, ss, rs, lax.rem(x + dx, 4)))

        if rest:
            columns()
        else:
            open_recv[name] = columns

    def arrived(name):
        open_recv.pop(name)()

    gather_start("hidden", hid_g, hid_ss, hid_rs)

    up = opeer(2)
    down = opeer(6)
    far = opeer(4)
    mate = o + 1 - 2 * lax.rem(o, 2)

    def groups(owner, first=0, count=GROUP_OWN):
        return gc.at[pl.ds(GROUP_OWN * owner + first, count)]

    def cache_copy(src, dst, n, to):
        return pltpu.make_async_remote_copy(
            src_ref=src,
            dst_ref=dst,
            send_sem=gc_ss.at[n],
            recv_sem=gc_rs.at[n],
            device_id={"owner": to},
            device_id_type=MESH,
        )

    part_of = GROUP_OWN // 4

    def piece(owner, i):
        return groups(owner, part_of * i, part_of)

    mate_up = lax.rem(mate + 2, NO)
    mate_down = lax.rem(mate + 6, NO)
    mate_far = lax.rem(mate + 4, NO)

    def own_up(i):
        return cache_copy(gcache_hbm.at[pl.ds(part_of * i, part_of)], piece(o, i), i, up)

    def own_down(i):
        return cache_copy(gcache_hbm.at[pl.ds(part_of * i, part_of)], piece(o, i), 4 + i, down)

    def own_mate():
        return cache_copy(gcache_hbm, groups(o), 8, mate)

    for i in range(4):
        own_up(i).start()
        own_down(3 - i).start()
    own_mate().start()

    def to_mate(owner, i, n):
        return cache_copy(piece(owner, i), piece(owner, i), n + i, mate)

    def to_up(i):
        return cache_copy(piece(down, i), piece(down, i), 17 + i, up)

    def to_down(i):
        return cache_copy(piece(up, i), piece(up, i), 17 + i, down)

    def lengths_copy(p, slot):
        return remote(glr.at[slot], glr.at[slot], gl_ss.at[p], gl_rs.at[slot], {"owner": p})

    over(1, NO, lambda k: lengths_copy(opeer(k), o).start())
    open_recv["lengths"] = lambda: over(
        1, NO, lambda k: lengths_copy(opeer(k), opeer(k)).wait_recv()
    )
    open_send["lengths"] = lambda: over(1, NO, lambda k: lengths_copy(opeer(k), o).wait_send())

    def caches_sent():
        for i in range(4):
            own_up(i).wait_send()
            own_down(i).wait_send()
        own_mate().wait_send()
        for i in range(4):
            to_mate(down, i, 9).wait_send()
            to_mate(up, i, 13).wait_send()
            to_mate(far, i, 21).wait_send()
        for i in range(2):
            to_up(i).wait_send()
            to_down(2 + i).wait_send()

    def from_down(i):
        cache_copy(piece(down, i), piece(down, i), i, up).wait_recv()
        to_mate(down, i, 9).start()
        if i < 2:
            to_up(i).start()

    def from_up(i):
        cache_copy(piece(up, i), piece(up, i), 4 + i, down).wait_recv()
        to_mate(up, i, 13).start()
        if i >= 2:
            to_down(i).start()

    def from_far(i):
        cache_copy(piece(far, i), piece(far, i), 17 + i, up).wait_recv()
        to_mate(far, i, 21).start()

    def from_mate():
        cache_copy(groups(mate), groups(mate), 8, mate).wait_recv()
        for i in range(4):
            to_mate(mate_down, i, 9).wait_recv()
            to_mate(mate_up, i, 13).wait_recv()
            to_mate(mate_far, i, 21).wait_recv()

    cache_steps = [
        lambda: (from_down(0), from_up(3)),
        lambda: (from_down(1), from_up(2)),
        lambda: (from_down(2), from_up(1), from_down(3), from_up(0)),
        lambda: (from_far(0), from_far(3), from_far(1), from_far(2)),
        from_mate,
    ]

    def caches(n):
        for _ in range(n):
            cache_steps.pop(0)()

    open_recv["caches"] = lambda: caches(len(cache_steps))
    open_send["caches"] = caches_sent
    for n, load in enumerate(loads):
        open_recv[n] = load.wait


    row = rows((NO * SLOT, REQ))
    wanted = (row // SLOT) * 8 + t // 4
    hits = jnp.zeros((NO * SLOT, REQ), F32)
    share = jnp.zeros((NO * SLOT, REQ), F32)
    for k in range(6):
        match = routes_ref[k : k + 1, :] == wanted
        hits = jnp.where(match, 1.0, hits)
        share = jnp.where(match, rweight_ref[k : k + 1, :], share)
    before = (rows((REQ, REQ)) < lanes((REQ, REQ))).astype(BF16)
    rank = dot_n(hits.astype(BF16), before)
    picked = (hits > 0.5) & (rank == (row % SLOT).astype(F32))
    pick_t = jnp.where(picked, 1.0, 0.0).astype(BF16)
    share = jnp.transpose(jnp.where(picked, share, 0.0))

    r_iota = rows((REQ, 1))
    slen = jnp.zeros((REQ, 1), jnp.int32)
    gof = jnp.zeros((REQ, 1), jnp.int32)
    for r in range(REQ):
        slen = jnp.where(r_iota == r, slen_s[r], slen)
        gof = jnp.where(r_iota == r, gof_s[r], gof)
    arrived(0)
    arrived("hidden")
    caches(1)
    unpack_all(hid_g, wide)
    q_g[t] = dot_t(rms(wide, again_ref), wq[...]).astype(BF16)
    relay_start("queries", q_g, q_ss, q_rs)

    caches(1)
    open_recv.pop("queries")
    relay_pass("queries", q_g, q_ss, q_rs, False)
    arrived("lengths")
    lane128 = lanes((REQ, 128))
    glen_wide = jnp.zeros((REQ, 128), jnp.int32)
    for d in range(NO):
        mine = (gof - GROUP_OWN * d == lane128) & (lane128 < GROUP_OWN)
        glen_wide = jnp.where(mine, glr[d, 0:1, :], glen_wide)
    glen = jnp.sum(glen_wide, axis=1, keepdims=True)

    arrived(1)
    arrived(2)
    arrived(3)

    open_recv.pop("queries")
    n = 16 * HG
    for j in range(4):
        g = lax.rem(x + (0, 1, 3, 2)[j], 4)
        if j > 0:
            column_of(q_g, q_ss, q_rs, g)
        for h in range(HG):
            a = q_g[8 * g + 2 * h]
            b = q_g[8 * g + 2 * h + 1]
            q_all[g * HG + h, :, 0:256] = a[:, 0:256]
            q_all[g * HG + h, :, 256:384] = (
                a[:, 256:384].astype(F32) + b[:, 0:128].astype(F32)
            ).astype(BF16)
            q_all[g * HG + h, :, 384:576] = b[:, 128:320]
        if j == 0:
            caches(1)
        q = q_all[pl.ds(g * HG, HG)]
        all_out, all_mass = block_part(q.reshape(HG * REQ, KVW), None, None, root[...])
        all_out = all_out.reshape(HG, REQ, LAT)
        all_mass = all_mass.reshape(HG, REQ, 1)
        for c in range(2):
            r0 = 16 * c
            root_out = all_out[:, r0 : r0 + 16].reshape(n, LAT)
            root_mass = all_mass[:, r0 : r0 + 16].reshape(n, 1)
            s_col = lanes((n, 256))
            s_row = rows((n, 256)) % 16
            s_len = jnp.concatenate([slen[r0 : r0 + 16]] * HG, axis=0)
            s_ok = (s_col // 16 == s_row) & (t * 16 + s_col % 16 < s_len)
            sfx_out, sfx_mass = block_part(
                q[:, r0 : r0 + 16].reshape(n, KVW), sfx[r0 : r0 + 16].reshape(256, KVW), s_ok
            )
            out, mass = join((root_out, root_mass), (sfx_out, sfx_mass))
            rs_out[g, c] = out
            rs_mass[g, c] = mass
    caches(1)
    open_recv.pop("caches")
    caches(1)

    def fetch(r):
        gg[r] = gc[gof_s[r]]

    over(0, REQ, fetch)

    square = lanes((16, 128)) == rows((16, 128))
    for j in range(4):
        g = lax.rem(x + (2, 1, 3, 0)[j], 4)
        for c in range(2):
            r0 = 16 * c
            q = q_all[pl.ds(g * HG, HG), r0 : r0 + 16].reshape(n, KVW)
            g_col = lanes((n, 512))
            g_row = rows((n, 512)) % 16
            g_len = jnp.concatenate([glen[r0 : r0 + 16]] * HG, axis=0)
            g_ok = (g_col // 32 == g_row) & (t * 32 + g_col % 32 < g_len)
            grp_out, grp_mass = block_part(q, gg[r0 : r0 + 16].reshape(512, KVW), g_ok)
            grp_out = grp_out.astype(BF16).astype(F32)
            out, mass = join((rs_out[g, c], rs_mass[g, c]), (grp_out, grp_mass))
            out = out.astype(BF16)
            for h in range(HG):
                s = slice(16 * h, 16 * h + 16)
                po[8 * g + 2 * h + c] = out[s]
                pm[8 * g + 2 * h + c] = jnp.sum(
                    jnp.where(square, mass[s], 0.0), axis=0, keepdims=True
                )

        def part_start(k, g=g):
            p = 8 * g + k
            spread_copy(pm, pmr, pm_ss, pm_rs, "tensor", p, t).start()
            spread_copy(po, pr, p_ss, p_rs, "tensor", p, t).start()

        if j == 3:
            over(1, 8, lambda k, g=g: part_start(lax.rem(z + k, 8), g))
            pr[t] = po[t]
            pmr[t] = pm[t]
        else:
            over(0, 8, lambda k, g=g: part_start(lax.rem(z + k, 8), g))

    def partial_wait(k):
        p = tpeer(k)
        spread_copy(pm, pmr, pm_ss, pm_rs, "tensor", p, p).wait_recv()
        spread_copy(po, pr, p_ss, p_rs, "tensor", p, p).wait_recv()

    def partial_sent(k):
        p = tpeer(k)
        spread_copy(pm, pmr, pm_ss, pm_rs, "tensor", p, t).wait_send()
        spread_copy(po, pr, p_ss, p_rs, "tensor", p, t).wait_send()

    open_recv["partial"] = lambda: over(1, NT, partial_wait)
    open_send["partial"] = lambda: over(1, NT, partial_sent)
    arrived("partial")

    masses = jnp.sum(jnp.where(square[None], pmr[...], 0.0), axis=-1, keepdims=True)
    top = jnp.max(masses, axis=0, keepdims=True)
    w = jnp.exp(masses - top)
    acc = jnp.zeros((16, LAT), F32)
    for k in range(NT):
        acc = acc + w[k] * pr[k].astype(F32)
    att_g[t] = (acc / jnp.sum(w, axis=0)).astype(BF16)
    relay_start("attention", att_g, att_ss, att_rs)
    arrived(4)
    arrived("attention")

    proj = jnp.zeros((REQ, 64), F32)
    for h in range(H):
        a = att_g[2 * h : 2 * h + 2].reshape(REQ, LAT)
        proj = proj + dot_t(a, wo[:, LAT * h : LAT * h + LAT])
    mid = (hidden_ref[...].astype(F32) + proj).astype(BF16)
    mid_g[t] = pack(mid)
    gather_start("mid", mid_g, mid_ss, mid_rs)
    arrived("mid")
    unpack_all(mid_g, wide)
    mix = rms(wide, mgain_ref)

    sent = dot_n(pick_t, mix)
    for d in range(NO):
        s = sent[SLOT * d : SLOT * d + SLOT]
        dsp_s[d] = jnp.concatenate([s[:, :HALF], s[:, HALF:]], axis=0).astype(BF16)
    spread_start("dispatch", dsp_s, dsp_r, dsp_ss, dsp_rs, "owner")
    dsp_r[o] = dsp_s[o]

    for n in range(5, 11):
        arrived(n)
    act = (silu(dot_t(mix, sg[...])) * dot_t(mix, su[...])).astype(BF16)
    part[...] = dot_n(act, sd[...])

    def slots(buf):
        low = jnp.concatenate([buf[d].astype(F32)[:SLOT] for d in range(NO)], axis=0)
        high = jnp.concatenate([buf[d].astype(F32)[SLOT:] for d in range(NO)], axis=0)
        return jnp.concatenate([low, high], axis=1).astype(BF16)

    arrived("dispatch")
    taken = slots(dsp_r)
    act = (silu(dot_t(taken, eg[...])) * dot_t(taken, eu[...])).astype(BF16)
    res = dot_n(act, ed[...])
    for d in range(NO):
        s = res[SLOT * d : SLOT * d + SLOT]
        ret_s[d] = jnp.concatenate([s[:, :HALF], s[:, HALF:]], axis=0).astype(BF16)
    spread_start("return", ret_s, ret_r, ret_ss, ret_rs, "owner")
    ret_r[o] = ret_s[o]
    s0 = share.astype(BF16)
    s1 = (share - s0.astype(F32)).astype(BF16)
    s2 = (share - s0.astype(F32) - s1.astype(F32)).astype(BF16)
    arrived("return")
    y = slots(ret_r)
    part[...] += dot_n(s0, y) + dot_n(s1, y) + dot_n(s2, y)

    low = lanes((16, 128)) < 64
    for i in range(NT // 2):
        a = part[0:16, 128 * i : 128 * i + 128]
        b = part[16:32, 128 * i : 128 * i + 128]
        rs_s[2 * i] = jnp.where(low, a, pltpu.roll(b, 64, 1)).astype(BF16)
        rs_s[2 * i + 1] = jnp.where(low, pltpu.roll(a, 64, 1), b).astype(BF16)

    spread_start("result", rs_s, rs_r, rs_ss, rs_rs, "tensor")
    rs_r[t] = rs_s[t]
    arrived("result")
    total = jnp.zeros((16, 128), F32)
    for k in range(NT):
        total = total + rs_r[k].astype(F32)
    summed = jnp.concatenate([total, pltpu.roll(total, 64, 1)], axis=0)[:, :64]
    out_ref[...] = (mid.astype(F32) + summed).astype(BF16)

    for wait in open_send.values():
        wait()


def local(
    hidden,
    attention_gain,
    query_weight,
    out_weight,
    root_cache,
    group_cache,
    group_length,
    suffix_cache,
    suffix_length,
    group_of,
    mixture_gain,
    routes,
    route_weight,
    expert_gate,
    expert_up,
    expert_down,
    shared_gate,
    shared_up,
    shared_down,
):
    vmem = pl.BlockSpec(memory_space=pltpu.VMEM)
    smem = pl.BlockSpec(memory_space=pltpu.SMEM)
    hbm = pl.BlockSpec(memory_space=pl.ANY)
    dma = pltpu.SemaphoreType.DMA
    return pl.pallas_call(
        kernel,
        out_shape=jax.ShapeDtypeStruct((REQ, 64), BF16),
        in_specs=[
            vmem, vmem, hbm, hbm, hbm, hbm, smem, hbm, smem, smem, vmem, vmem, vmem,
            hbm, hbm, hbm, hbm, hbm, hbm,
        ],
        out_specs=vmem,
        scratch_shapes=[
            pltpu.VMEM((384, D), BF16),
            pltpu.VMEM((64, H * LAT), BF16),
            pltpu.VMEM((KVW, 1024), BF16),
            pltpu.VMEM((NO * GROUP_OWN, 32, KVW), BF16),
            pltpu.VMEM((REQ, 32, KVW), BF16),
            pltpu.VMEM((REQ, 16, KVW), BF16),
            pltpu.VMEM((352, D), BF16),
            pltpu.VMEM((352, D), BF16),
            pltpu.VMEM((352, D), BF16),
            pltpu.VMEM((88, D), BF16),
            pltpu.VMEM((88, D), BF16),
            pltpu.VMEM((88, D), BF16),
            pltpu.VMEM((NO, 8, 128), jnp.int32),
            pltpu.VMEM((NT, 16, 128), BF16),
            pltpu.VMEM((NT, REQ, 384), BF16),
            pltpu.VMEM((H, REQ, KVW), BF16),
            pltpu.VMEM((4, 2, 16 * HG, LAT), F32),
            pltpu.VMEM((4, 2, 16 * HG, 1), F32),
            pltpu.VMEM((NT, 16, LAT), BF16),
            pltpu.VMEM((NT, 16, LAT), BF16),
            pltpu.VMEM((NT, 1, 128), F32),
            pltpu.VMEM((NT, 1, 128), F32),
            pltpu.VMEM((NT, 16, LAT), BF16),
            pltpu.VMEM((NT, 16, 128), BF16),
            pltpu.VMEM((NO, 2 * SLOT, HALF), BF16),
            pltpu.VMEM((NO, 2 * SLOT, HALF), BF16),
            pltpu.VMEM((NO, 2 * SLOT, HALF), BF16),
            pltpu.VMEM((NO, 2 * SLOT, HALF), BF16),
            pltpu.VMEM((NT, 16, 128), BF16),
            pltpu.VMEM((NT, 16, 128), BF16),
            pltpu.VMEM((REQ, D), F32),
            pltpu.VMEM((REQ, D), F32),
            dma((11,)),
        ]
        + [dma((NT,))] * 14
        + [dma((NO,))] * 6
        + [dma((25,))] * 2,
        compiler_params=pltpu.CompilerParams(
            collective_id=0, has_side_effects=True, vmem_limit_bytes=60 * 1024 * 1024
        ),
        name="layer",
    )(
        hidden,
        attention_gain,
        query_weight,
        out_weight,
        root_cache.T,
        group_cache,
        group_length,
        suffix_cache,
        suffix_length,
        group_of,
        mixture_gain,
        routes.T,
        route_weight.T,
        expert_gate,
        expert_up,
        expert_down,
        shared_gate,
        shared_up,
        shared_down,
    )


def solution(mesh):
    return jax.shard_map(
        local,
        mesh=mesh,
        in_specs=(
            P("owner", "tensor"),
            P(),
            P("tensor", None),
            P("tensor", None),
            P("tensor", None),
            P("owner", "tensor", None),
            P("owner"),
            P("owner", "tensor", None),
            P("owner"),
            P("owner"),
            P(),
            P("owner", None),
            P("owner", None),
            P(("owner", "tensor"), None, None),
            P(("owner", "tensor"), None, None),
            P(("owner", "tensor"), None, None),
            P("tensor", None),
            P("tensor", None),
            P("tensor", None),
        ),
        out_specs=P("owner", "tensor"),
        check_vma=False,
    )
```

```python
import functools

import jax
import jax.numpy as jnp
from jax import lax
from jax.experimental import pallas as pl
from jax.experimental.pallas import tpu as pltpu
from jax.sharding import PartitionSpec as P

D = 2048
H = 16
LAT = 512
KVW = 576
GROUP_OWN = 12
REQ = 32
NT = 32
NO = 8
SLOT = 8
HALF = 1024
HG = 4
SCALE = 192.0 ** (-0.5)
LOWEST = -1e30
EPS = 1e-06
MESH = pl.DeviceIdType.MESH
F32 = jnp.float32
BF16 = jnp.bfloat16


def dot_t(a, b):
    return lax.dot_general(a, b, (((1,), (1,)), ((), ())), preferred_element_type=F32)


def dot_n(a, b):
    return lax.dot_general(a, b, (((1,), (0,)), ((), ())), preferred_element_type=F32)


def lanes(shape):
    return lax.broadcasted_iota(jnp.int32, shape, len(shape) - 1)


def rows(shape):
    return lax.broadcasted_iota(jnp.int32, shape, len(shape) - 2)


def pack(x):
    return jnp.concatenate([x[:16], x[16:]], axis=1)


def unpack_all(blocks_ref, wide_ref):
    low = lanes((16, 128)) < 64
    for i in range(NT // 2):
        a = blocks_ref[2 * i].astype(F32)
        b = blocks_ref[2 * i + 1].astype(F32)
        wide_ref[0:16, 128 * i : 128 * i + 128] = jnp.where(low, a, pltpu.roll(b, 64, 1))
        wide_ref[16:32, 128 * i : 128 * i + 128] = jnp.where(low, pltpu.roll(a, 64, 1), b)


def rms(wide_ref, gain_ref):
    x = wide_ref[...]
    scaled = x * lax.rsqrt(jnp.mean(x * x, axis=-1, keepdims=True) + EPS)
    return (scaled * gain_ref[...].astype(F32)[None, :]).astype(BF16)


def block_part(q, keys, usable, keys_t=None):
    scores = (dot_t(q, keys) if keys_t is None else dot_n(q, keys_t)) * SCALE
    if usable is not None:
        scores = jnp.where(usable, scores, LOWEST)
    peak = jnp.max(scores, axis=-1, keepdims=True)
    weights = jnp.exp(scores - peak)
    if usable is not None:
        weights = jnp.where(usable, weights, 0.0)
    total = jnp.sum(weights, axis=-1, keepdims=True)
    weights = weights.astype(BF16)
    numerator = dot_n(weights, keys[:, :LAT]) if keys_t is None else dot_t(weights, keys_t[:LAT])
    present = total > 0.0
    safe = jnp.where(present, total, 1.0)
    return numerator / safe, jnp.where(present, peak + jnp.log(safe), LOWEST)


def join(first, second):
    first_out, first_mass = first
    second_out, second_mass = second
    top = jnp.maximum(first_mass, second_mass)
    first_w = jnp.exp(first_mass - top)
    second_w = jnp.exp(second_mass - top)
    total = first_w + second_w
    return (first_w * first_out + second_w * second_out) / total, top + jnp.log(total)


def silu(v):
    return v / (1.0 + jnp.exp(-v))


def kernel(
    hidden_hbm,
    again_hbm,
    wq_hbm,
    wo_hbm,
    root_hbm,
    gcache_hbm,
    glen_hbm,
    sfx_hbm,
    slen_hbm,
    gof_hbm,
    mgain_hbm,
    routes_hbm,
    rweight_hbm,
    eg_hbm,
    eu_hbm,
    ed_hbm,
    sg_hbm,
    su_hbm,
    sd_hbm,
    out_ref,
    hidden_ref,
    again_ref,
    mgain_ref,
    routes_ref,
    rweight_ref,
    glen_s,
    slen_s,
    gof_s,
    wq,
    wo,
    root,
    gc,
    gg,
    sfx,
    eg,
    eu,
    ed,
    sg,
    su,
    sd,
    glr,
    hid_g,
    q_g,
    q_all,
    rs_out,
    rs_mass,
    po,
    pr,
    pm,
    pmr,
    po2,
    pz,
    pm2,
    pmz,
    att_g,
    mid_g,
    dsp_s,
    dsp_r,
    ret_s,
    ret_r,
    rs_s,
    rs_r,
    wide,
    part,
    load_sem,
    hid_ss,
    hid_rs,
    q_ss,
    q_rs,
    p_ss,
    p_rs,
    pm_ss,
    pm_rs,
    p2_ss,
    p2_rs,
    pm2_ss,
    pm2_rs,
    att_ss,
    att_rs,
    mid_ss,
    mid_rs,
    rs_ss,
    rs_rs,
    dsp_ss,
    dsp_rs,
    ret_ss,
    ret_rs,
    gl_ss,
    gl_rs,
    gc_ss,
    gc_rs,
):
    o = lax.axis_index("owner")
    t = lax.axis_index("tensor")

    def tpeer(k):
        return lax.rem(t + k, NT)

    def opeer(k):
        return lax.rem(o + k, NO)

    x = t // 8
    z = lax.rem(t, 8)
    open_recv = {}
    open_send = {}

    def remote(src, dst, ss, rs, to):
        return pltpu.make_async_remote_copy(
            src_ref=src, dst_ref=dst, send_sem=ss, recv_sem=rs, device_id=to, device_id_type=MESH
        )

    def over(first, last, step):
        def body(k, carry):
            step(k)
            return carry

        lax.fori_loop(first, last, body, 0)

    def far_first(n):
        kz = n // 4
        kx = lax.rem(n, 4)
        dz = 4 + (1 - 2 * lax.rem(kz, 2)) * ((kz + 1) // 2)
        dx = 2 + (1 - 2 * lax.rem(kx, 2)) * ((kx + 1) // 2)
        return lax.rem(x + dx, 4) * 8 + lax.rem(z + dz, 8)

    barrier = pltpu.get_barrier_semaphore()

    def greet(to):
        pl.semaphore_signal(barrier, inc=1, device_id=to, device_id_type=MESH)

    over(0, NT - 1, lambda n: greet({"tensor": far_first(n)}))
    over(1, NO, lambda k: greet({"owner": opeer(k)}))

    small = [
        pltpu.make_async_copy(src, dst, load_sem.at[11 + n])
        for n, (src, dst) in enumerate(
            [
                (hidden_hbm, hidden_ref),
                (glen_hbm, glen_s),
                (slen_hbm, slen_s),
                (gof_hbm, gof_s),
                (routes_hbm, routes_ref),
                (rweight_hbm, rweight_ref),
                (again_hbm, again_ref),
                (mgain_hbm, mgain_ref),
            ]
        )
    ]
    for load in small:
        load.start()

    wq[0:32, :] = jnp.zeros((32, D), BF16)
    wq[288:384, :] = jnp.zeros((96, D), BF16)
    shift = pl.multiple_of(lax.rem(t, 2) * 32, 32)
    loads = [
        pltpu.make_async_copy(wq_hbm, wq.at[pl.ds(shift, 288)], load_sem.at[0]),
        pltpu.make_async_copy(root_hbm, root, load_sem.at[1]),
        pltpu.make_async_copy(sfx_hbm, sfx, load_sem.at[2]),
        pltpu.make_async_copy(
            gcache_hbm, gc.at[pl.ds(GROUP_OWN * o, GROUP_OWN)], load_sem.at[3]
        ),
        pltpu.make_async_copy(wo_hbm, wo, load_sem.at[4]),
        pltpu.make_async_copy(sg_hbm, sg, load_sem.at[5]),
        pltpu.make_async_copy(su_hbm, su, load_sem.at[6]),
        pltpu.make_async_copy(sd_hbm, sd, load_sem.at[7]),
        pltpu.make_async_copy(eg_hbm.at[0], eg, load_sem.at[8]),
        pltpu.make_async_copy(eu_hbm.at[0], eu, load_sem.at[9]),
        pltpu.make_async_copy(ed_hbm.at[0], ed, load_sem.at[10]),
    ]
    for load in loads:
        load.start()
    for load in small:
        load.wait()

    hid_g[t] = pack(hidden_ref[...])
    lane_row = lanes((8, 128))
    own_lengths = jnp.zeros((8, 128), jnp.int32)
    for g in range(GROUP_OWN):
        own_lengths = jnp.where(lane_row == g, glen_s[g], own_lengths)
    glr[o] = own_lengths

    pl.semaphore_wait(barrier, NT - 1 + NO - 1)

    def gather_start(name, buf, ss, rs):
        def copy(p, slot):
            return remote(buf.at[slot], buf.at[slot], ss.at[p], rs.at[slot], {"tensor": p})

        over(0, NT - 1, lambda n: copy(far_first(n), t).start())
        open_recv[name] = lambda: over(1, NT, lambda k: copy(tpeer(k), tpeer(k)).wait_recv())
        open_send[name] = lambda: over(1, NT, lambda k: copy(tpeer(k), t).wait_send())

    def spread_copy(src, dst, ss, rs, axis, peer, came_from):
        return remote(src.at[peer], dst.at[came_from], ss.at[peer], rs.at[came_from], {axis: peer})

    def spread_start(name, src, dst, ss, rs, axis):
        me, n, at = (t, NT, tpeer) if axis == "tensor" else (o, NO, opeer)
        order = far_first if axis == "tensor" else lambda k: opeer(k + 1)
        over(0, n - 1, lambda k: spread_copy(src, dst, ss, rs, axis, order(k), me).start())
        open_recv[name] = lambda: over(
            1, n, lambda k: spread_copy(src, dst, ss, rs, axis, at(k), at(k)).wait_recv()
        )
        open_send[name] = lambda: over(
            1, n, lambda k: spread_copy(src, dst, ss, rs, axis, at(k), me).wait_send()
        )

    def column_copy(buf, ss, rs, dz, slot):
        return remote(
            buf.at[slot], buf.at[slot], ss.at[dz], rs.at[slot], {"tensor": x * 8 + lax.rem(z + dz, 8)}
        )

    def row_copy(buf, ss, rs, zz, n, slot):
        dx = jnp.where(n == 0, 2, 2 * n - 1)
        return remote(
            buf.at[slot],
            buf.at[slot],
            ss.at[8 + 3 * zz + n],
            rs.at[slot],
            {"tensor": lax.rem(x + dx, 4) * 8 + z},
        )

    def relay_start(name, buf, ss, rs):
        over(0, 3, lambda n: row_copy(buf, ss, rs, 0, n, t).start())
        over(0, 7, lambda k: column_copy(buf, ss, rs, near(k), t).start())
        open_recv[name] = lambda: relay_pass(name, buf, ss, rs, True)

    def near(k):
        return 4 + (1 - 2 * lax.rem(6 - k, 2)) * ((7 - k) // 2)

    def column_of(buf, ss, rs, xx):
        def wait(k):
            slot = xx * 8 + k
            column_copy(buf, ss, rs, 1, slot).wait_recv()

        over(0, 8, wait)

    def relay_pass(name, buf, ss, rs, rest):
        def pass_on(k):
            dz = near(k)
            slot = x * 8 + lax.rem(z + dz, 8)
            column_copy(buf, ss, rs, dz, slot).wait_recv()
            over(0, 3, lambda n: row_copy(buf, ss, rs, dz, n, slot).start())

        over(0, 7, pass_on)

        def sent():
            over(1, 8, lambda dz: column_copy(buf, ss, rs, dz, t).wait_send())
            over(
                0,
                24,
                lambda m: row_copy(
                    buf, ss, rs, m // 3, lax.rem(m, 3), x * 8 + lax.rem(z + m // 3, 8)
                ).wait_send(),
            )

        open_send[name] = sent

        def columns():
            over(1, 4, lambda dx: column_of(buf, ss, rs, lax.rem(x + dx, 4)))

        if rest:
            columns()
        else:
            open_recv[name] = columns

    def arrived(name):
        open_recv.pop(name)()

    gather_start("hidden", hid_g, hid_ss, hid_rs)

    up = opeer(2)
    down = opeer(6)
    far = opeer(4)
    mate = o + 1 - 2 * lax.rem(o, 2)

    def groups(owner, first=0, count=GROUP_OWN):
        return gc.at[pl.ds(GROUP_OWN * owner + first, count)]

    def cache_copy(src, dst, n, to):
        return pltpu.make_async_remote_copy(
            src_ref=src,
            dst_ref=dst,
            send_sem=gc_ss.at[n],
            recv_sem=gc_rs.at[n],
            device_id={"owner": to},
            device_id_type=MESH,
        )

    part_of = GROUP_OWN // 4

    def piece(owner, i):
        return groups(owner, part_of * i, part_of)

    mate_up = lax.rem(mate + 2, NO)
    mate_down = lax.rem(mate + 6, NO)
    mate_far = lax.rem(mate + 4, NO)

    def own_up(i):
        return cache_copy(gcache_hbm.at[pl.ds(part_of * i, part_of)], piece(o, i), i, up)

    def own_down(i):
        return cache_copy(gcache_hbm.at[pl.ds(part_of * i, part_of)], piece(o, i), 4 + i, down)

    def own_mate():
        return cache_copy(gcache_hbm, groups(o), 8, mate)

    for i in range(4):
        own_up(i).start()
        own_down(3 - i).start()
    own_mate().start()

    def to_mate(owner, i, n):
        return cache_copy(piece(owner, i), piece(owner, i), n + i, mate)

    def to_up(i):
        return cache_copy(piece(down, i), piece(down, i), 17 + i, up)

    def to_down(i):
        return cache_copy(piece(up, i), piece(up, i), 17 + i, down)

    def lengths_copy(p, slot):
        return remote(glr.at[slot], glr.at[slot], gl_ss.at[p], gl_rs.at[slot], {"owner": p})

    over(1, NO, lambda k: lengths_copy(opeer(k), o).start())
    open_recv["lengths"] = lambda: over(
        1, NO, lambda k: lengths_copy(opeer(k), opeer(k)).wait_recv()
    )
    open_send["lengths"] = lambda: over(1, NO, lambda k: lengths_copy(opeer(k), o).wait_send())

    def caches_sent():
        for i in range(4):
            own_up(i).wait_send()
            own_down(i).wait_send()
        own_mate().wait_send()
        for i in range(4):
            to_mate(down, i, 9).wait_send()
            to_mate(up, i, 13).wait_send()
            to_mate(far, i, 21).wait_send()
        for i in range(2):
            to_up(i).wait_send()
            to_down(2 + i).wait_send()

    def from_down(i):
        cache_copy(piece(down, i), piece(down, i), i, up).wait_recv()
        to_mate(down, i, 9).start()
        if i < 2:
            to_up(i).start()

    def from_up(i):
        cache_copy(piece(up, i), piece(up, i), 4 + i, down).wait_recv()
        to_mate(up, i, 13).start()
        if i >= 2:
            to_down(i).start()

    def from_far(i):
        cache_copy(piece(far, i), piece(far, i), 17 + i, up).wait_recv()
        to_mate(far, i, 21).start()

    def from_mate():
        cache_copy(groups(mate), groups(mate), 8, mate).wait_recv()
        for i in range(4):
            to_mate(mate_down, i, 9).wait_recv()
            to_mate(mate_up, i, 13).wait_recv()
            to_mate(mate_far, i, 21).wait_recv()

    cache_steps = [
        lambda: (from_down(0), from_up(3)),
        lambda: (from_down(1), from_up(2)),
        lambda: (from_down(2), from_up(1), from_down(3), from_up(0)),
        lambda: (from_far(0), from_far(3), from_far(1), from_far(2)),
        from_mate,
    ]

    def caches(n):
        for _ in range(n):
            cache_steps.pop(0)()

    open_recv["caches"] = lambda: caches(len(cache_steps))
    open_send["caches"] = caches_sent
    for n, load in enumerate(loads):
        open_recv[n] = load.wait


    row = rows((NO * SLOT, REQ))
    wanted = (row // SLOT) * 8 + t // 4
    hits = jnp.zeros((NO * SLOT, REQ), F32)
    share = jnp.zeros((NO * SLOT, REQ), F32)
    for k in range(6):
        match = routes_ref[k : k + 1, :] == wanted
        hits = jnp.where(match, 1.0, hits)
        share = jnp.where(match, rweight_ref[k : k + 1, :], share)
    before = (rows((REQ, REQ)) < lanes((REQ, REQ))).astype(BF16)
    rank = dot_n(hits.astype(BF16), before)
    picked = (hits > 0.5) & (rank == (row % SLOT).astype(F32))
    pick_t = jnp.where(picked, 1.0, 0.0).astype(BF16)
    share = jnp.transpose(jnp.where(picked, share, 0.0))

    r_iota = rows((REQ, 1))
    slen = jnp.zeros((REQ, 1), jnp.int32)
    gof = jnp.zeros((REQ, 1), jnp.int32)
    for r in range(REQ):
        slen = jnp.where(r_iota == r, slen_s[r], slen)
        gof = jnp.where(r_iota == r, gof_s[r], gof)
    arrived(0)
    arrived("hidden")
    caches(1)
    unpack_all(hid_g, wide)
    proj = dot_t(rms(wide, again_ref), wq[...])
    low32 = lanes((16, 128)) < 32
    odd = lax.rem(t, 2) == 1
    first = [proj[0:16, 128 * i : 128 * i + 128] for i in range(3)]
    last = [proj[16:32, 128 * i : 128 * i + 128] for i in range(3)]
    inner = jnp.logical_and(low32, odd)
    q_g[t] = jnp.concatenate(
        [
            jnp.where(inner, first[2], first[0]),
            first[1],
            jnp.where(inner, last[2], last[0]),
            last[1],
            jnp.where(inner, 0.0, first[2]) + pltpu.roll(jnp.where(inner, 0.0, last[2]), 64, 1),
        ],
        axis=1,
    ).astype(BF16)
    relay_start("queries", q_g, q_ss, q_rs)

    caches(1)
    open_recv.pop("queries")
    relay_pass("queries", q_g, q_ss, q_rs, False)
    arrived("lengths")
    lane128 = lanes((REQ, 128))
    glen_wide = jnp.zeros((REQ, 128), jnp.int32)
    for d in range(NO):
        mine = (gof - GROUP_OWN * d == lane128) & (lane128 < GROUP_OWN)
        glen_wide = jnp.where(mine, glr[d, 0:1, :], glen_wide)
    glen = jnp.sum(glen_wide, axis=1, keepdims=True)

    arrived(1)
    arrived(2)
    arrived(3)

    open_recv.pop("queries")
    n = 16 * HG
    for j in range(4):
        g = lax.rem(x + (0, 1, 3, 2)[j], 4)
        if j > 0:
            column_of(q_g, q_ss, q_rs, g)
        for h in range(HG):
            a = q_g[8 * g + 2 * h]
            b = q_g[8 * g + 2 * h + 1]
            hh = g * HG + h
            a4 = a[:, 512:640].astype(F32)
            b4 = b[:, 512:640].astype(F32)
            for r0, a_cols, a_tail, b_tail in (
                (0, 0, a4, b4),
                (16, 256, pltpu.roll(a4, 64, 1), pltpu.roll(b4, 64, 1)),
            ):
                b_head = b[:, a_cols : a_cols + 128].astype(F32)
                q_all[hh, r0 : r0 + 16, 0:256] = a[:, a_cols : a_cols + 256]
                q_all[hh, r0 : r0 + 16, 256:384] = jnp.where(low32, a_tail, b_head).astype(BF16)
                q_all[hh, r0 : r0 + 16, 384:512] = b[:, a_cols + 128 : a_cols + 256]
                q_all[hh, r0 : r0 + 16, 512:576] = jnp.where(low32, b_head, b_tail)[:, :64].astype(
                    BF16
                )
        if j == 0:
            caches(1)
        q = q_all[pl.ds(g * HG, HG)]
        all_out, all_mass = block_part(q.reshape(HG * REQ, KVW), None, None, root[...])
        all_out = all_out.reshape(HG, REQ, LAT)
        all_mass = all_mass.reshape(HG, REQ, 1)
        for c in range(2):
            r0 = 16 * c
            root_out = all_out[:, r0 : r0 + 16].reshape(n, LAT)
            root_mass = all_mass[:, r0 : r0 + 16].reshape(n, 1)
            s_col = lanes((n, 256))
            s_row = rows((n, 256)) % 16
            s_len = jnp.concatenate([slen[r0 : r0 + 16]] * HG, axis=0)
            s_ok = (s_col // 16 == s_row) & (t * 16 + s_col % 16 < s_len)
            sfx_out, sfx_mass = block_part(
                q[:, r0 : r0 + 16].reshape(n, KVW), sfx[r0 : r0 + 16].reshape(256, KVW), s_ok
            )
            out, mass = join((root_out, root_mass), (sfx_out, sfx_mass))
            rs_out[g, c] = out
            rs_mass[g, c] = mass
    caches(1)
    open_recv.pop("caches")
    caches(1)

    def fetch(r):
        gg[r] = gc[gof_s[r]]

    over(0, REQ, fetch)

    square = lanes((16, 128)) == rows((16, 128))

    def z_far(k):
        return lax.rem(z + 4 + (1 - 2 * lax.rem(k, 2)) * ((k + 1) // 2), 8)

    def po_copy(p, g):
        return remote(
            po.at[p], pr.at[x * 8 + p - 8 * g], p_ss.at[p], p_rs.at[x * 8 + p - 8 * g], {"tensor": g * 8 + z}
        )

    def pm_copy(g):
        return remote(
            pm.at[pl.ds(8 * g, 8)], pmr.at[pl.ds(8 * x, 8)], pm_ss.at[g], pm_rs.at[x], {"tensor": g * 8 + z}
        )

    def po_wait(slot):
        remote(pr.at[slot], pr.at[slot], p_ss.at[slot], p_rs.at[slot], {"tensor": tpeer(1)}).wait_recv()

    def pm_wait(xx):
        block = pmr.at[pl.ds(8 * xx, 8)]
        remote(block, block, pm_ss.at[xx], pm_rs.at[xx], {"tensor": tpeer(1)}).wait_recv()

    for j in range(4):
        g = lax.rem(x + (2, 1, 3, 0)[j], 4)
        for c in range(2):
            r0 = 16 * c
            q = q_all[pl.ds(g * HG, HG), r0 : r0 + 16].reshape(n, KVW)
            g_col = lanes((n, 512))
            g_row = rows((n, 512)) % 16
            g_len = jnp.concatenate([glen[r0 : r0 + 16]] * HG, axis=0)
            g_ok = (g_col // 32 == g_row) & (t * 32 + g_col % 32 < g_len)
            grp_out, grp_mass = block_part(q, gg[r0 : r0 + 16].reshape(512, KVW), g_ok)
            grp_out = grp_out.astype(BF16).astype(F32)
            out, mass = join((rs_out[g, c], rs_mass[g, c]), (grp_out, grp_mass))
            out = out.astype(BF16)
            for h in range(HG):
                s = slice(16 * h, 16 * h + 16)
                po[8 * g + 2 * h + c] = out[s]
                pm[8 * g + 2 * h + c] = jnp.sum(
                    jnp.where(square, mass[s], 0.0), axis=0, keepdims=True
                )

        if j < 3:
            pm_copy(g).start()
            over(0, 8, lambda k, g=g: po_copy(8 * g + z_far(k), g).start())

    over(1, 4, lambda k: pm_wait(lax.rem(x + k, 4)))

    def combine(outs, mass_rows):
        mass = [jnp.sum(jnp.where(square, m, 0.0), axis=1, keepdims=True) for m in mass_rows]
        top = functools.reduce(jnp.maximum, mass)
        w = [jnp.exp(m - top) for m in mass]
        total = functools.reduce(jnp.add, w)
        acc = functools.reduce(jnp.add, [v * out.astype(F32) for v, out in zip(w, outs)])
        return (acc / total).astype(BF16), top + jnp.log(total)

    def join_row(k):
        zz = z_far(k)

        def wait(i):
            po_wait(lax.rem(x + i, 4) * 8 + zz)

        over(1, 4, wait)
        others = [lax.rem(x + i, 4) * 8 + zz for i in range(1, 4)]
        out, mass = combine(
            [po[x * 8 + zz]] + [pr[i] for i in others], [pm[x * 8 + zz]] + [pmr[i] for i in others]
        )
        po2[zz] = out
        pm2[zz] = jnp.sum(jnp.where(square, mass, 0.0), axis=0, keepdims=True)

    def to_column(src, dst, ss, rs, zz, slot):
        return remote(src.at[zz], dst.at[slot], ss.at[zz], rs.at[slot], {"tensor": x * 8 + zz})

    def join_and_send(k):
        join_row(k)
        zz = z_far(k)
        to_column(pm2, pmz, pm2_ss, pm2_rs, zz, z).start()
        to_column(po2, pz, p2_ss, p2_rs, zz, z).start()

    over(0, 7, join_and_send)
    join_row(7)
    pz[z] = po2[z]
    pmz[z] = pm2[z]

    def column_wait(k):
        zz = lax.rem(z + k, 8)
        to_column(pm2, pmz, pm2_ss, pm2_rs, zz, zz).wait_recv()
        to_column(po2, pz, p2_ss, p2_rs, zz, zz).wait_recv()

    def partial_sent():
        def row_sent(k):
            g = lax.rem(x + k, 4)
            pm_copy(g).wait_send()
            over(0, 8, lambda i: po_copy(8 * g + i, g).wait_send())

        over(1, 4, row_sent)

        def column_sent(k):
            zz = lax.rem(z + k, 8)
            to_column(pm2, pmz, pm2_ss, pm2_rs, zz, z).wait_send()
            to_column(po2, pz, p2_ss, p2_rs, zz, z).wait_send()

        over(1, 8, column_sent)

    open_send["partial"] = partial_sent
    over(1, 8, column_wait)
    att, _ = combine([pz[k] for k in range(8)], [pmz[k] for k in range(8)])
    att_g[t] = att
    relay_start("attention", att_g, att_ss, att_rs)
    arrived(4)
    arrived("attention")

    proj = jnp.zeros((REQ, 64), F32)
    for h in range(H):
        a = att_g[2 * h : 2 * h + 2].reshape(REQ, LAT)
        proj = proj + dot_t(a, wo[:, LAT * h : LAT * h + LAT])
    mid = (hidden_ref[...].astype(F32) + proj).astype(BF16)
    mid_g[t] = pack(mid)
    gather_start("mid", mid_g, mid_ss, mid_rs)
    arrived("mid")
    unpack_all(mid_g, wide)
    mix = rms(wide, mgain_ref)

    sent = dot_n(pick_t, mix)
    for d in range(NO):
        s = sent[SLOT * d : SLOT * d + SLOT]
        dsp_s[d] = jnp.concatenate([s[:, :HALF], s[:, HALF:]], axis=0).astype(BF16)
    spread_start("dispatch", dsp_s, dsp_r, dsp_ss, dsp_rs, "owner")
    dsp_r[o] = dsp_s[o]

    for n in range(5, 11):
        arrived(n)
    act = (silu(dot_t(mix, sg[...])) * dot_t(mix, su[...])).astype(BF16)
    part[...] = dot_n(act, sd[...])

    def slots(buf):
        low = jnp.concatenate([buf[d].astype(F32)[:SLOT] for d in range(NO)], axis=0)
        high = jnp.concatenate([buf[d].astype(F32)[SLOT:] for d in range(NO)], axis=0)
        return jnp.concatenate([low, high], axis=1).astype(BF16)

    arrived("dispatch")
    taken = slots(dsp_r)
    act = (silu(dot_t(taken, eg[...])) * dot_t(taken, eu[...])).astype(BF16)
    res = dot_n(act, ed[...])
    for d in range(NO):
        s = res[SLOT * d : SLOT * d + SLOT]
        ret_s[d] = jnp.concatenate([s[:, :HALF], s[:, HALF:]], axis=0).astype(BF16)
    spread_start("return", ret_s, ret_r, ret_ss, ret_rs, "owner")
    ret_r[o] = ret_s[o]
    s0 = share.astype(BF16)
    s1 = (share - s0.astype(F32)).astype(BF16)
    s2 = (share - s0.astype(F32) - s1.astype(F32)).astype(BF16)
    arrived("return")
    y = slots(ret_r)
    part[...] += dot_n(s0, y) + dot_n(s1, y) + dot_n(s2, y)

    low = lanes((16, 128)) < 64
    for i in range(NT // 2):
        a = part[0:16, 128 * i : 128 * i + 128]
        b = part[16:32, 128 * i : 128 * i + 128]
        rs_s[2 * i] = jnp.where(low, a, pltpu.roll(b, 64, 1)).astype(BF16)
        rs_s[2 * i + 1] = jnp.where(low, pltpu.roll(a, 64, 1), b).astype(BF16)

    spread_start("result", rs_s, rs_r, rs_ss, rs_rs, "tensor")
    rs_r[t] = rs_s[t]
    arrived("result")
    total = jnp.zeros((16, 128), F32)
    for k in range(NT):
        total = total + rs_r[k].astype(F32)
    summed = jnp.concatenate([total, pltpu.roll(total, 64, 1)], axis=0)[:, :64]
    out_ref[...] = (mid.astype(F32) + summed).astype(BF16)

    for wait in open_send.values():
        wait()


def local(
    hidden,
    attention_gain,
    query_weight,
    out_weight,
    root_cache,
    group_cache,
    group_length,
    suffix_cache,
    suffix_length,
    group_of,
    mixture_gain,
    routes,
    route_weight,
    expert_gate,
    expert_up,
    expert_down,
    shared_gate,
    shared_up,
    shared_down,
):
    vmem = pl.BlockSpec(memory_space=pltpu.VMEM)
    hbm = pl.BlockSpec(memory_space=pl.ANY)
    dma = pltpu.SemaphoreType.DMA
    return pl.pallas_call(
        kernel,
        out_shape=jax.ShapeDtypeStruct((REQ, 64), BF16),
        in_specs=[hbm] * 19,
        out_specs=vmem,
        scratch_shapes=[
            pltpu.VMEM((REQ, 64), BF16),
            pltpu.VMEM((D,), BF16),
            pltpu.VMEM((D,), BF16),
            pltpu.VMEM((6, REQ), jnp.int32),
            pltpu.VMEM((6, REQ), F32),
            pltpu.SMEM((GROUP_OWN,), jnp.int32),
            pltpu.SMEM((REQ,), jnp.int32),
            pltpu.SMEM((REQ,), jnp.int32),
            pltpu.VMEM((384, D), BF16),
            pltpu.VMEM((64, H * LAT), BF16),
            pltpu.VMEM((KVW, 1024), BF16),
            pltpu.VMEM((NO * GROUP_OWN, 32, KVW), BF16),
            pltpu.VMEM((REQ, 32, KVW), BF16),
            pltpu.VMEM((REQ, 16, KVW), BF16),
            pltpu.VMEM((352, D), BF16),
            pltpu.VMEM((352, D), BF16),
            pltpu.VMEM((352, D), BF16),
            pltpu.VMEM((88, D), BF16),
            pltpu.VMEM((88, D), BF16),
            pltpu.VMEM((88, D), BF16),
            pltpu.VMEM((NO, 8, 128), jnp.int32),
            pltpu.VMEM((NT, 16, 128), BF16),
            pltpu.VMEM((NT, 16, 640), BF16),
            pltpu.VMEM((H, REQ, KVW), BF16),
            pltpu.VMEM((4, 2, 16 * HG, LAT), F32),
            pltpu.VMEM((4, 2, 16 * HG, 1), F32),
            pltpu.VMEM((NT, 16, LAT), BF16),
            pltpu.VMEM((NT, 16, LAT), BF16),
            pltpu.VMEM((NT, 1, 128), F32),
            pltpu.VMEM((NT, 1, 128), F32),
            pltpu.VMEM((8, 16, LAT), BF16),
            pltpu.VMEM((8, 16, LAT), BF16),
            pltpu.VMEM((8, 1, 128), F32),
            pltpu.VMEM((8, 1, 128), F32),
            pltpu.VMEM((NT, 16, LAT), BF16),
            pltpu.VMEM((NT, 16, 128), BF16),
            pltpu.VMEM((NO, 2 * SLOT, HALF), BF16),
            pltpu.VMEM((NO, 2 * SLOT, HALF), BF16),
            pltpu.VMEM((NO, 2 * SLOT, HALF), BF16),
            pltpu.VMEM((NO, 2 * SLOT, HALF), BF16),
            pltpu.VMEM((NT, 16, 128), BF16),
            pltpu.VMEM((NT, 16, 128), BF16),
            pltpu.VMEM((REQ, D), F32),
            pltpu.VMEM((REQ, D), F32),
            dma((19,)),
        ]
        + [dma((NT,))] * 6
        + [dma((4,))] * 2
        + [dma((8,))] * 4
        + [dma((NT,))] * 6
        + [dma((NO,))] * 6
        + [dma((25,))] * 2,
        compiler_params=pltpu.CompilerParams(
            collective_id=0, has_side_effects=True, vmem_limit_bytes=60 * 1024 * 1024
        ),
        name="layer",
    )(
        hidden,
        attention_gain,
        query_weight,
        out_weight,
        root_cache.T,
        group_cache,
        group_length,
        suffix_cache,
        suffix_length,
        group_of,
        mixture_gain,
        routes.T,
        route_weight.T,
        expert_gate,
        expert_up,
        expert_down,
        shared_gate,
        shared_up,
        shared_down,
    )


def solution(mesh):
    return jax.shard_map(
        local,
        mesh=mesh,
        in_specs=(
            P("owner", "tensor"),
            P(),
            P("tensor", None),
            P("tensor", None),
            P("tensor", None),
            P("owner", "tensor", None),
            P("owner"),
            P("owner", "tensor", None),
            P("owner"),
            P("owner"),
            P(),
            P("owner", None),
            P("owner", None),
            P(("owner", "tensor"), None, None),
            P(("owner", "tensor"), None, None),
            P(("owner", "tensor"), None, None),
            P("tensor", None),
            P("tensor", None),
            P("tensor", None),
        ),
        out_specs=P("owner", "tensor"),
        check_vma=False,
    )
```

```python
import functools

import jax
import jax.numpy as jnp
from jax import lax
from jax.experimental import pallas as pl
from jax.experimental.pallas import tpu as pltpu
from jax.sharding import PartitionSpec as P

D = 2048
H = 16
LAT = 512
KVW = 576
GROUP_OWN = 12
REQ = 32
NT = 32
NO = 8
SLOT = 8
HALF = 1024
HG = 4
SCALE = 192.0 ** (-0.5)
LOWEST = -1e30
EPS = 1e-06
MESH = pl.DeviceIdType.MESH
F32 = jnp.float32
BF16 = jnp.bfloat16


def dot_t(a, b):
    return lax.dot_general(a, b, (((1,), (1,)), ((), ())), preferred_element_type=F32)


def dot_n(a, b):
    return lax.dot_general(a, b, (((1,), (0,)), ((), ())), preferred_element_type=F32)


def lanes(shape):
    return lax.broadcasted_iota(jnp.int32, shape, len(shape) - 1)


def rows(shape):
    return lax.broadcasted_iota(jnp.int32, shape, len(shape) - 2)


def pack(x):
    return jnp.concatenate([x[:16], x[16:]], axis=1)


def unpack_all(blocks_ref, wide_ref):
    low = lanes((16, 128)) < 64
    for i in range(NT // 2):
        a = blocks_ref[2 * i].astype(F32)
        b = blocks_ref[2 * i + 1].astype(F32)
        wide_ref[0:16, 128 * i : 128 * i + 128] = jnp.where(low, a, pltpu.roll(b, 64, 1))
        wide_ref[16:32, 128 * i : 128 * i + 128] = jnp.where(low, pltpu.roll(a, 64, 1), b)


def rms(wide_ref, gain_ref):
    x = wide_ref[...]
    scaled = x * lax.rsqrt(jnp.mean(x * x, axis=-1, keepdims=True) + EPS)
    return (scaled * gain_ref[...].astype(F32)[None, :]).astype(BF16)


def block_part(q, keys, usable, keys_t=None):
    scores = (dot_t(q, keys) if keys_t is None else dot_n(q, keys_t)) * SCALE
    if usable is not None:
        scores = jnp.where(usable, scores, LOWEST)
    peak = jnp.max(scores, axis=-1, keepdims=True)
    weights = jnp.exp(scores - peak)
    if usable is not None:
        weights = jnp.where(usable, weights, 0.0)
    total = jnp.sum(weights, axis=-1, keepdims=True)
    weights = weights.astype(BF16)
    numerator = dot_n(weights, keys[:, :LAT]) if keys_t is None else dot_t(weights, keys_t[:LAT])
    present = total > 0.0
    safe = jnp.where(present, total, 1.0)
    return numerator / safe, jnp.where(present, peak + jnp.log(safe), LOWEST)


def join(first, second):
    first_out, first_mass = first
    second_out, second_mass = second
    top = jnp.maximum(first_mass, second_mass)
    first_w = jnp.exp(first_mass - top)
    second_w = jnp.exp(second_mass - top)
    total = first_w + second_w
    return (first_w * first_out + second_w * second_out) / total, top + jnp.log(total)


def silu(v):
    return v / (1.0 + jnp.exp(-v))


def kernel(
    hidden_hbm,
    again_hbm,
    wq_hbm,
    wo_hbm,
    root_hbm,
    gcache_hbm,
    glen_hbm,
    sfx_hbm,
    slen_hbm,
    gof_hbm,
    mgain_hbm,
    routes_hbm,
    rweight_hbm,
    eg_hbm,
    eu_hbm,
    ed_hbm,
    sg_hbm,
    su_hbm,
    sd_hbm,
    out_ref,
    hidden_ref,
    again_ref,
    mgain_ref,
    routes_ref,
    rweight_ref,
    glen_s,
    slen_s,
    gof_s,
    wq,
    wo,
    root,
    gc,
    gg,
    sfx,
    eg,
    eu,
    ed,
    sg,
    su,
    sd,
    glr,
    hid_g,
    q_g,
    q_all,
    rs_out,
    rs_mass,
    po,
    pr,
    pm,
    pmr,
    po2,
    pz,
    pm2,
    pmz,
    att_g,
    mid_g,
    dsp_s,
    dsp_r,
    ret_s,
    ret_r,
    rs_s,
    rs_r,
    wide,
    part,
    load_sem,
    hid_ss,
    hid_rs,
    q_ss,
    q_rs,
    p_ss,
    p_rs,
    pm_ss,
    pm_rs,
    p2_ss,
    p2_rs,
    pm2_ss,
    pm2_rs,
    att_ss,
    att_rs,
    mid_ss,
    mid_rs,
    rs_ss,
    rs_rs,
    dsp_ss,
    dsp_rs,
    ret_ss,
    ret_rs,
    gl_ss,
    gl_rs,
    gc_ss,
    gc_rs,
):
    o = lax.axis_index("owner")
    t = lax.axis_index("tensor")

    def tpeer(k):
        return lax.rem(t + k, NT)

    def opeer(k):
        return lax.rem(o + k, NO)

    x = t // 8
    z = lax.rem(t, 8)
    open_recv = {}
    open_send = {}

    def remote(src, dst, ss, rs, to):
        return pltpu.make_async_remote_copy(
            src_ref=src, dst_ref=dst, send_sem=ss, recv_sem=rs, device_id=to, device_id_type=MESH
        )

    def over(first, last, step):
        def body(k, carry):
            step(k)
            return carry

        lax.fori_loop(first, last, body, 0)

    def far_first(n):
        kz = n // 4
        kx = lax.rem(n, 4)
        dz = 4 + (1 - 2 * lax.rem(kz, 2)) * ((kz + 1) // 2)
        dx = 2 + (1 - 2 * lax.rem(kx, 2)) * ((kx + 1) // 2)
        return lax.rem(x + dx, 4) * 8 + lax.rem(z + dz, 8)

    barrier = pltpu.get_barrier_semaphore()

    def greet(to):
        pl.semaphore_signal(barrier, inc=1, device_id=to, device_id_type=MESH)

    over(0, NT - 1, lambda n: greet({"tensor": far_first(n)}))
    over(1, NO, lambda k: greet({"owner": opeer(k)}))

    small = [
        pltpu.make_async_copy(src, dst, load_sem.at[11 + n])
        for n, (src, dst) in enumerate(
            [
                (hidden_hbm, hidden_ref),
                (glen_hbm, glen_s),
                (slen_hbm, slen_s),
                (gof_hbm, gof_s),
                (routes_hbm, routes_ref),
                (rweight_hbm, rweight_ref),
                (again_hbm, again_ref),
                (mgain_hbm, mgain_ref),
            ]
        )
    ]
    for load in small:
        load.start()

    wq[0:32, :] = jnp.zeros((32, D), BF16)
    wq[288:384, :] = jnp.zeros((96, D), BF16)
    shift = pl.multiple_of(lax.rem(t, 2) * 32, 32)
    loads = [
        pltpu.make_async_copy(wq_hbm, wq.at[pl.ds(shift, 288)], load_sem.at[0]),
        pltpu.make_async_copy(root_hbm, root, load_sem.at[1]),
        pltpu.make_async_copy(sfx_hbm, sfx, load_sem.at[2]),
        pltpu.make_async_copy(
            gcache_hbm, gc.at[pl.ds(GROUP_OWN * o, GROUP_OWN)], load_sem.at[3]
        ),
        pltpu.make_async_copy(wo_hbm, wo, load_sem.at[4]),
        pltpu.make_async_copy(sg_hbm, sg, load_sem.at[5]),
        pltpu.make_async_copy(su_hbm, su, load_sem.at[6]),
        pltpu.make_async_copy(sd_hbm, sd, load_sem.at[7]),
        pltpu.make_async_copy(eg_hbm.at[0], eg, load_sem.at[8]),
        pltpu.make_async_copy(eu_hbm.at[0], eu, load_sem.at[9]),
        pltpu.make_async_copy(ed_hbm.at[0], ed, load_sem.at[10]),
    ]
    for load in loads:
        load.start()
    for load in small:
        load.wait()

    hid_g[t] = pack(hidden_ref[...])
    lane_row = lanes((8, 128))
    own_lengths = jnp.zeros((8, 128), jnp.int32)
    for g in range(GROUP_OWN):
        own_lengths = jnp.where(lane_row == g, glen_s[g], own_lengths)
    glr[o] = own_lengths

    pl.semaphore_wait(barrier, NT - 1 + NO - 1)

    def bulk(buf, count, ss, rs, n=0, m=0):
        block = buf.at[pl.ds(0, count)]
        return remote(block, block, ss.at[m], rs.at[n], {"tensor": tpeer(1)})

    def gather_start(name, buf, ss, rs):
        over(
            0,
            NT - 1,
            lambda n: remote(
                buf.at[t], buf.at[t], ss.at[0], rs.at[0], {"tensor": far_first(n)}
            ).start(),
        )
        open_recv[name] = lambda: bulk(buf, NT - 1, ss, rs).wait_recv()
        open_send[name] = lambda: bulk(buf, NT - 1, ss, rs).wait_send()

    def spread_start(name, src, dst, ss, rs, axis):
        me, n = (t, NT) if axis == "tensor" else (o, NO)
        order = (
            far_first
            if axis == "tensor"
            else lambda k: opeer(4 + (1 - 2 * lax.rem(k, 2)) * ((k + 1) // 2))
        )

        def send(k):
            p = order(k)
            remote(src.at[p], dst.at[me], ss.at[0], rs.at[0], {axis: p}).start()

        over(0, n - 1, send)
        open_recv[name] = lambda: bulk(dst, n - 1, ss, rs).wait_recv()
        open_send[name] = lambda: bulk(src, n - 1, ss, rs).wait_send()

    def column_copy(buf, ss, rs, dz, slot):
        return remote(
            buf.at[slot],
            buf.at[slot],
            ss.at[0],
            rs.at[lax.rem(slot, 8)],
            {"tensor": x * 8 + lax.rem(z + dz, 8)},
        )

    def row_copy(buf, ss, rs, n, slot):
        dx = jnp.where(n == 0, 2, 2 * n - 1)
        return remote(
            buf.at[slot],
            buf.at[slot],
            ss.at[0],
            rs.at[8 + x],
            {"tensor": lax.rem(x + dx, 4) * 8 + z},
        )

    def relay_start(name, buf, ss, rs):
        over(0, 3, lambda n: row_copy(buf, ss, rs, n, t).start())
        over(0, 7, lambda k: column_copy(buf, ss, rs, near(k), t).start())
        open_recv[name] = lambda: relay_pass(name, buf, ss, rs, True)

    def near(k):
        return 4 + (1 - 2 * lax.rem(6 - k, 2)) * ((7 - k) // 2)

    def column_of(buf, ss, rs, xx):
        block = buf.at[pl.ds(8 * xx, 8)]
        remote(block, block, ss.at[0], rs.at[8 + xx], {"tensor": tpeer(1)}).wait_recv()

    def relay_pass(name, buf, ss, rs, rest):
        def pass_on(k):
            dz = near(k)
            slot = x * 8 + lax.rem(z + dz, 8)
            column_copy(buf, ss, rs, dz, slot).wait_recv()
            over(0, 3, lambda n: row_copy(buf, ss, rs, n, slot).start())

        over(0, 7, pass_on)

        open_send[name] = lambda: bulk(buf, NT - 1, ss, rs).wait_send()

        def columns():
            over(1, 4, lambda dx: column_of(buf, ss, rs, lax.rem(x + dx, 4)))

        if rest:
            columns()
        else:
            open_recv[name] = columns

    def arrived(name):
        open_recv.pop(name)()

    gather_start("hidden", hid_g, hid_ss, hid_rs)

    up = opeer(2)
    down = opeer(6)
    far = opeer(4)
    mate = o + 1 - 2 * lax.rem(o, 2)

    def groups(owner, first=0, count=GROUP_OWN):
        return gc.at[pl.ds(GROUP_OWN * owner + first, count)]

    def cache_copy(src, dst, n, to):
        return pltpu.make_async_remote_copy(
            src_ref=src,
            dst_ref=dst,
            send_sem=gc_ss.at[0 if n in (0, 1, 6, 7) else 1],
            recv_sem=gc_rs.at[n if n < 8 else n - 8 if 17 <= n < 21 else 8],
            device_id={"owner": to},
            device_id_type=MESH,
        )

    part_of = GROUP_OWN // 4

    def piece(owner, i):
        return groups(owner, part_of * i, part_of)

    mate_up = lax.rem(mate + 2, NO)
    mate_down = lax.rem(mate + 6, NO)
    mate_far = lax.rem(mate + 4, NO)

    def own_up(i):
        return cache_copy(gcache_hbm.at[pl.ds(part_of * i, part_of)], piece(o, i), i, up)

    def own_down(i):
        return cache_copy(gcache_hbm.at[pl.ds(part_of * i, part_of)], piece(o, i), 4 + i, down)

    def own_mate():
        return cache_copy(gcache_hbm, groups(o), 8, mate)

    for i in range(2):
        own_up(i).start()
        own_down(3 - i).start()
    own_mate().start()

    def to_mate(owner, i, n):
        return cache_copy(piece(owner, i), piece(owner, i), n + i, mate)

    def to_up(i):
        return cache_copy(piece(down, i), piece(down, i), 17 + i, up)

    def to_down(i):
        return cache_copy(piece(up, i), piece(up, i), 17 + i, down)

    over(
        1,
        NO,
        lambda k: remote(
            glr.at[o], glr.at[o], gl_ss.at[0], gl_rs.at[0], {"owner": opeer(k)}
        ).start(),
    )
    open_recv["lengths"] = lambda: bulk(glr, NO - 1, gl_ss, gl_rs).wait_recv()
    open_send["lengths"] = lambda: bulk(glr, NO - 1, gl_ss, gl_rs).wait_send()

    def caches_sent():
        bulk(gc, 72, gc_ss, gc_rs, 0, 1).wait_send()

    def from_down(i):
        cache_copy(piece(down, i), piece(down, i), i, up).wait_recv()
        to_mate(down, i, 9).start()
        if i < 2:
            to_up(i).start()

    def from_up(i):
        cache_copy(piece(up, i), piece(up, i), 4 + i, down).wait_recv()
        to_mate(up, i, 13).start()
        if i >= 2:
            to_down(i).start()

    def from_far(i):
        cache_copy(piece(far, i), piece(far, i), 17 + i, up).wait_recv()
        to_mate(far, i, 21).start()

    def from_mate():
        bulk(gc, 4 * GROUP_OWN, gc_ss, gc_rs, 8, 0).wait_recv()

    def second_half():
        bulk(gc, GROUP_OWN, gc_ss, gc_rs, 0, 0).wait_send()
        for i in range(2):
            own_up(2 + i).start()
            own_down(1 - i).start()

    cache_steps = [
        second_half,
        lambda: (from_down(0), from_up(3)),
        lambda: (from_down(1), from_up(2)),
        lambda: (from_down(2), from_up(1), from_down(3), from_up(0)),
        lambda: (from_far(0), from_far(3), from_far(1), from_far(2)),
        from_mate,
    ]

    def caches(n):
        for _ in range(n):
            cache_steps.pop(0)()

    open_recv["caches"] = lambda: caches(len(cache_steps))
    open_send["caches"] = caches_sent
    for n, load in enumerate(loads):
        open_recv[n] = load.wait


    row = rows((NO * SLOT, REQ))
    wanted = (row // SLOT) * 8 + t // 4
    hits = jnp.zeros((NO * SLOT, REQ), F32)
    share = jnp.zeros((NO * SLOT, REQ), F32)
    for k in range(6):
        match = routes_ref[k : k + 1, :] == wanted
        hits = jnp.where(match, 1.0, hits)
        share = jnp.where(match, rweight_ref[k : k + 1, :], share)
    before = (rows((REQ, REQ)) < lanes((REQ, REQ))).astype(BF16)
    rank = dot_n(hits.astype(BF16), before)
    picked = (hits > 0.5) & (rank == (row % SLOT).astype(F32))
    pick_t = jnp.where(picked, 1.0, 0.0).astype(BF16)
    share = jnp.transpose(jnp.where(picked, share, 0.0))

    r_iota = rows((REQ, 1))
    slen = jnp.zeros((REQ, 1), jnp.int32)
    gof = jnp.zeros((REQ, 1), jnp.int32)
    for r in range(REQ):
        slen = jnp.where(r_iota == r, slen_s[r], slen)
        gof = jnp.where(r_iota == r, gof_s[r], gof)
    arrived(0)
    caches(1)
    arrived("hidden")
    unpack_all(hid_g, wide)
    proj = dot_t(rms(wide, again_ref), wq[...])
    low32 = lanes((16, 128)) < 32
    odd = lax.rem(t, 2) == 1
    first = [proj[0:16, 128 * i : 128 * i + 128] for i in range(3)]
    last = [proj[16:32, 128 * i : 128 * i + 128] for i in range(3)]
    inner = jnp.logical_and(low32, odd)
    q_g[t] = jnp.concatenate(
        [
            jnp.where(inner, first[2], first[0]),
            first[1],
            jnp.where(inner, last[2], last[0]),
            last[1],
            jnp.where(inner, 0.0, first[2]) + pltpu.roll(jnp.where(inner, 0.0, last[2]), 64, 1),
        ],
        axis=1,
    ).astype(BF16)
    relay_start("queries", q_g, q_ss, q_rs)

    caches(2)
    open_recv.pop("queries")
    relay_pass("queries", q_g, q_ss, q_rs, False)
    arrived("lengths")
    lane128 = lanes((REQ, 128))
    glen_wide = jnp.zeros((REQ, 128), jnp.int32)
    for d in range(NO):
        mine = (gof - GROUP_OWN * d == lane128) & (lane128 < GROUP_OWN)
        glen_wide = jnp.where(mine, glr[d, 0:1, :], glen_wide)
    glen = jnp.sum(glen_wide, axis=1, keepdims=True)

    arrived(1)
    arrived(2)
    arrived(3)

    open_recv.pop("queries")
    n = 16 * HG
    for j in range(4):
        g = lax.rem(x + (0, 1, 3, 2)[j], 4)
        if j > 0:
            column_of(q_g, q_ss, q_rs, g)
        for h in range(HG):
            a = q_g[8 * g + 2 * h]
            b = q_g[8 * g + 2 * h + 1]
            hh = g * HG + h
            a4 = a[:, 512:640].astype(F32)
            b4 = b[:, 512:640].astype(F32)
            for r0, a_cols, a_tail, b_tail in (
                (0, 0, a4, b4),
                (16, 256, pltpu.roll(a4, 64, 1), pltpu.roll(b4, 64, 1)),
            ):
                b_head = b[:, a_cols : a_cols + 128].astype(F32)
                q_all[hh, r0 : r0 + 16, 0:256] = a[:, a_cols : a_cols + 256]
                q_all[hh, r0 : r0 + 16, 256:384] = jnp.where(low32, a_tail, b_head).astype(BF16)
                q_all[hh, r0 : r0 + 16, 384:512] = b[:, a_cols + 128 : a_cols + 256]
                q_all[hh, r0 : r0 + 16, 512:576] = jnp.where(low32, b_head, b_tail)[:, :64].astype(
                    BF16
                )
        if j == 0:
            caches(1)
        q = q_all[pl.ds(g * HG, HG)]
        all_out, all_mass = block_part(q.reshape(HG * REQ, KVW), None, None, root[...])
        all_out = all_out.reshape(HG, REQ, LAT)
        all_mass = all_mass.reshape(HG, REQ, 1)
        for c in range(2):
            r0 = 16 * c
            root_out = all_out[:, r0 : r0 + 16].reshape(n, LAT)
            root_mass = all_mass[:, r0 : r0 + 16].reshape(n, 1)
            s_col = lanes((n, 256))
            s_row = rows((n, 256)) % 16
            s_len = jnp.concatenate([slen[r0 : r0 + 16]] * HG, axis=0)
            s_ok = (s_col // 16 == s_row) & (t * 16 + s_col % 16 < s_len)
            sfx_out, sfx_mass = block_part(
                q[:, r0 : r0 + 16].reshape(n, KVW), sfx[r0 : r0 + 16].reshape(256, KVW), s_ok
            )
            out, mass = join((root_out, root_mass), (sfx_out, sfx_mass))
            rs_out[g, c] = out
            rs_mass[g, c] = mass
    caches(1)
    open_recv.pop("caches")
    caches(1)

    def fetch(r):
        gg[r] = gc[gof_s[r]]

    over(0, REQ, fetch)

    square = lanes((16, 128)) == rows((16, 128))

    def z_far(k):
        return lax.rem(z + 4 + (1 - 2 * lax.rem(k, 2)) * ((k + 1) // 2), 8)

    def po_copy(p, g):
        return remote(
            po.at[p], pr.at[x * 8 + p - 8 * g], p_ss.at[0], p_rs.at[p - 8 * g], {"tensor": g * 8 + z}
        )

    def pm_copy(g):
        return remote(
            pm.at[pl.ds(8 * g, 8)], pmr.at[pl.ds(8 * x, 8)], pm_ss.at[0], pm_rs.at[0], {"tensor": g * 8 + z}
        )

    for j in range(4):
        g = lax.rem(x + (2, 1, 3, 0)[j], 4)
        for c in range(2):
            r0 = 16 * c
            q = q_all[pl.ds(g * HG, HG), r0 : r0 + 16].reshape(n, KVW)
            g_col = lanes((n, 512))
            g_row = rows((n, 512)) % 16
            g_len = jnp.concatenate([glen[r0 : r0 + 16]] * HG, axis=0)
            g_ok = (g_col // 32 == g_row) & (t * 32 + g_col % 32 < g_len)
            grp_out, grp_mass = block_part(q, gg[r0 : r0 + 16].reshape(512, KVW), g_ok)
            grp_out = grp_out.astype(BF16).astype(F32)
            out, mass = join((rs_out[g, c], rs_mass[g, c]), (grp_out, grp_mass))
            out = out.astype(BF16)
            for h in range(HG):
                s = slice(16 * h, 16 * h + 16)
                po[8 * g + 2 * h + c] = out[s]
                pm[8 * g + 2 * h + c] = jnp.sum(
                    jnp.where(square, mass[s], 0.0), axis=0, keepdims=True
                )

        if j < 3:
            pm_copy(g).start()
            over(0, 8, lambda k, g=g: po_copy(8 * g + z_far(k), g).start())

    bulk(pmr, 24, pm_ss, pm_rs).wait_recv()

    def combine(outs, mass_rows):
        mass = [jnp.sum(jnp.where(square, m, 0.0), axis=1, keepdims=True) for m in mass_rows]
        top = functools.reduce(jnp.maximum, mass)
        w = [jnp.exp(m - top) for m in mass]
        total = functools.reduce(jnp.add, w)
        acc = functools.reduce(jnp.add, [v * out.astype(F32) for v, out in zip(w, outs)])
        return (acc / total).astype(BF16), top + jnp.log(total)

    def join_row(k):
        zz = z_far(k)

        bulk(pr, 3, p_ss, p_rs, zz).wait_recv()
        others = [lax.rem(x + i, 4) * 8 + zz for i in range(1, 4)]
        out, mass = combine(
            [po[x * 8 + zz]] + [pr[i] for i in others], [pm[x * 8 + zz]] + [pmr[i] for i in others]
        )
        po2[zz] = out
        pm2[zz] = jnp.sum(jnp.where(square, mass, 0.0), axis=0, keepdims=True)

    def to_column(src, dst, ss, rs, zz, slot):
        return remote(src.at[zz], dst.at[slot], ss.at[0], rs.at[0], {"tensor": x * 8 + zz})

    def join_and_send(k):
        join_row(k)
        zz = z_far(k)
        to_column(pm2, pmz, pm2_ss, pm2_rs, zz, z).start()
        to_column(po2, pz, p2_ss, p2_rs, zz, z).start()

    over(0, 7, join_and_send)
    join_row(7)
    pz[z] = po2[z]
    pmz[z] = pm2[z]

    def partial_sent():
        bulk(pm, 24, pm_ss, pm_rs).wait_send()
        bulk(po, 24, p_ss, p_rs).wait_send()
        bulk(pm2, 7, pm2_ss, pm2_rs).wait_send()
        bulk(po2, 7, p2_ss, p2_rs).wait_send()

    open_send["partial"] = partial_sent
    bulk(pmz, 7, pm2_ss, pm2_rs).wait_recv()
    bulk(pz, 7, p2_ss, p2_rs).wait_recv()
    att, _ = combine([pz[k] for k in range(8)], [pmz[k] for k in range(8)])
    att_g[t] = att
    relay_start("attention", att_g, att_ss, att_rs)
    arrived(4)
    arrived("attention")

    proj = jnp.zeros((REQ, 64), F32)
    for h in range(H):
        a = att_g[2 * h : 2 * h + 2].reshape(REQ, LAT)
        proj = proj + dot_t(a, wo[:, LAT * h : LAT * h + LAT])
    mid = (hidden_ref[...].astype(F32) + proj).astype(BF16)
    mid_g[t] = pack(mid)
    gather_start("mid", mid_g, mid_ss, mid_rs)
    arrived("mid")
    unpack_all(mid_g, wide)
    mix = rms(wide, mgain_ref)

    sent = dot_n(pick_t, mix)
    for d in range(NO):
        s = sent[SLOT * d : SLOT * d + SLOT]
        dsp_s[d] = jnp.concatenate([s[:, :HALF], s[:, HALF:]], axis=0).astype(BF16)
    spread_start("dispatch", dsp_s, dsp_r, dsp_ss, dsp_rs, "owner")
    dsp_r[o] = dsp_s[o]

    for n in range(5, 11):
        arrived(n)
    act = (silu(dot_t(mix, sg[...])) * dot_t(mix, su[...])).astype(BF16)
    part[...] = dot_n(act, sd[...])

    def slots(buf):
        low = jnp.concatenate([buf[d].astype(F32)[:SLOT] for d in range(NO)], axis=0)
        high = jnp.concatenate([buf[d].astype(F32)[SLOT:] for d in range(NO)], axis=0)
        return jnp.concatenate([low, high], axis=1).astype(BF16)

    arrived("dispatch")
    taken = slots(dsp_r)
    act = (silu(dot_t(taken, eg[...])) * dot_t(taken, eu[...])).astype(BF16)
    res = dot_n(act, ed[...])
    for d in range(NO):
        s = res[SLOT * d : SLOT * d + SLOT]
        ret_s[d] = jnp.concatenate([s[:, :HALF], s[:, HALF:]], axis=0).astype(BF16)
    spread_start("return", ret_s, ret_r, ret_ss, ret_rs, "owner")
    ret_r[o] = ret_s[o]
    s0 = share.astype(BF16)
    s1 = (share - s0.astype(F32)).astype(BF16)
    s2 = (share - s0.astype(F32) - s1.astype(F32)).astype(BF16)
    arrived("return")
    y = slots(ret_r)
    part[...] += dot_n(s0, y) + dot_n(s1, y) + dot_n(s2, y)

    low = lanes((16, 128)) < 64
    for i in range(NT // 2):
        a = part[0:16, 128 * i : 128 * i + 128]
        b = part[16:32, 128 * i : 128 * i + 128]
        rs_s[2 * i] = jnp.where(low, a, pltpu.roll(b, 64, 1)).astype(BF16)
        rs_s[2 * i + 1] = jnp.where(low, pltpu.roll(a, 64, 1), b).astype(BF16)

    spread_start("result", rs_s, rs_r, rs_ss, rs_rs, "tensor")
    rs_r[t] = rs_s[t]
    arrived("result")
    total = jnp.zeros((16, 128), F32)
    for k in range(NT):
        total = total + rs_r[k].astype(F32)
    summed = jnp.concatenate([total, pltpu.roll(total, 64, 1)], axis=0)[:, :64]
    out_ref[...] = (mid.astype(F32) + summed).astype(BF16)

    for wait in open_send.values():
        wait()


def local(
    hidden,
    attention_gain,
    query_weight,
    out_weight,
    root_cache,
    group_cache,
    group_length,
    suffix_cache,
    suffix_length,
    group_of,
    mixture_gain,
    routes,
    route_weight,
    expert_gate,
    expert_up,
    expert_down,
    shared_gate,
    shared_up,
    shared_down,
):
    vmem = pl.BlockSpec(memory_space=pltpu.VMEM)
    hbm = pl.BlockSpec(memory_space=pl.ANY)
    dma = pltpu.SemaphoreType.DMA
    return pl.pallas_call(
        kernel,
        out_shape=jax.ShapeDtypeStruct((REQ, 64), BF16),
        in_specs=[hbm] * 19,
        out_specs=vmem,
        scratch_shapes=[
            pltpu.VMEM((REQ, 64), BF16),
            pltpu.VMEM((D,), BF16),
            pltpu.VMEM((D,), BF16),
            pltpu.VMEM((6, REQ), jnp.int32),
            pltpu.VMEM((6, REQ), F32),
            pltpu.SMEM((GROUP_OWN,), jnp.int32),
            pltpu.SMEM((REQ,), jnp.int32),
            pltpu.SMEM((REQ,), jnp.int32),
            pltpu.VMEM((384, D), BF16),
            pltpu.VMEM((64, H * LAT), BF16),
            pltpu.VMEM((KVW, 1024), BF16),
            pltpu.VMEM((NO * GROUP_OWN, 32, KVW), BF16),
            pltpu.VMEM((REQ, 32, KVW), BF16),
            pltpu.VMEM((REQ, 16, KVW), BF16),
            pltpu.VMEM((352, D), BF16),
            pltpu.VMEM((352, D), BF16),
            pltpu.VMEM((352, D), BF16),
            pltpu.VMEM((88, D), BF16),
            pltpu.VMEM((88, D), BF16),
            pltpu.VMEM((88, D), BF16),
            pltpu.VMEM((NO, 8, 128), jnp.int32),
            pltpu.VMEM((NT, 16, 128), BF16),
            pltpu.VMEM((NT, 16, 640), BF16),
            pltpu.VMEM((H, REQ, KVW), BF16),
            pltpu.VMEM((4, 2, 16 * HG, LAT), F32),
            pltpu.VMEM((4, 2, 16 * HG, 1), F32),
            pltpu.VMEM((NT, 16, LAT), BF16),
            pltpu.VMEM((NT, 16, LAT), BF16),
            pltpu.VMEM((NT, 1, 128), F32),
            pltpu.VMEM((NT, 1, 128), F32),
            pltpu.VMEM((8, 16, LAT), BF16),
            pltpu.VMEM((8, 16, LAT), BF16),
            pltpu.VMEM((8, 1, 128), F32),
            pltpu.VMEM((8, 1, 128), F32),
            pltpu.VMEM((NT, 16, LAT), BF16),
            pltpu.VMEM((NT, 16, 128), BF16),
            pltpu.VMEM((NO, 2 * SLOT, HALF), BF16),
            pltpu.VMEM((NO, 2 * SLOT, HALF), BF16),
            pltpu.VMEM((NO, 2 * SLOT, HALF), BF16),
            pltpu.VMEM((NO, 2 * SLOT, HALF), BF16),
            pltpu.VMEM((NT, 16, 128), BF16),
            pltpu.VMEM((NT, 16, 128), BF16),
            pltpu.VMEM((REQ, D), F32),
            pltpu.VMEM((REQ, D), F32),
            dma((19,)),
        ]
        + [dma((n,)) for n in (1, 1, 1, 12, 1, 8, 1, 1, 1, 1, 1, 1, 1, 12, 1, 1, 1, 1, 1, 1, 1, 1, 1, 1, 2, 13)],
        compiler_params=pltpu.CompilerParams(
            collective_id=0, has_side_effects=True, vmem_limit_bytes=60 * 1024 * 1024
        ),
        name="layer",
    )(
        hidden,
        attention_gain,
        query_weight,
        out_weight,
        root_cache.T,
        group_cache,
        group_length,
        suffix_cache,
        suffix_length,
        group_of,
        mixture_gain,
        routes.T,
        route_weight.T,
        expert_gate,
        expert_up,
        expert_down,
        shared_gate,
        shared_up,
        shared_down,
    )


def solution(mesh):
    return jax.shard_map(
        local,
        mesh=mesh,
        in_specs=(
            P("owner", "tensor"),
            P(),
            P("tensor", None),
            P("tensor", None),
            P("tensor", None),
            P("owner", "tensor", None),
            P("owner"),
            P("owner", "tensor", None),
            P("owner"),
            P("owner"),
            P(),
            P("owner", None),
            P("owner", None),
            P(("owner", "tensor"), None, None),
            P(("owner", "tensor"), None, None),
            P(("owner", "tensor"), None, None),
            P("tensor", None),
            P("tensor", None),
            P("tensor", None),
        ),
        out_specs=P("owner", "tensor"),
        check_vma=False,
    )
```

```python
import functools

import jax
import jax.numpy as jnp
from jax import lax
from jax.experimental import pallas as pl
from jax.experimental.pallas import tpu as pltpu
from jax.sharding import PartitionSpec as P

D = 2048
H = 16
LAT = 512
KVW = 576
GROUP_OWN = 12
REQ = 32
NT = 32
NO = 8
SLOT = 8
HG = 4
SCALE = 192.0 ** (-0.5)
LOWEST = -1e30
EPS = 1e-06
MESH = pl.DeviceIdType.MESH
F32 = jnp.float32
BF16 = jnp.bfloat16


def dot_t(a, b):
    return lax.dot_general(a, b, (((1,), (1,)), ((), ())), preferred_element_type=F32)


def dot_n(a, b):
    return lax.dot_general(a, b, (((1,), (0,)), ((), ())), preferred_element_type=F32)


def lanes(shape):
    return lax.broadcasted_iota(jnp.int32, shape, len(shape) - 1)


def rows(shape):
    return lax.broadcasted_iota(jnp.int32, shape, len(shape) - 2)


def pack(x):
    return jnp.concatenate([x[:16], x[16:]], axis=1)


def unpack_all(blocks_ref, wide_ref):
    low = lanes((16, 128)) < 64
    for i in range(NT // 2):
        a = blocks_ref[2 * i].astype(F32)
        b = blocks_ref[2 * i + 1].astype(F32)
        wide_ref[0:16, 128 * i : 128 * i + 128] = jnp.where(low, a, pltpu.roll(b, 64, 1))
        wide_ref[16:32, 128 * i : 128 * i + 128] = jnp.where(low, pltpu.roll(a, 64, 1), b)


def rms(wide_ref, gain_ref):
    x = wide_ref[...]
    scaled = x * lax.rsqrt(jnp.mean(x * x, axis=-1, keepdims=True) + EPS)
    return (scaled * gain_ref[...].astype(F32)[None, :]).astype(BF16)


def block_part(q, keys, usable, keys_t=None):
    scores = (dot_t(q, keys) if keys_t is None else dot_n(q, keys_t)) * SCALE
    if usable is not None:
        scores = jnp.where(usable, scores, LOWEST)
    peak = jnp.max(scores, axis=-1, keepdims=True)
    weights = jnp.exp(scores - peak)
    if usable is not None:
        weights = jnp.where(usable, weights, 0.0)
    total = jnp.sum(weights, axis=-1, keepdims=True)
    weights = weights.astype(BF16)
    numerator = dot_n(weights, keys[:, :LAT]) if keys_t is None else dot_t(weights, keys_t[:LAT])
    present = total > 0.0
    safe = jnp.where(present, total, 1.0)
    return numerator, 1.0 / safe, jnp.where(present, peak + jnp.log(safe), LOWEST)


def join(first, second):
    first_sum, first_factor, first_mass = first
    second_sum, second_factor, second_mass = second
    top = jnp.maximum(first_mass, second_mass)
    first_w = jnp.exp(first_mass - top)
    second_w = jnp.exp(second_mass - top)
    total = first_w + second_w
    inverse = 1.0 / total
    out = (first_w * first_factor * inverse) * first_sum
    return out + (second_w * second_factor * inverse) * second_sum, top + jnp.log(total)


def pack_slots(s):
    row = rows((SLOT, 128))
    tiles = []
    for k in range(12):
        j = 128 * (12 + k // 3)
        spare = pltpu.roll(s[:, j : j + 128], (6 - 2 * (k % 3)) % 8, 0)
        tiles.append(jnp.where(row < 6, s[:, 128 * k : 128 * k + 128], spare))
    return jnp.concatenate(
        [jnp.concatenate(tiles[:6], axis=1), jnp.concatenate(tiles[6:], axis=1)], axis=0
    ).astype(BF16)


def unpack_slots(block):
    block = block.astype(F32)
    row = rows((SLOT, 128))
    tiles = [block[8 * (k // 6) : 8 * (k // 6) + 8, 128 * (k % 6) : 128 * (k % 6) + 128] for k in range(12)]
    for j in range(4):
        a, b, c = (pltpu.roll(tiles[3 * j + m], 2 * m + 2, 0) for m in range(3))
        tiles.append(jnp.where(row < 2, a, jnp.where(row < 4, b, c)))
    return jnp.concatenate(tiles, axis=1)


def silu(v):
    return v / (1.0 + jnp.exp(-v))


def kernel(
    hidden_hbm,
    again_hbm,
    wq_hbm,
    wo_hbm,
    root_hbm,
    gcache_hbm,
    glen_hbm,
    sfx_hbm,
    slen_hbm,
    gof_hbm,
    mgain_hbm,
    routes_hbm,
    rweight_hbm,
    eg_hbm,
    eu_hbm,
    ed_hbm,
    sg_hbm,
    su_hbm,
    sd_hbm,
    out_ref,
    hidden_ref,
    again_ref,
    mgain_ref,
    routes_ref,
    rweight_ref,
    glen_s,
    slen_s,
    gof_s,
    wq,
    wo,
    root,
    gc,
    gg,
    sfx,
    eg,
    eu,
    ed,
    sg,
    su,
    sd,
    glr,
    hid_g,
    q_g,
    q_all,
    rs_out,
    rs_mass,
    po,
    pr,
    pm,
    pmr,
    po2,
    pz,
    pm2,
    pmz,
    att_g,
    mid_g,
    dsp_s,
    dsp_r,
    ret_s,
    ret_r,
    rs_s,
    rs_r,
    wide,
    part,
    load_sem,
    hid_ss,
    hid_rs,
    q_ss,
    q_rs,
    p_ss,
    p_rs,
    pm_ss,
    pm_rs,
    p2_ss,
    p2_rs,
    pm2_ss,
    pm2_rs,
    att_ss,
    att_rs,
    mid_ss,
    mid_rs,
    rs_ss,
    rs_rs,
    dsp_ss,
    dsp_rs,
    ret_ss,
    ret_rs,
    gl_ss,
    gl_rs,
    gc_ss,
    gc_rs,
):
    o = lax.axis_index("owner")
    t = lax.axis_index("tensor")

    def tpeer(k):
        return lax.rem(t + k, NT)

    def opeer(k):
        return lax.rem(o + k, NO)

    x = t // 8
    z = lax.rem(t, 8)
    open_recv = {}
    open_send = {}

    def remote(src, dst, ss, rs, to):
        return pltpu.make_async_remote_copy(
            src_ref=src, dst_ref=dst, send_sem=ss, recv_sem=rs, device_id=to, device_id_type=MESH
        )

    def over(first, last, step):
        def body(k, carry):
            step(k)
            return carry

        lax.fori_loop(first, last, body, 0)

    def far_first(n):
        kz = n // 4
        kx = lax.rem(n, 4)
        dz = 4 + (1 - 2 * lax.rem(kz, 2)) * ((kz + 1) // 2)
        dx = 2 + (1 - 2 * lax.rem(kx, 2)) * ((kx + 1) // 2)
        return lax.rem(x + dx, 4) * 8 + lax.rem(z + dz, 8)

    barrier = pltpu.get_barrier_semaphore()

    def greet(to):
        pl.semaphore_signal(barrier, inc=1, device_id=to, device_id_type=MESH)

    over(0, NT - 1, lambda n: greet({"tensor": far_first(n)}))
    over(1, NO, lambda k: greet({"owner": opeer(k)}))

    small = [
        pltpu.make_async_copy(src, dst, load_sem.at[11 + n])
        for n, (src, dst) in enumerate(
            [
                (hidden_hbm, hidden_ref),
                (glen_hbm, glen_s),
                (slen_hbm, slen_s),
                (gof_hbm, gof_s),
                (routes_hbm, routes_ref),
                (rweight_hbm, rweight_ref),
                (again_hbm, again_ref),
                (mgain_hbm, mgain_ref),
            ]
        )
    ]
    for load in small:
        load.start()

    wq[0:32, :] = jnp.zeros((32, D), BF16)
    wq[288:384, :] = jnp.zeros((96, D), BF16)
    shift = pl.multiple_of(lax.rem(t, 2) * 32, 32)
    loads = [
        pltpu.make_async_copy(wq_hbm, wq.at[pl.ds(shift, 288)], load_sem.at[0]),
        pltpu.make_async_copy(root_hbm, root, load_sem.at[1]),
        pltpu.make_async_copy(sfx_hbm, sfx, load_sem.at[2]),
        pltpu.make_async_copy(
            gcache_hbm, gc.at[pl.ds(GROUP_OWN * o, GROUP_OWN)], load_sem.at[3]
        ),
        pltpu.make_async_copy(wo_hbm, wo, load_sem.at[4]),
        pltpu.make_async_copy(sg_hbm, sg, load_sem.at[5]),
        pltpu.make_async_copy(su_hbm, su, load_sem.at[6]),
        pltpu.make_async_copy(sd_hbm, sd, load_sem.at[7]),
        pltpu.make_async_copy(eg_hbm.at[0], eg, load_sem.at[8]),
        pltpu.make_async_copy(eu_hbm.at[0], eu, load_sem.at[9]),
        pltpu.make_async_copy(ed_hbm.at[0], ed, load_sem.at[10]),
    ]
    for load in loads:
        load.start()
    for load in small:
        load.wait()

    hid_g[t] = pack(hidden_ref[...])
    lane_row = lanes((8, 128))
    own_lengths = jnp.zeros((8, 128), jnp.int32)
    for g in range(GROUP_OWN):
        own_lengths = jnp.where(lane_row == g, glen_s[g], own_lengths)
    glr[o] = own_lengths

    pl.semaphore_wait(barrier, NT - 1 + NO - 1)

    def bulk(buf, count, ss, rs, n=0, m=0):
        block = buf.at[pl.ds(0, count)]
        return remote(block, block, ss.at[m], rs.at[n], {"tensor": tpeer(1)})

    def gather_start(name, buf, ss, rs):
        over(
            0,
            NT - 1,
            lambda n: remote(
                buf.at[t], buf.at[t], ss.at[0], rs.at[0], {"tensor": far_first(n)}
            ).start(),
        )
        open_recv[name] = lambda: bulk(buf, NT - 1, ss, rs).wait_recv()
        open_send[name] = lambda: bulk(buf, NT - 1, ss, rs).wait_send()

    def spread_start(name, src, dst, ss, rs, axis):
        me, n = (t, NT) if axis == "tensor" else (o, NO)
        order = (
            far_first
            if axis == "tensor"
            else lambda k: opeer(4 + (1 - 2 * lax.rem(k, 2)) * ((k + 1) // 2))
        )

        def send(k):
            p = order(k)
            remote(src.at[p], dst.at[me], ss.at[0], rs.at[0], {axis: p}).start()

        over(0, n - 1, send)
        open_recv[name] = lambda: bulk(dst, n - 1, ss, rs).wait_recv()
        open_send[name] = lambda: bulk(src, n - 1, ss, rs).wait_send()

    def column_copy(buf, ss, rs, dz, slot):
        return remote(
            buf.at[slot],
            buf.at[slot],
            ss.at[0],
            rs.at[lax.rem(slot, 8)],
            {"tensor": x * 8 + lax.rem(z + dz, 8)},
        )

    def row_copy(buf, ss, rs, n, slot):
        dx = jnp.where(n == 0, 2, 2 * n - 1)
        return remote(
            buf.at[slot],
            buf.at[slot],
            ss.at[0],
            rs.at[8 + x],
            {"tensor": lax.rem(x + dx, 4) * 8 + z},
        )

    def relay_start(name, buf, ss, rs):
        over(0, 3, lambda n: row_copy(buf, ss, rs, n, t).start())
        over(0, 7, lambda k: column_copy(buf, ss, rs, near(k), t).start())
        open_recv[name] = lambda: relay_pass(name, buf, ss, rs, True)

    def near(k):
        return 4 + (1 - 2 * lax.rem(6 - k, 2)) * ((7 - k) // 2)

    def column_of(buf, ss, rs, xx):
        block = buf.at[pl.ds(8 * xx, 8)]
        remote(block, block, ss.at[0], rs.at[8 + xx], {"tensor": tpeer(1)}).wait_recv()

    def relay_pass(name, buf, ss, rs, rest):
        def pass_on(k):
            dz = near(k)
            slot = x * 8 + lax.rem(z + dz, 8)
            column_copy(buf, ss, rs, dz, slot).wait_recv()
            over(0, 3, lambda n: row_copy(buf, ss, rs, n, slot).start())

        over(0, 7, pass_on)

        open_send[name] = lambda: bulk(buf, NT - 1, ss, rs).wait_send()

        def columns():
            over(1, 4, lambda dx: column_of(buf, ss, rs, lax.rem(x + dx, 4)))

        if rest:
            columns()
        else:
            open_recv[name] = columns

    def arrived(name):
        open_recv.pop(name)()

    gather_start("hidden", hid_g, hid_ss, hid_rs)

    up = opeer(2)
    down = opeer(6)
    far = opeer(4)
    mate = o + 1 - 2 * lax.rem(o, 2)

    def groups(owner, first=0, count=GROUP_OWN):
        return gc.at[pl.ds(GROUP_OWN * owner + first, count)]

    def cache_copy(src, dst, n, to):
        return pltpu.make_async_remote_copy(
            src_ref=src,
            dst_ref=dst,
            send_sem=gc_ss.at[0 if n in (0, 1, 6, 7) else 1],
            recv_sem=gc_rs.at[n if n < 8 else n - 8 if 17 <= n < 21 else 8],
            device_id={"owner": to},
            device_id_type=MESH,
        )

    part_of = GROUP_OWN // 4

    def piece(owner, i):
        return groups(owner, part_of * i, part_of)

    mate_up = lax.rem(mate + 2, NO)
    mate_down = lax.rem(mate + 6, NO)
    mate_far = lax.rem(mate + 4, NO)

    def own_up(i):
        return cache_copy(gcache_hbm.at[pl.ds(part_of * i, part_of)], piece(o, i), i, up)

    def own_down(i):
        return cache_copy(gcache_hbm.at[pl.ds(part_of * i, part_of)], piece(o, i), 4 + i, down)

    def own_mate():
        return cache_copy(gcache_hbm, groups(o), 8, mate)

    for i in range(2):
        own_up(i).start()
        own_down(3 - i).start()
    own_mate().start()

    def to_mate(owner, i, n):
        return cache_copy(piece(owner, i), piece(owner, i), n + i, mate)

    def to_up(i):
        return cache_copy(piece(down, i), piece(down, i), 17 + i, up)

    def to_down(i):
        return cache_copy(piece(up, i), piece(up, i), 17 + i, down)

    over(
        1,
        NO,
        lambda k: remote(
            glr.at[o], glr.at[o], gl_ss.at[0], gl_rs.at[0], {"owner": opeer(k)}
        ).start(),
    )
    open_recv["lengths"] = lambda: bulk(glr, NO - 1, gl_ss, gl_rs).wait_recv()
    open_send["lengths"] = lambda: bulk(glr, NO - 1, gl_ss, gl_rs).wait_send()

    def caches_sent():
        bulk(gc, 72, gc_ss, gc_rs, 0, 1).wait_send()

    def from_down(i):
        cache_copy(piece(down, i), piece(down, i), i, up).wait_recv()
        to_mate(down, i, 9).start()
        if i < 2:
            to_up(i).start()

    def from_up(i):
        cache_copy(piece(up, i), piece(up, i), 4 + i, down).wait_recv()
        to_mate(up, i, 13).start()
        if i >= 2:
            to_down(i).start()

    def from_far(i):
        cache_copy(piece(far, i), piece(far, i), 17 + i, up).wait_recv()
        to_mate(far, i, 21).start()

    def from_mate():
        bulk(gc, 4 * GROUP_OWN, gc_ss, gc_rs, 8, 0).wait_recv()

    def second_half():
        bulk(gc, GROUP_OWN, gc_ss, gc_rs, 0, 0).wait_send()
        for i in range(2):
            own_up(2 + i).start()
            own_down(1 - i).start()

    cache_steps = [
        second_half,
        lambda: (from_down(0), from_up(3)),
        lambda: (from_down(1), from_up(2)),
        lambda: (from_down(2), from_up(1), from_down(3), from_up(0)),
        lambda: (from_far(0), from_far(3), from_far(1), from_far(2)),
        from_mate,
    ]

    def caches(n):
        for _ in range(n):
            cache_steps.pop(0)()

    open_recv["caches"] = lambda: caches(len(cache_steps))
    open_send["caches"] = caches_sent
    for n, load in enumerate(loads):
        open_recv[n] = load.wait


    row = rows((NO * SLOT, REQ))
    wanted = (row // SLOT) * 8 + t // 4
    hits = jnp.zeros((NO * SLOT, REQ), F32)
    share = jnp.zeros((NO * SLOT, REQ), F32)
    for k in range(6):
        match = routes_ref[k : k + 1, :] == wanted
        hits = jnp.where(match, 1.0, hits)
        share = jnp.where(match, rweight_ref[k : k + 1, :], share)
    before = (rows((REQ, REQ)) < lanes((REQ, REQ))).astype(BF16)
    rank = dot_n(hits.astype(BF16), before)
    picked = (hits > 0.5) & (rank == (row % SLOT).astype(F32))
    pick_t = jnp.where(picked, 1.0, 0.0).astype(BF16)
    share = jnp.transpose(jnp.where(picked, share, 0.0))

    r_iota = rows((REQ, 1))
    slen = jnp.zeros((REQ, 1), jnp.int32)
    gof = jnp.zeros((REQ, 1), jnp.int32)
    for r in range(REQ):
        slen = jnp.where(r_iota == r, slen_s[r], slen)
        gof = jnp.where(r_iota == r, gof_s[r], gof)
    arrived(0)
    caches(1)
    arrived("hidden")
    unpack_all(hid_g, wide)
    proj = dot_t(rms(wide, again_ref), wq[...])
    low32 = lanes((16, 128)) < 32
    odd = lax.rem(t, 2) == 1
    first = [proj[0:16, 128 * i : 128 * i + 128] for i in range(3)]
    last = [proj[16:32, 128 * i : 128 * i + 128] for i in range(3)]
    inner = jnp.logical_and(low32, odd)
    q_g[t] = jnp.concatenate(
        [
            jnp.where(inner, first[2], first[0]),
            first[1],
            jnp.where(inner, last[2], last[0]),
            last[1],
            jnp.where(inner, 0.0, first[2]) + pltpu.roll(jnp.where(inner, 0.0, last[2]), 64, 1),
        ],
        axis=1,
    ).astype(BF16)
    relay_start("queries", q_g, q_ss, q_rs)

    caches(2)
    open_recv.pop("queries")
    relay_pass("queries", q_g, q_ss, q_rs, False)
    arrived("lengths")
    lane128 = lanes((REQ, 128))
    glen_wide = jnp.zeros((REQ, 128), jnp.int32)
    for d in range(NO):
        mine = (gof - GROUP_OWN * d == lane128) & (lane128 < GROUP_OWN)
        glen_wide = jnp.where(mine, glr[d, 0:1, :], glen_wide)
    glen = jnp.sum(glen_wide, axis=1, keepdims=True)

    arrived(1)
    arrived(2)
    arrived(3)

    open_recv.pop("queries")
    n = 16 * HG
    for j in range(4):
        g = lax.rem(x + (0, 1, 3, 2)[j], 4)
        if j > 0:
            column_of(q_g, q_ss, q_rs, g)
        for h in range(HG):
            a = q_g[8 * g + 2 * h]
            b = q_g[8 * g + 2 * h + 1]
            hh = g * HG + h
            a4 = a[:, 512:640].astype(F32)
            b4 = b[:, 512:640].astype(F32)
            for r0, a_cols, a_tail, b_tail in (
                (0, 0, a4, b4),
                (16, 256, pltpu.roll(a4, 64, 1), pltpu.roll(b4, 64, 1)),
            ):
                b_head = b[:, a_cols : a_cols + 128].astype(F32)
                q_all[hh, r0 : r0 + 16, 0:256] = a[:, a_cols : a_cols + 256]
                q_all[hh, r0 : r0 + 16, 256:384] = jnp.where(low32, a_tail, b_head).astype(BF16)
                q_all[hh, r0 : r0 + 16, 384:512] = b[:, a_cols + 128 : a_cols + 256]
                q_all[hh, r0 : r0 + 16, 512:576] = jnp.where(low32, b_head, b_tail)[:, :64].astype(
                    BF16
                )
        if j == 0:
            caches(1)
        q = q_all[pl.ds(g * HG, HG)]
        all_out, all_factor, all_mass = block_part(q.reshape(HG * REQ, KVW), None, None, root[...])
        all_out = all_out.reshape(HG, REQ, LAT)
        all_factor = all_factor.reshape(HG, REQ, 1)
        all_mass = all_mass.reshape(HG, REQ, 1)
        for c in range(2):
            r0 = 16 * c
            root_out = all_out[:, r0 : r0 + 16].reshape(n, LAT)
            root_factor = all_factor[:, r0 : r0 + 16].reshape(n, 1)
            root_mass = all_mass[:, r0 : r0 + 16].reshape(n, 1)
            s_col = lanes((n, 256))
            s_row = rows((n, 256)) % 16
            s_len = jnp.concatenate([slen[r0 : r0 + 16]] * HG, axis=0)
            s_ok = (s_col // 16 == s_row) & (t * 16 + s_col % 16 < s_len)
            sfx_part = block_part(
                q[:, r0 : r0 + 16].reshape(n, KVW), sfx[r0 : r0 + 16].reshape(256, KVW), s_ok
            )
            out, mass = join((root_out, root_factor, root_mass), sfx_part)
            rs_out[g, c] = out
            rs_mass[g, c] = mass
    caches(1)
    open_recv.pop("caches")
    caches(1)

    def fetch(r):
        gg[r] = gc[gof_s[r]]

    over(0, REQ, fetch)

    square = lanes((16, 128)) == rows((16, 128))

    def z_far(k):
        return lax.rem(z + 4 + (1 - 2 * lax.rem(k, 2)) * ((k + 1) // 2), 8)

    def po_copy(p, g):
        return remote(
            po.at[p], pr.at[x * 8 + p - 8 * g], p_ss.at[0], p_rs.at[p - 8 * g], {"tensor": g * 8 + z}
        )

    def pm_copy(g):
        return remote(
            pm.at[pl.ds(8 * g, 8)], pmr.at[pl.ds(8 * x, 8)], pm_ss.at[0], pm_rs.at[0], {"tensor": g * 8 + z}
        )

    for j in range(4):
        g = lax.rem(x + (2, 1, 3, 0)[j], 4)
        for c in range(2):
            r0 = 16 * c
            q = q_all[pl.ds(g * HG, HG), r0 : r0 + 16].reshape(n, KVW)
            g_col = lanes((n, 512))
            g_row = rows((n, 512)) % 16
            g_len = jnp.concatenate([glen[r0 : r0 + 16]] * HG, axis=0)
            g_ok = (g_col // 32 == g_row) & (t * 32 + g_col % 32 < g_len)
            grp_sum, grp_factor, grp_mass = block_part(q, gg[r0 : r0 + 16].reshape(512, KVW), g_ok)
            grp_out = (grp_sum * grp_factor).astype(BF16).astype(F32)
            out, mass = join((rs_out[g, c], 1.0, rs_mass[g, c]), (grp_out, 1.0, grp_mass))
            out = out.astype(BF16)
            for h in range(HG):
                s = slice(16 * h, 16 * h + 16)
                po[8 * g + 2 * h + c] = out[s]
                pm[8 * g + 2 * h + c] = jnp.sum(
                    jnp.where(square, mass[s], 0.0), axis=0, keepdims=True
                )

        if j < 3:
            pm_copy(g).start()
            over(0, 8, lambda k, g=g: po_copy(8 * g + z_far(k), g).start())

    bulk(pmr, 24, pm_ss, pm_rs).wait_recv()

    def combine(outs, mass_rows):
        mass = [jnp.sum(jnp.where(square, m, 0.0), axis=1, keepdims=True) for m in mass_rows]
        top = functools.reduce(jnp.maximum, mass)
        w = [jnp.exp(m - top) for m in mass]
        total = functools.reduce(jnp.add, w)
        acc = functools.reduce(jnp.add, [v * out.astype(F32) for v, out in zip(w, outs)])
        return (acc * (1.0 / total)).astype(BF16), top + jnp.log(total)

    def join_row(k):
        zz = z_far(k)

        bulk(pr, 3, p_ss, p_rs, zz).wait_recv()
        others = [lax.rem(x + i, 4) * 8 + zz for i in range(1, 4)]
        out, mass = combine(
            [po[x * 8 + zz]] + [pr[i] for i in others], [pm[x * 8 + zz]] + [pmr[i] for i in others]
        )
        po2[zz] = out
        pm2[zz] = jnp.sum(jnp.where(square, mass, 0.0), axis=0, keepdims=True)

    def to_column(src, dst, ss, rs, zz, slot):
        return remote(src.at[zz], dst.at[slot], ss.at[0], rs.at[0], {"tensor": x * 8 + zz})

    def join_and_send(k):
        join_row(k)
        zz = z_far(k)
        to_column(pm2, pmz, pm2_ss, pm2_rs, zz, z).start()
        to_column(po2, pz, p2_ss, p2_rs, zz, z).start()

    over(0, 7, join_and_send)
    join_row(7)
    pz[z] = po2[z]
    pmz[z] = pm2[z]

    def partial_sent():
        bulk(pm, 24, pm_ss, pm_rs).wait_send()
        bulk(po, 24, p_ss, p_rs).wait_send()
        bulk(pm2, 7, pm2_ss, pm2_rs).wait_send()
        bulk(po2, 7, p2_ss, p2_rs).wait_send()

    open_send["partial"] = partial_sent
    bulk(pmz, 7, pm2_ss, pm2_rs).wait_recv()
    bulk(pz, 7, p2_ss, p2_rs).wait_recv()
    att, _ = combine([pz[k] for k in range(8)], [pmz[k] for k in range(8)])
    att_g[t] = att
    relay_start("attention", att_g, att_ss, att_rs)
    arrived(4)
    arrived("attention")

    proj = jnp.zeros((REQ, 64), F32)
    for h in range(H):
        a = att_g[2 * h : 2 * h + 2].reshape(REQ, LAT)
        proj = proj + dot_t(a, wo[:, LAT * h : LAT * h + LAT])
    mid = (hidden_ref[...].astype(F32) + proj).astype(BF16)
    mid_g[t] = pack(mid)
    gather_start("mid", mid_g, mid_ss, mid_rs)
    arrived("mid")
    unpack_all(mid_g, wide)
    mix = rms(wide, mgain_ref)

    sent = dot_n(pick_t, mix)
    for d in range(NO):
        s = sent[SLOT * d : SLOT * d + SLOT]
        dsp_s[d] = pack_slots(s)
    spread_start("dispatch", dsp_s, dsp_r, dsp_ss, dsp_rs, "owner")
    dsp_r[o] = dsp_s[o]

    for n in range(5, 11):
        arrived(n)
    act = (silu(dot_t(mix, sg[...])) * dot_t(mix, su[...])).astype(BF16)
    part[...] = dot_n(act, sd[...])

    def slots(buf):
        return jnp.concatenate([unpack_slots(buf[d]) for d in range(NO)], axis=0).astype(BF16)

    arrived("dispatch")
    taken = slots(dsp_r)
    act = (silu(dot_t(taken, eg[...])) * dot_t(taken, eu[...])).astype(BF16)
    res = dot_n(act, ed[...])
    for d in range(NO):
        s = res[SLOT * d : SLOT * d + SLOT]
        ret_s[d] = pack_slots(s)
    spread_start("return", ret_s, ret_r, ret_ss, ret_rs, "owner")
    ret_r[o] = ret_s[o]
    s0 = share.astype(BF16)
    s1 = (share - s0.astype(F32)).astype(BF16)
    s2 = (share - s0.astype(F32) - s1.astype(F32)).astype(BF16)
    arrived("return")
    y = slots(ret_r)
    part[...] += dot_n(s0, y) + dot_n(s1, y) + dot_n(s2, y)

    low = lanes((16, 128)) < 64
    for i in range(NT // 2):
        a = part[0:16, 128 * i : 128 * i + 128]
        b = part[16:32, 128 * i : 128 * i + 128]
        rs_s[2 * i] = jnp.where(low, a, pltpu.roll(b, 64, 1)).astype(BF16)
        rs_s[2 * i + 1] = jnp.where(low, pltpu.roll(a, 64, 1), b).astype(BF16)

    spread_start("result", rs_s, rs_r, rs_ss, rs_rs, "tensor")
    rs_r[t] = rs_s[t]
    arrived("result")
    total = jnp.zeros((16, 128), F32)
    for k in range(NT):
        total = total + rs_r[k].astype(F32)
    summed = jnp.concatenate([total, pltpu.roll(total, 64, 1)], axis=0)[:, :64]
    out_ref[...] = (mid.astype(F32) + summed).astype(BF16)

    for wait in open_send.values():
        wait()


def local(
    hidden,
    attention_gain,
    query_weight,
    out_weight,
    root_cache,
    group_cache,
    group_length,
    suffix_cache,
    suffix_length,
    group_of,
    mixture_gain,
    routes,
    route_weight,
    expert_gate,
    expert_up,
    expert_down,
    shared_gate,
    shared_up,
    shared_down,
):
    vmem = pl.BlockSpec(memory_space=pltpu.VMEM)
    hbm = pl.BlockSpec(memory_space=pl.ANY)
    dma = pltpu.SemaphoreType.DMA
    return pl.pallas_call(
        kernel,
        out_shape=jax.ShapeDtypeStruct((REQ, 64), BF16),
        in_specs=[hbm] * 19,
        out_specs=vmem,
        scratch_shapes=[
            pltpu.VMEM((REQ, 64), BF16),
            pltpu.VMEM((D,), BF16),
            pltpu.VMEM((D,), BF16),
            pltpu.VMEM((6, REQ), jnp.int32),
            pltpu.VMEM((6, REQ), F32),
            pltpu.SMEM((GROUP_OWN,), jnp.int32),
            pltpu.SMEM((REQ,), jnp.int32),
            pltpu.SMEM((REQ,), jnp.int32),
            pltpu.VMEM((384, D), BF16),
            pltpu.VMEM((64, H * LAT), BF16),
            pltpu.VMEM((KVW, 1024), BF16),
            pltpu.VMEM((NO * GROUP_OWN, 32, KVW), BF16),
            pltpu.VMEM((REQ, 32, KVW), BF16),
            pltpu.VMEM((REQ, 16, KVW), BF16),
            pltpu.VMEM((352, D), BF16),
            pltpu.VMEM((352, D), BF16),
            pltpu.VMEM((352, D), BF16),
            pltpu.VMEM((88, D), BF16),
            pltpu.VMEM((88, D), BF16),
            pltpu.VMEM((88, D), BF16),
            pltpu.VMEM((NO, 8, 128), jnp.int32),
            pltpu.VMEM((NT, 16, 128), BF16),
            pltpu.VMEM((NT, 16, 640), BF16),
            pltpu.VMEM((H, REQ, KVW), BF16),
            pltpu.VMEM((4, 2, 16 * HG, LAT), F32),
            pltpu.VMEM((4, 2, 16 * HG, 1), F32),
            pltpu.VMEM((NT, 16, LAT), BF16),
            pltpu.VMEM((NT, 16, LAT), BF16),
            pltpu.VMEM((NT, 1, 128), F32),
            pltpu.VMEM((NT, 1, 128), F32),
            pltpu.VMEM((8, 16, LAT), BF16),
            pltpu.VMEM((8, 16, LAT), BF16),
            pltpu.VMEM((8, 1, 128), F32),
            pltpu.VMEM((8, 1, 128), F32),
            pltpu.VMEM((NT, 16, LAT), BF16),
            pltpu.VMEM((NT, 16, 128), BF16),
            pltpu.VMEM((NO, 16, 768), BF16),
            pltpu.VMEM((NO, 16, 768), BF16),
            pltpu.VMEM((NO, 16, 768), BF16),
            pltpu.VMEM((NO, 16, 768), BF16),
            pltpu.VMEM((NT, 16, 128), BF16),
            pltpu.VMEM((NT, 16, 128), BF16),
            pltpu.VMEM((REQ, D), F32),
            pltpu.VMEM((REQ, D), F32),
            dma((19,)),
        ]
        + [dma((n,)) for n in (1, 1, 1, 12, 1, 8, 1, 1, 1, 1, 1, 1, 1, 12, 1, 1, 1, 1, 1, 1, 1, 1, 1, 1, 2, 13)],
        compiler_params=pltpu.CompilerParams(
            collective_id=0, has_side_effects=True, vmem_limit_bytes=60 * 1024 * 1024
        ),
        name="layer",
    )(
        hidden,
        attention_gain,
        query_weight,
        out_weight,
        root_cache.T,
        group_cache,
        group_length,
        suffix_cache,
        suffix_length,
        group_of,
        mixture_gain,
        routes.T,
        route_weight.T,
        expert_gate,
        expert_up,
        expert_down,
        shared_gate,
        shared_up,
        shared_down,
    )


def solution(mesh):
    return jax.shard_map(
        local,
        mesh=mesh,
        in_specs=(
            P("owner", "tensor"),
            P(),
            P("tensor", None),
            P("tensor", None),
            P("tensor", None),
            P("owner", "tensor", None),
            P("owner"),
            P("owner", "tensor", None),
            P("owner"),
            P("owner"),
            P(),
            P("owner", None),
            P("owner", None),
            P(("owner", "tensor"), None, None),
            P(("owner", "tensor"), None, None),
            P(("owner", "tensor"), None, None),
            P("tensor", None),
            P("tensor", None),
            P("tensor", None),
        ),
        out_specs=P("owner", "tensor"),
        check_vma=False,
    )
```

```python
import functools

import jax
import jax.numpy as jnp
from jax import lax
from jax.experimental import pallas as pl
from jax.experimental.pallas import tpu as pltpu
from jax.sharding import PartitionSpec as P

D = 2048
H = 16
LAT = 512
KVW = 576
GROUP_OWN = 12
REQ = 32
NT = 32
NO = 8
SLOT = 8
HG = 4
SCALE = 192.0 ** (-0.5)
LOWEST = -1e30
EPS = 1e-06
MESH = pl.DeviceIdType.MESH
F32 = jnp.float32
BF16 = jnp.bfloat16


def dot_t(a, b):
    return lax.dot_general(a, b, (((1,), (1,)), ((), ())), preferred_element_type=F32)


def dot_n(a, b):
    return lax.dot_general(a, b, (((1,), (0,)), ((), ())), preferred_element_type=F32)


def lanes(shape):
    return lax.broadcasted_iota(jnp.int32, shape, len(shape) - 1)


def rows(shape):
    return lax.broadcasted_iota(jnp.int32, shape, len(shape) - 2)


def pack(x):
    return jnp.concatenate([x[:16], x[16:]], axis=1)


def unpack_all(blocks_ref, wide_ref):
    low = lanes((16, 128)) < 64
    for i in range(NT // 2):
        a = blocks_ref[2 * i].astype(F32)
        b = blocks_ref[2 * i + 1].astype(F32)
        wide_ref[0:16, 128 * i : 128 * i + 128] = jnp.where(low, a, pltpu.roll(b, 64, 1))
        wide_ref[16:32, 128 * i : 128 * i + 128] = jnp.where(low, pltpu.roll(a, 64, 1), b)


def rms(wide_ref, gain_ref):
    x = wide_ref[...]
    scaled = x * lax.rsqrt(jnp.mean(x * x, axis=-1, keepdims=True) + EPS)
    return (scaled * gain_ref[...].astype(F32)[None, :]).astype(BF16)


def block_part(q, keys, usable, keys_t=None):
    scores = (dot_t(q, keys) if keys_t is None else dot_n(q, keys_t)) * SCALE
    if usable is not None:
        scores = jnp.where(usable, scores, LOWEST)
    peak = jnp.max(scores, axis=-1, keepdims=True)
    weights = jnp.exp(scores - peak)
    if usable is not None:
        weights = jnp.where(usable, weights, 0.0)
    total = jnp.sum(weights, axis=-1, keepdims=True)
    weights = weights.astype(BF16)
    numerator = dot_n(weights, keys[:, :LAT]) if keys_t is None else dot_t(weights, keys_t[:LAT])
    present = total > 0.0
    safe = jnp.where(present, total, 1.0)
    return numerator, 1.0 / safe, jnp.where(present, peak + jnp.log(safe), LOWEST)


def join(first, second):
    first_sum, first_factor, first_mass = first
    second_sum, second_factor, second_mass = second
    top = jnp.maximum(first_mass, second_mass)
    first_w = jnp.exp(first_mass - top)
    second_w = jnp.exp(second_mass - top)
    total = first_w + second_w
    inverse = 1.0 / total
    out = (first_w * first_factor * inverse) * first_sum
    return out + (second_w * second_factor * inverse) * second_sum, top + jnp.log(total)


def pack_slots(s):
    row = rows((SLOT, 128))
    tiles = []
    for k in range(12):
        j = 128 * (12 + k // 3)
        spare = pltpu.roll(s[:, j : j + 128], (6 - 2 * (k % 3)) % 8, 0)
        tiles.append(jnp.where(row < 6, s[:, 128 * k : 128 * k + 128], spare))
    return jnp.concatenate(
        [jnp.concatenate(tiles[:6], axis=1), jnp.concatenate(tiles[6:], axis=1)], axis=0
    ).astype(BF16)


def unpack_slots(block):
    block = block.astype(F32)
    row = rows((SLOT, 128))
    tiles = [block[8 * (k // 6) : 8 * (k // 6) + 8, 128 * (k % 6) : 128 * (k % 6) + 128] for k in range(12)]
    for j in range(4):
        a, b, c = (pltpu.roll(tiles[3 * j + m], 2 * m + 2, 0) for m in range(3))
        tiles.append(jnp.where(row < 2, a, jnp.where(row < 4, b, c)))
    return jnp.concatenate(tiles, axis=1)


def silu(v):
    return v / (1.0 + jnp.exp(-v))


def kernel(
    hidden_hbm,
    again_hbm,
    wq_hbm,
    wo_hbm,
    root_hbm,
    gcache_hbm,
    glen_hbm,
    sfx_hbm,
    slen_hbm,
    gof_hbm,
    mgain_hbm,
    routes_hbm,
    rweight_hbm,
    eg_hbm,
    eu_hbm,
    ed_hbm,
    sg_hbm,
    su_hbm,
    sd_hbm,
    out_ref,
    hidden_ref,
    again_ref,
    mgain_ref,
    routes_ref,
    rweight_ref,
    glen_s,
    slen_s,
    gof_s,
    wq,
    wo,
    root,
    gc,
    gg,
    sfx,
    eg,
    eu,
    ed,
    sg,
    su,
    sd,
    glr,
    hid_g,
    q_g,
    q_all,
    rs_out,
    rs_mass,
    po,
    pr,
    pm,
    pmr,
    po2,
    pz,
    pm2,
    pmz,
    att_g,
    mid_g,
    dsp_s,
    dsp_r,
    ret_s,
    ret_r,
    rs_s,
    rs_r,
    wide,
    part,
    load_sem,
    hid_ss,
    hid_rs,
    q_ss,
    q_rs,
    p_ss,
    p_rs,
    pm_ss,
    pm_rs,
    p2_ss,
    p2_rs,
    pm2_ss,
    pm2_rs,
    att_ss,
    att_rs,
    mid_ss,
    mid_rs,
    rs_ss,
    rs_rs,
    dsp_ss,
    dsp_rs,
    ret_ss,
    ret_rs,
    gl_ss,
    gl_rs,
    gc_ss,
    gc_rs,
):
    o = lax.axis_index("owner")
    t = lax.axis_index("tensor")

    def tpeer(k):
        return lax.rem(t + k, NT)

    def opeer(k):
        return lax.rem(o + k, NO)

    x = t // 8
    z = lax.rem(t, 8)
    open_recv = {}
    open_send = {}

    def remote(src, dst, ss, rs, to):
        return pltpu.make_async_remote_copy(
            src_ref=src, dst_ref=dst, send_sem=ss, recv_sem=rs, device_id=to, device_id_type=MESH
        )

    def over(first, last, step):
        def body(k, carry):
            step(k)
            return carry

        lax.fori_loop(first, last, body, 0)

    def far_first(n):
        kz = n // 4
        kx = lax.rem(n, 4)
        dz = 4 + (1 - 2 * lax.rem(kz, 2)) * ((kz + 1) // 2)
        dx = 2 + (1 - 2 * lax.rem(kx, 2)) * ((kx + 1) // 2)
        return lax.rem(x + dx, 4) * 8 + lax.rem(z + dz, 8)

    barrier = pltpu.get_barrier_semaphore()

    def greet(to):
        pl.semaphore_signal(barrier, inc=1, device_id=to, device_id_type=MESH)

    over(0, NT - 1, lambda n: greet({"tensor": far_first(n)}))
    over(1, NO, lambda k: greet({"owner": opeer(k)}))

    small = [
        pltpu.make_async_copy(src, dst, load_sem.at[11 + n])
        for n, (src, dst) in enumerate(
            [
                (hidden_hbm, hidden_ref),
                (glen_hbm, glen_s),
                (slen_hbm, slen_s),
                (gof_hbm, gof_s),
                (routes_hbm, routes_ref),
                (rweight_hbm, rweight_ref),
                (again_hbm, again_ref),
                (mgain_hbm, mgain_ref),
            ]
        )
    ]
    for load in small:
        load.start()

    wq[0:32, :] = jnp.zeros((32, D), BF16)
    wq[288:384, :] = jnp.zeros((96, D), BF16)
    shift = pl.multiple_of(lax.rem(t, 2) * 32, 32)
    loads = [
        pltpu.make_async_copy(wq_hbm, wq.at[pl.ds(shift, 288)], load_sem.at[0]),
        pltpu.make_async_copy(root_hbm, root, load_sem.at[1]),
        pltpu.make_async_copy(sfx_hbm, sfx, load_sem.at[2]),
        pltpu.make_async_copy(
            gcache_hbm, gc.at[pl.ds(GROUP_OWN * o, GROUP_OWN)], load_sem.at[3]
        ),
        pltpu.make_async_copy(wo_hbm, wo, load_sem.at[4]),
        pltpu.make_async_copy(sg_hbm, sg, load_sem.at[5]),
        pltpu.make_async_copy(su_hbm, su, load_sem.at[6]),
        pltpu.make_async_copy(sd_hbm, sd, load_sem.at[7]),
        pltpu.make_async_copy(eg_hbm.at[0], eg, load_sem.at[8]),
        pltpu.make_async_copy(eu_hbm.at[0], eu, load_sem.at[9]),
        pltpu.make_async_copy(ed_hbm.at[0], ed, load_sem.at[10]),
    ]
    for load in loads:
        load.start()
    for load in small:
        load.wait()

    hid_g[t] = pack(hidden_ref[...])
    lane_row = lanes((8, 128))
    own_lengths = jnp.zeros((8, 128), jnp.int32)
    for g in range(GROUP_OWN):
        own_lengths = jnp.where(lane_row == g, glen_s[g], own_lengths)
    glr[o] = own_lengths

    pl.semaphore_wait(barrier, NT - 1 + NO - 1)

    def bulk(buf, count, ss, rs, n=0, m=0):
        block = buf.at[pl.ds(0, count)]
        return remote(block, block, ss.at[m], rs.at[n], {"tensor": tpeer(1)})

    def gather_start(name, buf, ss, rs):
        over(
            0,
            NT - 1,
            lambda n: remote(
                buf.at[t], buf.at[t], ss.at[0], rs.at[0], {"tensor": far_first(n)}
            ).start(),
        )
        open_recv[name] = lambda: bulk(buf, NT - 1, ss, rs).wait_recv()
        open_send[name] = lambda: bulk(buf, NT - 1, ss, rs).wait_send()

    def spread_start(name, src, dst, ss, rs, axis):
        me, n = (t, NT) if axis == "tensor" else (o, NO)
        order = (
            far_first
            if axis == "tensor"
            else lambda k: opeer(4 + (1 - 2 * lax.rem(k, 2)) * ((k + 1) // 2))
        )

        def send(k):
            p = order(k)
            remote(src.at[p], dst.at[me], ss.at[0], rs.at[0], {axis: p}).start()

        over(0, n - 1, send)
        open_recv[name] = lambda: bulk(dst, n - 1, ss, rs).wait_recv()
        open_send[name] = lambda: bulk(src, n - 1, ss, rs).wait_send()

    def column_copy(buf, ss, rs, dz, slot):
        return remote(
            buf.at[slot],
            buf.at[slot],
            ss.at[0],
            rs.at[lax.rem(slot, 8)],
            {"tensor": x * 8 + lax.rem(z + dz, 8)},
        )

    def row_copy(buf, ss, rs, n, slot):
        dx = jnp.where(n == 0, 2, 2 * n - 1)
        return remote(
            buf.at[slot],
            buf.at[slot],
            ss.at[0],
            rs.at[8 + x],
            {"tensor": lax.rem(x + dx, 4) * 8 + z},
        )

    def relay_start(name, buf, ss, rs):
        over(0, 3, lambda n: row_copy(buf, ss, rs, n, t).start())
        over(0, 7, lambda k: column_copy(buf, ss, rs, near(k), t).start())
        open_recv[name] = lambda: relay_pass(name, buf, ss, rs, True)

    def near(k):
        return 4 + (1 - 2 * lax.rem(6 - k, 2)) * ((7 - k) // 2)

    def column_of(buf, ss, rs, xx):
        block = buf.at[pl.ds(8 * xx, 8)]
        remote(block, block, ss.at[0], rs.at[8 + xx], {"tensor": tpeer(1)}).wait_recv()

    def relay_pass(name, buf, ss, rs, rest):
        def pass_on(k):
            dz = near(k)
            slot = x * 8 + lax.rem(z + dz, 8)
            column_copy(buf, ss, rs, dz, slot).wait_recv()
            over(0, 3, lambda n: row_copy(buf, ss, rs, n, slot).start())

        over(0, 7, pass_on)

        open_send[name] = lambda: bulk(buf, NT - 1, ss, rs).wait_send()

        def columns():
            over(1, 4, lambda dx: column_of(buf, ss, rs, lax.rem(x + dx, 4)))

        if rest:
            columns()
        else:
            open_recv[name] = columns

    def arrived(name):
        open_recv.pop(name)()

    gather_start("hidden", hid_g, hid_ss, hid_rs)

    up = opeer(2)
    down = opeer(6)
    far = opeer(4)
    mate = o + 1 - 2 * lax.rem(o, 2)

    def groups(owner, first=0, count=GROUP_OWN):
        return gc.at[pl.ds(GROUP_OWN * owner + first, count)]

    def cache_copy(src, dst, n, to):
        return pltpu.make_async_remote_copy(
            src_ref=src,
            dst_ref=dst,
            send_sem=gc_ss.at[0 if n in (0, 1, 6, 7) else 1],
            recv_sem=gc_rs.at[n if n < 8 else n - 8 if 17 <= n < 21 else 8],
            device_id={"owner": to},
            device_id_type=MESH,
        )

    part_of = GROUP_OWN // 4

    def piece(owner, i):
        return groups(owner, part_of * i, part_of)

    mate_up = lax.rem(mate + 2, NO)
    mate_down = lax.rem(mate + 6, NO)
    mate_far = lax.rem(mate + 4, NO)

    def own_up(i):
        return cache_copy(gcache_hbm.at[pl.ds(part_of * i, part_of)], piece(o, i), i, up)

    def own_down(i):
        return cache_copy(gcache_hbm.at[pl.ds(part_of * i, part_of)], piece(o, i), 4 + i, down)

    def own_mate():
        return cache_copy(gcache_hbm, groups(o), 8, mate)

    for i in range(2):
        own_up(i).start()
        own_down(3 - i).start()
    own_mate().start()

    def to_mate(owner, i, n):
        return cache_copy(piece(owner, i), piece(owner, i), n + i, mate)

    def to_up(i):
        return cache_copy(piece(down, i), piece(down, i), 17 + i, up)

    def to_down(i):
        return cache_copy(piece(up, i), piece(up, i), 17 + i, down)

    over(
        1,
        NO,
        lambda k: remote(
            glr.at[o], glr.at[o], gl_ss.at[0], gl_rs.at[0], {"owner": opeer(k)}
        ).start(),
    )
    open_recv["lengths"] = lambda: bulk(glr, NO - 1, gl_ss, gl_rs).wait_recv()
    open_send["lengths"] = lambda: bulk(glr, NO - 1, gl_ss, gl_rs).wait_send()

    def caches_sent():
        bulk(gc, 72, gc_ss, gc_rs, 0, 1).wait_send()

    def from_down(i):
        cache_copy(piece(down, i), piece(down, i), i, up).wait_recv()
        to_mate(down, i, 9).start()
        if i < 2:
            to_up(i).start()

    def from_up(i):
        cache_copy(piece(up, i), piece(up, i), 4 + i, down).wait_recv()
        to_mate(up, i, 13).start()
        if i >= 2:
            to_down(i).start()

    def from_far(i):
        cache_copy(piece(far, i), piece(far, i), 17 + i, up).wait_recv()
        to_mate(far, i, 21).start()

    def from_mate():
        bulk(gc, 4 * GROUP_OWN, gc_ss, gc_rs, 8, 0).wait_recv()

    def second_half():
        bulk(gc, GROUP_OWN, gc_ss, gc_rs, 0, 0).wait_send()
        for i in range(2):
            own_up(2 + i).start()
            own_down(1 - i).start()

    cache_steps = [
        second_half,
        lambda: (from_down(0), from_up(3)),
        lambda: (from_down(1), from_up(2)),
        lambda: (from_down(2), from_up(1), from_down(3), from_up(0)),
        lambda: (from_far(0), from_far(3), from_far(1), from_far(2)),
        from_mate,
    ]

    def caches(n):
        for _ in range(n):
            cache_steps.pop(0)()

    open_recv["caches"] = lambda: caches(len(cache_steps))
    open_send["caches"] = caches_sent
    for n, load in enumerate(loads):
        open_recv[n] = load.wait


    row = rows((NO * SLOT, REQ))
    wanted = (row // SLOT) * 8 + t // 4
    hits = jnp.zeros((NO * SLOT, REQ), F32)
    share = jnp.zeros((NO * SLOT, REQ), F32)
    for k in range(6):
        match = routes_ref[k : k + 1, :] == wanted
        hits = jnp.where(match, 1.0, hits)
        share = jnp.where(match, rweight_ref[k : k + 1, :], share)
    before = (rows((REQ, REQ)) < lanes((REQ, REQ))).astype(BF16)
    rank = dot_n(hits.astype(BF16), before)
    picked = (hits > 0.5) & (rank == (row % SLOT).astype(F32))
    pick_t = jnp.where(picked, 1.0, 0.0).astype(BF16)
    share = jnp.transpose(jnp.where(picked, share, 0.0))

    r_iota = rows((REQ, 1))
    slen = jnp.zeros((REQ, 1), jnp.int32)
    gof = jnp.zeros((REQ, 1), jnp.int32)
    for r in range(REQ):
        slen = jnp.where(r_iota == r, slen_s[r], slen)
        gof = jnp.where(r_iota == r, gof_s[r], gof)
    arrived(0)
    caches(1)
    arrived("hidden")
    unpack_all(hid_g, wide)
    proj = dot_t(rms(wide, again_ref), wq[...])
    low32 = lanes((16, 128)) < 32
    odd = lax.rem(t, 2) == 1
    first = [proj[0:16, 128 * i : 128 * i + 128] for i in range(3)]
    last = [proj[16:32, 128 * i : 128 * i + 128] for i in range(3)]
    inner = jnp.logical_and(low32, odd)
    q_g[t] = jnp.concatenate(
        [
            jnp.where(inner, first[2], first[0]),
            first[1],
            jnp.where(inner, last[2], last[0]),
            last[1],
            jnp.where(inner, 0.0, first[2]) + pltpu.roll(jnp.where(inner, 0.0, last[2]), 64, 1),
        ],
        axis=1,
    ).astype(BF16)
    relay_start("queries", q_g, q_ss, q_rs)

    caches(2)
    open_recv.pop("queries")
    relay_pass("queries", q_g, q_ss, q_rs, False)
    arrived("lengths")
    lane128 = lanes((REQ, 128))
    glen_wide = jnp.zeros((REQ, 128), jnp.int32)
    for d in range(NO):
        mine = (gof - GROUP_OWN * d == lane128) & (lane128 < GROUP_OWN)
        glen_wide = jnp.where(mine, glr[d, 0:1, :], glen_wide)
    glen = jnp.sum(glen_wide, axis=1, keepdims=True)

    arrived(1)
    arrived(2)
    arrived(3)

    open_recv.pop("queries")
    n = 16 * HG
    for j in range(4):
        g = lax.rem(x + (0, 1, 3, 2)[j], 4)
        if j > 0:
            column_of(q_g, q_ss, q_rs, g)
        for h in range(HG):
            a = q_g[8 * g + 2 * h]
            b = q_g[8 * g + 2 * h + 1]
            hh = g * HG + h
            a4 = a[:, 512:640].astype(F32)
            b4 = b[:, 512:640].astype(F32)
            for r0, a_cols, a_tail, b_tail in (
                (0, 0, a4, b4),
                (16, 256, pltpu.roll(a4, 64, 1), pltpu.roll(b4, 64, 1)),
            ):
                b_head = b[:, a_cols : a_cols + 128].astype(F32)
                q_all[hh, r0 : r0 + 16, 0:256] = a[:, a_cols : a_cols + 256]
                q_all[hh, r0 : r0 + 16, 256:384] = jnp.where(low32, a_tail, b_head).astype(BF16)
                q_all[hh, r0 : r0 + 16, 384:512] = b[:, a_cols + 128 : a_cols + 256]
                q_all[hh, r0 : r0 + 16, 512:576] = jnp.where(low32, b_head, b_tail)[:, :64].astype(
                    BF16
                )
        if j in (0, 3):
            caches(1)
        q = q_all[pl.ds(g * HG, HG)]
        all_out, all_factor, all_mass = block_part(q.reshape(HG * REQ, KVW), None, None, root[...])
        all_out = all_out.reshape(HG, REQ, LAT)
        all_factor = all_factor.reshape(HG, REQ, 1)
        all_mass = all_mass.reshape(HG, REQ, 1)
        for c in range(2):
            r0 = 16 * c
            root_out = all_out[:, r0 : r0 + 16].reshape(n, LAT)
            root_factor = all_factor[:, r0 : r0 + 16].reshape(n, 1)
            root_mass = all_mass[:, r0 : r0 + 16].reshape(n, 1)
            s_col = lanes((n, 256))
            s_row = rows((n, 256)) % 16
            s_len = jnp.concatenate([slen[r0 : r0 + 16]] * HG, axis=0)
            s_ok = (s_col // 16 == s_row) & (t * 16 + s_col % 16 < s_len)
            sfx_part = block_part(
                q[:, r0 : r0 + 16].reshape(n, KVW), sfx[r0 : r0 + 16].reshape(256, KVW), s_ok
            )
            out, mass = join((root_out, root_factor, root_mass), sfx_part)
            rs_out[g, c] = out
            rs_mass[g, c] = mass
    open_recv.pop("caches")
    caches(1)

    def fetch(r):
        gg[r] = gc[gof_s[r]]

    over(0, REQ, fetch)

    square = lanes((16, 128)) == rows((16, 128))

    def z_far(k):
        return lax.rem(z + 4 + (1 - 2 * lax.rem(k, 2)) * ((k + 1) // 2), 8)

    def po_copy(p, g):
        return remote(
            po.at[p], pr.at[x * 8 + p - 8 * g], p_ss.at[0], p_rs.at[p - 8 * g], {"tensor": g * 8 + z}
        )

    def pm_copy(g):
        return remote(
            pm.at[pl.ds(8 * g, 8)], pmr.at[pl.ds(8 * x, 8)], pm_ss.at[0], pm_rs.at[0], {"tensor": g * 8 + z}
        )

    for j in range(4):
        g = lax.rem(x + (2, 1, 3, 0)[j], 4)
        for c in range(2):
            r0 = 16 * c
            q = q_all[pl.ds(g * HG, HG), r0 : r0 + 16].reshape(n, KVW)
            g_col = lanes((n, 512))
            g_row = rows((n, 512)) % 16
            g_len = jnp.concatenate([glen[r0 : r0 + 16]] * HG, axis=0)
            g_ok = (g_col // 32 == g_row) & (t * 32 + g_col % 32 < g_len)
            grp_sum, grp_factor, grp_mass = block_part(q, gg[r0 : r0 + 16].reshape(512, KVW), g_ok)
            grp_out = (grp_sum * grp_factor).astype(BF16).astype(F32)
            out, mass = join((rs_out[g, c], 1.0, rs_mass[g, c]), (grp_out, 1.0, grp_mass))
            out = out.astype(BF16)
            for h in range(HG):
                s = slice(16 * h, 16 * h + 16)
                po[8 * g + 2 * h + c] = out[s]
                pm[8 * g + 2 * h + c] = jnp.sum(
                    jnp.where(square, mass[s], 0.0), axis=0, keepdims=True
                )

        if j < 3:
            pm_copy(g).start()
            over(0, 8, lambda k, g=g: po_copy(8 * g + z_far(k), g).start())

    bulk(pmr, 24, pm_ss, pm_rs).wait_recv()

    def combine(outs, mass_rows):
        mass = [jnp.sum(jnp.where(square, m, 0.0), axis=1, keepdims=True) for m in mass_rows]
        top = functools.reduce(jnp.maximum, mass)
        w = [jnp.exp(m - top) for m in mass]
        total = functools.reduce(jnp.add, w)
        acc = functools.reduce(jnp.add, [v * out.astype(F32) for v, out in zip(w, outs)])
        return (acc * (1.0 / total)).astype(BF16), top + jnp.log(total)

    def join_row(k):
        zz = z_far(k)

        bulk(pr, 3, p_ss, p_rs, zz).wait_recv()
        others = [lax.rem(x + i, 4) * 8 + zz for i in range(1, 4)]
        out, mass = combine(
            [po[x * 8 + zz]] + [pr[i] for i in others], [pm[x * 8 + zz]] + [pmr[i] for i in others]
        )
        po2[zz] = out
        pm2[zz] = jnp.sum(jnp.where(square, mass, 0.0), axis=0, keepdims=True)

    def to_column(src, dst, ss, rs, zz, slot):
        return remote(src.at[zz], dst.at[slot], ss.at[0], rs.at[0], {"tensor": x * 8 + zz})

    def join_and_send(k):
        join_row(k)
        zz = z_far(k)
        to_column(pm2, pmz, pm2_ss, pm2_rs, zz, z).start()
        to_column(po2, pz, p2_ss, p2_rs, zz, z).start()

    over(0, 7, join_and_send)
    join_row(7)
    pz[z] = po2[z]
    pmz[z] = pm2[z]

    def partial_sent():
        bulk(pm, 24, pm_ss, pm_rs).wait_send()
        bulk(po, 24, p_ss, p_rs).wait_send()
        bulk(pm2, 7, pm2_ss, pm2_rs).wait_send()
        bulk(po2, 7, p2_ss, p2_rs).wait_send()

    open_send["partial"] = partial_sent
    bulk(pmz, 7, pm2_ss, pm2_rs).wait_recv()
    bulk(pz, 7, p2_ss, p2_rs).wait_recv()
    att, _ = combine([pz[k] for k in range(8)], [pmz[k] for k in range(8)])
    att_g[t] = att
    relay_start("attention", att_g, att_ss, att_rs)
    arrived(4)
    arrived("attention")

    proj = jnp.zeros((REQ, 64), F32)
    for h in range(H):
        a = att_g[2 * h : 2 * h + 2].reshape(REQ, LAT)
        proj = proj + dot_t(a, wo[:, LAT * h : LAT * h + LAT])
    mid = (hidden_ref[...].astype(F32) + proj).astype(BF16)
    mid_g[t] = pack(mid)
    gather_start("mid", mid_g, mid_ss, mid_rs)
    arrived("mid")
    unpack_all(mid_g, wide)
    mix = rms(wide, mgain_ref)

    sent = dot_n(pick_t, mix)
    for d in range(NO):
        s = sent[SLOT * d : SLOT * d + SLOT]
        dsp_s[d] = pack_slots(s)
    spread_start("dispatch", dsp_s, dsp_r, dsp_ss, dsp_rs, "owner")
    dsp_r[o] = dsp_s[o]

    for n in range(5, 11):
        arrived(n)
    act = (silu(dot_t(mix, sg[...])) * dot_t(mix, su[...])).astype(BF16)
    part[...] = dot_n(act, sd[...])

    def slots(buf):
        return jnp.concatenate([unpack_slots(buf[d]) for d in range(NO)], axis=0).astype(BF16)

    arrived("dispatch")
    taken = slots(dsp_r)
    act = (silu(dot_t(taken, eg[...])) * dot_t(taken, eu[...])).astype(BF16)
    res = dot_n(act, ed[...])
    for d in range(NO):
        s = res[SLOT * d : SLOT * d + SLOT]
        ret_s[d] = pack_slots(s)
    spread_start("return", ret_s, ret_r, ret_ss, ret_rs, "owner")
    ret_r[o] = ret_s[o]
    s0 = share.astype(BF16)
    s1 = (share - s0.astype(F32)).astype(BF16)
    s2 = (share - s0.astype(F32) - s1.astype(F32)).astype(BF16)
    arrived("return")
    y = slots(ret_r)
    part[...] += dot_n(s0, y) + dot_n(s1, y) + dot_n(s2, y)

    low = lanes((16, 128)) < 64
    for i in range(NT // 2):
        a = part[0:16, 128 * i : 128 * i + 128]
        b = part[16:32, 128 * i : 128 * i + 128]
        rs_s[2 * i] = jnp.where(low, a, pltpu.roll(b, 64, 1)).astype(BF16)
        rs_s[2 * i + 1] = jnp.where(low, pltpu.roll(a, 64, 1), b).astype(BF16)

    spread_start("result", rs_s, rs_r, rs_ss, rs_rs, "tensor")
    rs_r[t] = rs_s[t]
    arrived("result")
    total = jnp.zeros((16, 128), F32)
    for k in range(NT):
        total = total + rs_r[k].astype(F32)
    summed = jnp.concatenate([total, pltpu.roll(total, 64, 1)], axis=0)[:, :64]
    out_ref[...] = (mid.astype(F32) + summed).astype(BF16)

    for wait in open_send.values():
        wait()


def local(
    hidden,
    attention_gain,
    query_weight,
    out_weight,
    root_cache,
    group_cache,
    group_length,
    suffix_cache,
    suffix_length,
    group_of,
    mixture_gain,
    routes,
    route_weight,
    expert_gate,
    expert_up,
    expert_down,
    shared_gate,
    shared_up,
    shared_down,
):
    vmem = pl.BlockSpec(memory_space=pltpu.VMEM)
    hbm = pl.BlockSpec(memory_space=pl.ANY)
    dma = pltpu.SemaphoreType.DMA
    return pl.pallas_call(
        kernel,
        out_shape=jax.ShapeDtypeStruct((REQ, 64), BF16),
        in_specs=[hbm] * 19,
        out_specs=vmem,
        scratch_shapes=[
            pltpu.VMEM((REQ, 64), BF16),
            pltpu.VMEM((D,), BF16),
            pltpu.VMEM((D,), BF16),
            pltpu.VMEM((6, REQ), jnp.int32),
            pltpu.VMEM((6, REQ), F32),
            pltpu.SMEM((GROUP_OWN,), jnp.int32),
            pltpu.SMEM((REQ,), jnp.int32),
            pltpu.SMEM((REQ,), jnp.int32),
            pltpu.VMEM((384, D), BF16),
            pltpu.VMEM((64, H * LAT), BF16),
            pltpu.VMEM((KVW, 1024), BF16),
            pltpu.VMEM((NO * GROUP_OWN, 32, KVW), BF16),
            pltpu.VMEM((REQ, 32, KVW), BF16),
            pltpu.VMEM((REQ, 16, KVW), BF16),
            pltpu.VMEM((352, D), BF16),
            pltpu.VMEM((352, D), BF16),
            pltpu.VMEM((352, D), BF16),
            pltpu.VMEM((88, D), BF16),
            pltpu.VMEM((88, D), BF16),
            pltpu.VMEM((88, D), BF16),
            pltpu.VMEM((NO, 8, 128), jnp.int32),
            pltpu.VMEM((NT, 16, 128), BF16),
            pltpu.VMEM((NT, 16, 640), BF16),
            pltpu.VMEM((H, REQ, KVW), BF16),
            pltpu.VMEM((4, 2, 16 * HG, LAT), F32),
            pltpu.VMEM((4, 2, 16 * HG, 1), F32),
            pltpu.VMEM((NT, 16, LAT), BF16),
            pltpu.VMEM((NT, 16, LAT), BF16),
            pltpu.VMEM((NT, 1, 128), F32),
            pltpu.VMEM((NT, 1, 128), F32),
            pltpu.VMEM((8, 16, LAT), BF16),
            pltpu.VMEM((8, 16, LAT), BF16),
            pltpu.VMEM((8, 1, 128), F32),
            pltpu.VMEM((8, 1, 128), F32),
            pltpu.VMEM((NT, 16, LAT), BF16),
            pltpu.VMEM((NT, 16, 128), BF16),
            pltpu.VMEM((NO, 16, 768), BF16),
            pltpu.VMEM((NO, 16, 768), BF16),
            pltpu.VMEM((NO, 16, 768), BF16),
            pltpu.VMEM((NO, 16, 768), BF16),
            pltpu.VMEM((NT, 16, 128), BF16),
            pltpu.VMEM((NT, 16, 128), BF16),
            pltpu.VMEM((REQ, D), F32),
            pltpu.VMEM((REQ, D), F32),
            dma((19,)),
        ]
        + [dma((n,)) for n in (1, 1, 1, 12, 1, 8, 1, 1, 1, 1, 1, 1, 1, 12, 1, 1, 1, 1, 1, 1, 1, 1, 1, 1, 2, 13)],
        compiler_params=pltpu.CompilerParams(
            collective_id=0, has_side_effects=True, vmem_limit_bytes=60 * 1024 * 1024
        ),
        name="layer",
    )(
        hidden,
        attention_gain,
        query_weight,
        out_weight,
        root_cache.T,
        group_cache,
        group_length,
        suffix_cache,
        suffix_length,
        group_of,
        mixture_gain,
        routes.T,
        route_weight.T,
        expert_gate,
        expert_up,
        expert_down,
        shared_gate,
        shared_up,
        shared_down,
    )


def solution(mesh):
    return jax.shard_map(
        local,
        mesh=mesh,
        in_specs=(
            P("owner", "tensor"),
            P(),
            P("tensor", None),
            P("tensor", None),
            P("tensor", None),
            P("owner", "tensor", None),
            P("owner"),
            P("owner", "tensor", None),
            P("owner"),
            P("owner"),
            P(),
            P("owner", None),
            P("owner", None),
            P(("owner", "tensor"), None, None),
            P(("owner", "tensor"), None, None),
            P(("owner", "tensor"), None, None),
            P("tensor", None),
            P("tensor", None),
            P("tensor", None),
        ),
        out_specs=P("owner", "tensor"),
        check_vma=False,
    )
```
